32 devices in a mesh: dp: 8 (over z, y), seq: 4 (over x, core).
Axes of the slice: x: 2, y: 2, z: 4, core: 2. Of those that a mesh axis runs over, the one named last changes fastest.
Arguments:
- tokens: bfloat16 [8, 2048, 896], P('dp', 'seq'), may hold values from -30 to 30
- neighbours: bfloat16 [8, 32, 2, 128, 896], P('dp', 'seq'), may hold values from -6 to 6
- norm_gains: float32 [3, 896], replicated, may hold values from 0.25 to 1.75
- position_bias: float32 [16, 6], replicated, may hold values from -1.5 to 1.5
- query_self: bfloat16 [896, 1024], P('dp', 'seq'), may hold values from -0.1875 to 0.1875
- key_self: bfloat16 [896, 1024], P('dp', 'seq'), may hold values from -0.1875 to 0.1875
- value_self: bfloat16 [896, 1024], P('dp', 'seq'), may hold values from -0.1875 to 0.1875
- output_self: bfloat16 [1024, 896], P('dp', 'seq'), may hold values from -1 to 1
- query_cross: bfloat16 [896, 1024], P('dp', 'seq'), may hold values from -0.1875 to 0.1875
- key_cross: bfloat16 [896, 1024], P('dp', 'seq'), may hold values from -0.1875 to 0.1875
- value_cross: bfloat16 [896, 1024], P('dp', 'seq'), may hold values from -0.1875 to 0.1875
- output_cross: bfloat16 [1024, 896], P('dp', 'seq'), may hold values from -1.5 to 1.5
- inner_weight: bfloat16 [896, 3584], P('dp', 'seq'), may hold values from -0.1875 to 0.1875
- outer_weight: bfloat16 [3584, 896], P('dp', 'seq'), may hold values from -0.09375 to 0.09375
- cotangent: bfloat16 [8, 2048, 896], P('dp', 'seq'), may hold values from -6 to 6
Outputs:
- result: bfloat16 [8, 2048, 896], P('dp', 'seq')
- grad_tokens: bfloat16 [8, 2048, 896], P('dp', 'seq')
- grad_neighbours: bfloat16 [8, 32, 2, 128, 896], P('dp', 'seq')
- grad_gains: float32 [3, 896], replicated
- grad_bias: float32 [16, 6], replicated
- grad_query_self: float32 [896, 1024], P('dp', 'seq')
- grad_key_self: float32 [896, 1024], P('dp', 'seq')
- grad_value_self: float32 [896, 1024], P('dp', 'seq')
- grad_output_self: float32 [1024, 896], P('dp', 'seq')
- grad_query_cross: float32 [896, 1024], P('dp', 'seq')
- grad_key_cross: float32 [896, 1024], P('dp', 'seq')
- grad_value_cross: float32 [896, 1024], P('dp', 'seq')
- grad_output_cross: float32 [1024, 896], P('dp', 'seq')
- grad_inner: float32 [896, 3584], P('dp', 'seq')
- grad_outer: float32 [3584, 896], P('dp', 'seq')
The draws below stay inside these ranges and needn't reach their ends.
All inputs are finite; a program needn't handle non-finite values.
Results may differ from the reference program's by a relative error of at most 0.025.
Values may be sent and summed in bfloat16 or wider, within the bound.
A program may use at most 384 MiB of HBM per device.

```python
import math
import jax
import jax.numpy as jnp
from jax import lax

D = 896
H = 16
HD = 64
FF = 3584
SEGMENT = 64
NEIGH = 2
RLEN = 128
BLOCK = 256
NB = 6
AW = 1024
SEQ_LEN = 2048
GROUP_TOK = 2048
GROUP_SEGS = 32
LANES = 8


def draw_tokens(key, part):
    base_key = jax.random.fold_in(key, 17)
    normal_key, row_key, col_key = jax.random.split(base_key, 3)
    full_shape = (LANES, GROUP_TOK, D)
    base_values = jnp.clip(jax.random.normal(normal_key, full_shape, jnp.float32), -4.0, 4.0)
    row_scale = jnp.exp(jax.random.uniform(row_key, (LANES, GROUP_TOK, 1), jnp.float32, math.log(0.5), math.log(5.0)))
    col_scale = jnp.exp(jax.random.uniform(col_key, (D,), jnp.float32, math.log(0.7), math.log(1.4)))
    return (base_values * row_scale * col_scale).astype(jnp.bfloat16)


def levels(stream_key, shape, shards, low, top_value):
    gain, own = 1.0, jax.random.fold_in(stream_key, 6)
    for dim, blocks in shards:
        steps = jnp.exp(jax.random.uniform(jax.random.fold_in(own, dim), (blocks,), jnp.float32, low / len(shards), top_value / len(shards)))
        gain = gain * jnp.repeat(steps, shape[dim] // blocks).reshape([-1 if axis == dim else 1 for axis in range(len(shape))])
    return gain


def normal_values(stream_key, extent, width, bound, cuts=(), kind=jnp.bfloat16):
    drawn = width * jax.random.normal(stream_key, extent, jnp.float32)
    if cuts:
        drawn = drawn * levels(stream_key, extent, cuts, -0.22, 0.18)
    return jnp.clip(drawn, -bound, bound).astype(kind)


def setup_inputs(seed: int = 0) -> dict:
    arg_keys = jax.random.split(jax.random.key(seed), 16)
    tokens = draw_tokens(jax.random.fold_in(arg_keys[15], 71), 0)
    neighbours = normal_values(arg_keys[1], (LANES, GROUP_SEGS, NEIGH, RLEN, D), 1.0, 6.0, ((0, 8), (1, 4)))
    norm_gains = jnp.clip(1.0 + 0.15 * jax.random.normal(arg_keys[2], (3, D), jnp.float32), 0.25, 1.75)
    position_bias = jnp.clip(jax.random.uniform(arg_keys[3], (H, NB), jnp.float32, -1.5, 1.5), -1.5, 1.5)
    query_self = normal_values(arg_keys[4], (D, AW), D ** -0.5, 0.1875, ((0, 8), (1, 4)))
    key_self = normal_values(arg_keys[5], (D, AW), D ** -0.5, 0.1875, ((0, 8), (1, 4)))
    value_self = normal_values(arg_keys[6], (D, AW), D ** -0.5, 0.1875, ((0, 8), (1, 4)))
    output_self = normal_values(arg_keys[7], (AW, D), (max(2, AW // 32)) ** -0.5, 1.0, ((0, 8), (1, 4)))
    query_cross = normal_values(arg_keys[8], (D, AW), D ** -0.5, 0.1875, ((0, 8), (1, 4)))
    key_cross = normal_values(arg_keys[9], (D, AW), D ** -0.5, 0.1875, ((0, 8), (1, 4)))
    value_cross = normal_values(arg_keys[10], (D, AW), D ** -0.5, 0.1875, ((0, 8), (1, 4)))
    output_cross = normal_values(arg_keys[11], (AW, D), (max(2, AW // 64)) ** -0.5, 1.5, ((0, 8), (1, 4)))
    inner_weight = normal_values(arg_keys[12], (D, FF), D ** -0.5, 0.1875, ((0, 8), (1, 4)))
    outer_weight = normal_values(arg_keys[13], (FF, D), FF ** -0.5, 0.09375, ((0, 8), (1, 4)))
    cotangent = normal_values(arg_keys[14], (LANES, GROUP_TOK, D), 1.0, 6.0, ((0, 8), (1, 4)))
    return {"tokens": tokens, "neighbours": neighbours, "norm_gains": norm_gains, "position_bias": position_bias, "query_self": query_self, "key_self": key_self, "value_self": value_self, "output_self": output_self, "query_cross": query_cross, "key_cross": key_cross, "value_cross": value_cross, "output_cross": output_cross, "inner_weight": inner_weight, "outer_weight": outer_weight, "cotangent": cotangent}


EPSILON = 1e-06
NEGATIVE = -1e+30
HIGHEST = lax.Precision.HIGHEST

@jax.custom_vjp
def low(v):
    return lax.optimization_barrier(v.astype(jnp.bfloat16)).astype(jnp.float32)

@jax.custom_vjp
def low_back(v):
    return v

def low_keep(v):
    return (low(v), None)

def low_pass(kept, grad):
    return (grad,)

def back_keep(v):
    return (v, None)

def back_low(kept, grad):
    return (low(grad),)
low.defvjp(low_keep, low_pass)
low_back.defvjp(back_keep, back_low)

def round_both(operand):
    return low(low_back(operand))

def matmul(left_side, right_side):
    return jnp.dot(left_side, right_side, precision=HIGHEST, preferred_element_type=jnp.float32)

def rms_norm(inputs, gain_row):
    factor = lax.rsqrt(lax.optimization_barrier(jnp.mean(inputs * inputs, axis=-1, keepdims=True)) + EPSILON)
    return inputs * factor * gain_row

def self_block(packed, key_rows, value_rows, position_bias):
    query_rows, start_row = packed
    logits = jnp.einsum('qhd,khd->hqk', query_rows, key_rows, precision=HIGHEST) * HD ** (-0.5)
    query_blocks = (start_row + jnp.arange(query_rows.shape[0], dtype=jnp.int32)) // BLOCK
    key_blocks = jnp.arange(key_rows.shape[0], dtype=jnp.int32) // BLOCK
    distance = query_blocks[:, None] - key_blocks[None, :]
    bucket = jnp.clip(distance, 0, NB - 1)
    scores = low_back(logits + jnp.take(position_bias, bucket, axis=1))
    scores = jnp.where(distance[None] >= 0, scores, NEGATIVE)
    log_total = jax.nn.logsumexp(scores, axis=-1, keepdims=True)
    weights = low(jnp.exp(scores - log_total))
    return jnp.einsum('hqk,khd->qhd', weights, value_rows, precision=HIGHEST)

def self_attention(normed, position_bias, weights):
    length = normed.shape[0]
    queries = round_both(matmul(normed, weights[0])).reshape(length, H, HD)
    key_rows = round_both(matmul(normed, weights[1])).reshape(length, H, HD)
    value_rows = round_both(matmul(normed, weights[2])).reshape(length, H, HD)
    block_rows = math.gcd(length, 512)
    starts = jnp.arange(0, length, block_rows, dtype=jnp.int32)
    query_grid = queries.reshape(length // block_rows, block_rows, H, HD)

    def one_block(packed):
        return self_block(packed, key_rows, value_rows, position_bias)
    mixed_rows = lax.map(jax.checkpoint(one_block), (query_grid, starts))
    mixed_rows = round_both(mixed_rows.reshape(length, H * HD))
    return low_back(matmul(mixed_rows, weights[3]))

def cross_attention(normed, neighbour, weights):
    length = normed.shape[0]
    attn_width = H * HD
    slot_count = length // SEGMENT + 1
    queries = round_both(matmul(normed, weights[4]))
    padded = jnp.concatenate([jnp.zeros((1, attn_width), jnp.float32), queries, jnp.zeros((SEGMENT - 1, attn_width), jnp.float32)], axis=0)
    padded = padded.reshape(slot_count, SEGMENT, H, HD)
    flat_states = neighbour.reshape(-1, D)
    zero_slot = jnp.zeros((1, NEIGH * RLEN, H, HD), jnp.float32)
    key_rows = round_both(matmul(flat_states, weights[5])).reshape(-1, NEIGH * RLEN, H, HD)
    value_rows = round_both(matmul(flat_states, weights[6])).reshape(-1, NEIGH * RLEN, H, HD)
    key_rows = jnp.concatenate([zero_slot, key_rows], axis=0)
    value_rows = jnp.concatenate([zero_slot, value_rows], axis=0)
    scores = low_back(jnp.einsum('sqhd,skhd->shqk', padded, key_rows, precision=HIGHEST) * HD ** (-0.5))
    soft_weights = low(jax.nn.softmax(scores, axis=-1))
    mixed_rows = jnp.einsum('shqk,skhd->sqhd', soft_weights, value_rows, precision=HIGHEST)
    mixed_rows = round_both(mixed_rows.reshape(slot_count * SEGMENT, attn_width)[1:length + 1])
    return low_back(matmul(mixed_rows, weights[7]))

def feed_forward(normed, weights):
    gate_value = low_back(matmul(normed, weights[8]))
    hidden_act = low(jax.nn.gelu(gate_value, approximate=True))
    return low_back(matmul(hidden_act, weights[9]))

def decoder_layer(inputs, neighbour, norm_gains, position_bias, weights):
    after_self = inputs + self_attention(low(rms_norm(inputs, norm_gains[0])), position_bias, weights)
    after_cross = after_self + cross_attention(low(rms_norm(after_self, norm_gains[1])), neighbour, weights)
    return after_cross + feed_forward(low(rms_norm(after_cross, norm_gains[2])), weights)

def reference(tokens, neighbours, norm_gains, position_bias, query_self, key_self, value_self, output_self, query_cross, key_cross, value_cross, output_cross, inner_weight, outer_weight, cotangent):
    seq_count = LANES * (GROUP_TOK // SEQ_LEN)
    inputs = tokens.astype(jnp.float32).reshape(seq_count, SEQ_LEN, D)
    neighbour = neighbours.astype(jnp.float32).reshape(seq_count, SEQ_LEN // SEGMENT, NEIGH * RLEN, D)
    weights = (query_self.astype(jnp.float32), key_self.astype(jnp.float32), value_self.astype(jnp.float32), output_self.astype(jnp.float32), query_cross.astype(jnp.float32), key_cross.astype(jnp.float32), value_cross.astype(jnp.float32), output_cross.astype(jnp.float32), inner_weight.astype(jnp.float32), outer_weight.astype(jnp.float32))

    def forward(inputs, neighbour, norm_gains, position_bias, weights):

        def one_sequence(packed):
            return decoder_layer(packed[0], packed[1], norm_gains, position_bias, weights)
        return lax.map(one_sequence, (inputs, neighbour))
    result, pullback = jax.vjp(forward, inputs, neighbour, norm_gains, position_bias, weights)
    gradients = pullback(cotangent.astype(jnp.float32).reshape(seq_count, SEQ_LEN, D))
    grad_weights = gradients[4]
    return (result.reshape(LANES, GROUP_TOK, D).astype(jnp.bfloat16), gradients[0].reshape(LANES, GROUP_TOK, D).astype(jnp.bfloat16), gradients[1].reshape(LANES, GROUP_SEGS, NEIGH, RLEN, D).astype(jnp.bfloat16), gradients[2], gradients[3], grad_weights[0], grad_weights[1], grad_weights[2], grad_weights[3], grad_weights[4], grad_weights[5], grad_weights[6], grad_weights[7], grad_weights[8], grad_weights[9])
```

```python
import functools

import jax
import jax.numpy as jnp
from jax import lax
from jax.experimental import pallas as pl
from jax.experimental.pallas import tpu as pltpu
from jax.sharding import PartitionSpec as P

HD = 64
SEGMENT = 64
BLOCK = 256
NB = 6
SEQ_MIN = 2048
EPSILON = 1e-06
NEGATIVE = -1e30
BF = jnp.bfloat16
F32 = jnp.float32
VMEM_LIMIT = 56 * 2**20
BOTH = ("dp", "seq")


def dot(a, b, ca=1, cb=0):
    return lax.dot_general(a, b, (((ca,), (cb,)), ((), ())), preferred_element_type=F32)


def linear(a, b):
    return dot(a, b)


def input_grad(a, b):
    return dot(a, b, 1, 1)


def weight_grad(a, b):
    return dot(a, b, 0, 0)


def rounded(v):
    return v.astype(BF)


def rms_apply(inputs, gain_row):
    factor = lax.rsqrt(jnp.mean(inputs * inputs, axis=-1, keepdims=True) + EPSILON)
    return inputs * factor * gain_row


def norm_back(inputs, gain_row, upstream):
    normed_value, pullback = jax.vjp(rms_apply, inputs, gain_row)
    return pullback(upstream)


def gelu_tanh(operand):
    return jax.nn.gelu(operand, approximate=True)


def swap(value, axis, by):
    peers = lax.axis_size(axis)
    return lax.ppermute(value, axis, [(i, i ^ by) for i in range(peers)])


def vmem_spec():
    return pl.BlockSpec(memory_space=pltpu.VMEM)


def smem_spec():
    return pl.BlockSpec(memory_space=pltpu.SMEM)


def copy_kernel(index_ref, in_ref, out_ref):
    out_ref[...] = in_ref[...].reshape(out_ref.shape)


def reorder_rows(stacked, mine):
    count, rows, cols = stacked.shape
    if rows % 16 or cols % 128:
        order = jnp.arange(count, dtype=jnp.int32) ^ mine
        return jnp.take(stacked, order, axis=0).reshape(count * rows, cols)
    spec = pltpu.PrefetchScalarGridSpec(
        num_scalar_prefetch=1,
        grid=(count,),
        in_specs=[pl.BlockSpec((1, rows, cols), lambda i, m: (m[0] ^ i, 0, 0))],
        out_specs=pl.BlockSpec((rows, cols), lambda i, m: (i, 0)),
    )
    return pl.pallas_call(
        copy_kernel,
        grid_spec=spec,
        out_shape=jax.ShapeDtypeStruct((count * rows, cols), stacked.dtype),
    )(mine.reshape(1), stacked)


def columns_from_blocks(stacked, mine):
    count, rows, cols = stacked.shape
    spec = pltpu.PrefetchScalarGridSpec(
        num_scalar_prefetch=1,
        grid=(count,),
        in_specs=[pl.BlockSpec((1, rows, cols), lambda i, m: (m[0] ^ i, 0, 0))],
        out_specs=pl.BlockSpec((rows, cols), lambda i, m: (0, i)),
    )
    return pl.pallas_call(
        copy_kernel,
        grid_spec=spec,
        out_shape=jax.ShapeDtypeStruct((rows, count * cols), stacked.dtype),
    )(mine.reshape(1), stacked)


def blocks_from_columns(flat, count, mine):
    rows, width = flat.shape
    cols = width // count
    spec = pltpu.PrefetchScalarGridSpec(
        num_scalar_prefetch=1,
        grid=(count,),
        in_specs=[pl.BlockSpec((rows, cols), lambda i, m: (0, m[0] ^ i))],
        out_specs=pl.BlockSpec((1, rows, cols), lambda i, m: (i, 0, 0)),
    )
    return pl.pallas_call(
        copy_kernel,
        grid_spec=spec,
        out_shape=jax.ShapeDtypeStruct((count, rows, cols), flat.dtype),
    )(mine.reshape(1), flat)


def assemble(blocks, dp, seq):
    _, rows, cols = blocks.shape
    return blocks.reshape(dp, seq, rows, cols).transpose(0, 2, 1, 3).reshape(dp * rows, seq * cols)


def block_sum(left, right):
    dp, seq = lax.axis_size("dp"), lax.axis_size("seq")
    rows, cols = left.shape[1] // dp, right.shape[1] // seq
    blocks = rounded(weight_grad(left, right)).reshape(dp, rows, seq, cols).transpose(0, 2, 1, 3)
    blocks = blocks.reshape(dp * seq, rows, cols)
    return lax.psum_scatter(blocks, BOTH, scatter_dimension=0, tiled=True)[0].astype(F32)


def device_pairs(target):
    dp, pairs = lax.axis_size("dp"), []
    for i in range(dp):
        for j in range(4):
            z, y, x, c = target(i // 2, i % 2, j // 2, j % 2)
            pairs.append((i * 4 + j, (z * 2 + y) * 4 + x * 2 + c))
    return pairs


def over_z(value, k):
    return lax.ppermute(value, BOTH, device_pairs(lambda z, y, x, c: (z ^ k, y, x, c)))


def over_a(value):
    return lax.ppermute(
        value, BOTH, device_pairs(lambda z, y, x, c: (z, y ^ c, x ^ (1 - c), c))
    )


def over_b(value):
    return lax.ppermute(
        value, BOTH, device_pairs(lambda z, y, x, c: (z, y ^ (1 - c), x ^ c, c))
    )


def over_core(value):
    return lax.ppermute(value, BOTH, device_pairs(lambda z, y, x, c: (z, y, x, 1 - c)))


def my_place():
    i, j = lax.axis_index("dp"), lax.axis_index("seq")
    return jnp.stack([i // 2, i % 2, j // 2, j % 2]).astype(jnp.int32)


def gather_group(shard):
    depth = lax.axis_size("dp") // 2
    near = jnp.stack([shard] + [over_z(shard, k) for k in range(1, depth)])
    both = jnp.concatenate([near, over_a(near)], axis=0)
    far = over_b(both)
    return [both, far, over_core(both), over_core(far)]


def piece_origin(place_ref, c, b, t, depth):
    z, y, x, core = (place_ref[i] for i in range(4))
    a, k = t // depth, t % depth
    core = core ^ c
    dx = jnp.where(core == 0, a, b)
    dy = jnp.where(core == 0, b, a)
    return (z ^ k) * 2 + (y ^ dy), (x ^ dx) * 2 + core


def assemble_attention_kernel(depth, place_ref, *refs):
    pieces, (recall, query, out_self, out_cross), sems = refs[:4], refs[4:8], refs[8]
    rows = query.shape[0] // (2 * depth)
    cols = query.shape[1] // 4
    half = cols // 2

    def step(t, carry):
        for i in range(4):
            i_dp, i_seq = piece_origin(place_ref, i // 2, i % 2, t, depth)
            down = pl.ds(pl.multiple_of(i_dp * rows, rows), rows)
            across = pl.multiple_of(i_seq * cols, cols)
            piece = pieces[i].at[t]

            def move(first, target, sem):
                pltpu.make_async_copy(piece.at[pl.ds(first, rows), :], target, sems.at[sem]).start()

            move(0, recall.at[down, pl.ds(across, cols)], 0)
            move(rows, recall.at[down, pl.ds(across + 4 * cols, cols)], 0)
            move(2 * rows, query.at[down, pl.ds(across, cols)], 1)
            lanes = pl.ds(pl.multiple_of(i_dp * half, half), half)
            for w, out in ((0, out_self), (1, out_cross)):
                for h in range(2):
                    top = pl.multiple_of((i_seq * 2 + h) * rows, rows)
                    pltpu.make_async_copy(
                        piece.at[pl.ds((3 + w) * rows, rows), pl.ds(h * half, half)],
                        out.at[pl.ds(top, rows), lanes],
                        sems.at[2 + w],
                    ).start()
        return carry

    lax.fori_loop(0, 2 * depth, step, 0)
    for sem, out in enumerate((recall, query, out_self, out_cross)):
        pltpu.make_async_copy(out, out, sems.at[sem]).wait()


def assemble_attention(pieces, place):
    count, packed, cols = pieces[0].shape
    rows = packed // 5
    model, width = rows * count, cols * 4
    shapes = [(model, 2 * width), (model, width), (8 * rows, width), (8 * rows, width)]
    return pl.pallas_call(
        functools.partial(assemble_attention_kernel, count // 2),
        in_specs=[smem_spec()] + [pl.BlockSpec(memory_space=pl.ANY)] * 4,
        out_specs=[vmem_spec()] * 4,
        out_shape=[jax.ShapeDtypeStruct(s, BF) for s in shapes],
        scratch_shapes=[pltpu.SemaphoreType.DMA((4,))],
        compiler_params=pltpu.CompilerParams(vmem_limit_bytes=VMEM_LIMIT),
    )(place, *pieces)


def assemble_feed_kernel(depth, place_ref, *refs):
    pieces, (inner, outer), stage, sems = refs[:4], refs[4:6], refs[6], refs[7]
    rows = inner.shape[0] // (2 * depth)
    cols = inner.shape[1] // 4
    part = cols // 4

    def step(t, carry):
        for i in range(4):
            i_dp, i_seq = piece_origin(place_ref, i // 2, i % 2, t, depth)
            piece = pieces[i].at[t]
            down = pl.ds(pl.multiple_of(i_dp * rows, rows), rows)
            across = pl.ds(pl.multiple_of(i_seq * cols, cols), cols)
            pltpu.make_async_copy(
                piece.at[pl.ds(rows, rows), :], stage.at[i_dp, i_seq], sems.at[1]
            ).start()
            pltpu.make_async_copy(
                piece.at[pl.ds(0, rows), :], inner.at[down, across], sems.at[0]
            ).start()
        return carry

    lax.fori_loop(0, 2 * depth, step, 0)
    pltpu.make_async_copy(stage, stage, sems.at[1]).wait()

    def spread(i, carry):
        for t in range(4):
            line = [stage[i, j, :, t * part : (t + 1) * part] for j in range(4)]
            where = pl.multiple_of((i * 4 + t) * rows, rows)
            outer[pl.ds(where, rows), :] = jnp.concatenate(line, axis=1)
        return carry

    lax.fori_loop(0, 2 * depth, spread, 0)
    pltpu.make_async_copy(inner, inner, sems.at[0]).wait()


def assemble_feed(pieces, place):
    count, packed, cols = pieces[0].shape
    rows = packed // 2
    return pl.pallas_call(
        functools.partial(assemble_feed_kernel, count // 2),
        in_specs=[smem_spec()] + [pl.BlockSpec(memory_space=pl.ANY)] * 4,
        out_specs=[vmem_spec()] * 2,
        out_shape=[
            jax.ShapeDtypeStruct((rows * count, cols * 4), BF),
            jax.ShapeDtypeStruct((4 * rows * count, cols), BF),
        ],
        scratch_shapes=[
            pltpu.VMEM((count, 4, rows, cols), BF),
            pltpu.SemaphoreType.DMA((2,)),
        ],
        compiler_params=pltpu.CompilerParams(vmem_limit_bytes=VMEM_LIMIT),
    )(place, *pieces)


def put_block(place_ref, out_ref, core, i_dp, flip, value):
    z, y = place_ref[0], place_ref[1]
    dy = (i_dp % 2) ^ y
    b = jnp.where(core == 0, dy, flip)
    a = jnp.where(core == 0, flip, dy)
    out_ref[b, a, (i_dp // 2) ^ z] = value


def wide_grad_kernel(*refs):
    place_ref, left, kept_right, sent_right = refs[:4]
    kept, sent = refs[-2:]
    flip = pl.program_id(1)
    rows = kept.shape[3]
    core = place_ref[3]
    for right, out, c in ((kept_right, kept, core), (sent_right, sent, 1 - core)):
        value = rounded(dot(left[...], right[...], 0, 0))
        for i_dp in range(value.shape[0] // rows):
            put_block(place_ref, out, c, i_dp, flip, value[i_dp * rows : (i_dp + 1) * rows])


def tall_grad_kernel(*refs):
    place_ref, left, right = refs[:3]
    kept, sent = refs[-2:]
    rows, cols = kept.shape[3], kept.shape[4]
    half = cols // 2
    x, core = place_ref[2], place_ref[3]
    for j in range(4):
        value = rounded(dot(right[:, 2 * j * rows : 2 * (j + 1) * rows], left[...], 0, 0))
        for out, mine in ((kept, core == j % 2), (sent, core != j % 2)):

            @pl.when(mine)
            def _():
                for i_dp in range(value.shape[1] // half):
                    lanes = slice(i_dp * half, (i_dp + 1) * half)
                    block = jnp.concatenate([value[:rows, lanes], value[rows:, lanes]], axis=1)
                    put_block(place_ref, out, j % 2, i_dp, (j // 2) ^ x, block)


def outer_grad_kernel(*refs):
    place_ref, left, right = refs[:3]
    kept, sent = refs[-2:]
    rows, cols = kept.shape[3], kept.shape[4]
    part = cols // 4
    i_z = pl.program_id(0)
    x, core = place_ref[2], place_ref[3]
    for j in range(4):
        value = rounded(dot(left[...], right[:, j * part : (j + 1) * part], 0, 0))
        for out, mine in ((kept, core == j % 2), (sent, core != j % 2)):

            @pl.when(mine)
            def _():
                for i_y in range(2):
                    base = i_y * 4 * rows
                    line = [value[base + t * rows : base + (t + 1) * rows] for t in range(4)]
                    block = jnp.concatenate(line, axis=1)
                    put_block(place_ref, out, j % 2, i_z * 2 + i_y, (j // 2) ^ x, block)


def group_grad(kind, place, left, right, first, total, before=None, parts=1):
    dp = lax.axis_size("dp")
    depth = dp // 2
    tokens, height = left.shape
    width = right.shape[1]
    if kind == "tall":
        rows, cols = width // 8, 2 * height // dp
    elif kind == "outer":
        rows, cols = height // dp // 4, width
    else:
        rows, cols = height // dp, width // 4 // parts
    whole = jax.ShapeDtypeStruct((2, 2, depth, total * rows, cols), BF)
    block = (2, 2, depth, rows, cols)
    if kind == "wide":
        kernel, grid, operands = wide_grad_kernel, (parts, 2), [left, right, right]
        specs = [
            pl.BlockSpec((tokens, height), lambda p, i, m: (0, 0)),
            pl.BlockSpec((tokens, cols), lambda p, i, m: (0, p * 4 + (m[2] ^ i) * 2 + m[3])),
            pl.BlockSpec((tokens, cols), lambda p, i, m: (0, p * 4 + (m[2] ^ i) * 2 + 1 - m[3])),
        ]
        out_spec = pl.BlockSpec(block, lambda p, i, m: (0, 0, 0, first + p, 0))
    elif kind == "outer":
        kernel, grid, operands = outer_grad_kernel, (depth,), [left, right]
        specs = [
            pl.BlockSpec((tokens, height // depth), lambda i, m: (0, i)),
            pl.BlockSpec((tokens, width), lambda i, m: (0, 0)),
        ]
        out_spec = pl.BlockSpec(block, lambda i, m: (0, 0, 0, first, 0))
    else:
        kernel, grid, operands = tall_grad_kernel, (1,), [left, right]
        specs = [
            pl.BlockSpec((tokens, height), lambda i, m: (0, 0)),
            pl.BlockSpec((tokens, width), lambda i, m: (0, 0)),
        ]
        out_spec = pl.BlockSpec(block, lambda i, m: (0, 0, 0, first, 0))
    aliases = {}
    if before is not None:
        aliases = {1 + len(operands): 0, 2 + len(operands): 1}
        operands = operands + list(before)
        specs = specs + [pl.BlockSpec(memory_space=pl.ANY)] * 2
    return pl.pallas_call(
        kernel,
        grid_spec=pltpu.PrefetchScalarGridSpec(
            num_scalar_prefetch=1, grid=grid, in_specs=specs, out_specs=[out_spec] * 2
        ),
        out_shape=[whole, whole],
        input_output_aliases=aliases,
        compiler_params=pltpu.CompilerParams(vmem_limit_bytes=VMEM_LIMIT),
        cost_estimate=pl.CostEstimate(
            flops=2 * tokens * height * width,
            bytes_accessed=2 * (left.size + right.size + height * width),
            transcendentals=0,
        ),
    )(place, *operands)


def sum_group(pieces):
    kept, sent = pieces
    got = over_core(sent).astype(F32)
    got_b = over_b(rounded(kept[1].astype(F32) + got[1])).astype(F32)
    near = kept[0].astype(F32) + got[0]
    got_a = over_a(rounded(near[1] + got_b[1])).astype(F32)
    line = rounded(near[0] + got_b[0] + got_a)
    total = line[0].astype(F32)
    for k in range(1, line.shape[0]):
        total = total + over_z(line[k], k).astype(F32)
    return total


def triple_grad_kernel(place_ref, left, right, kept, sent):
    value = rounded(dot(left[...], right[...], 0, 0))
    rows = kept.shape[1]
    z, y = place_ref[0], place_ref[1]
    for out, flip in ((kept, 0), (sent, 1)):
        for i_y in range(2):

            @pl.when((y ^ i_y) == flip)
            def _():
                for i_z in range(kept.shape[0]):
                    top = (i_z * 2 + i_y) * rows
                    out[i_z ^ z] = value[top : top + rows]


def triple_sum(place, left, right):
    dp = lax.axis_size("dp")
    rows, cols = left.shape[1] // dp, right.shape[1]
    shape = jax.ShapeDtypeStruct((dp // 2, rows, cols), BF)
    kept, sent = pl.pallas_call(
        triple_grad_kernel,
        in_specs=[smem_spec(), vmem_spec(), vmem_spec()],
        out_specs=[vmem_spec()] * 2,
        out_shape=[shape, shape],
        compiler_params=pltpu.CompilerParams(vmem_limit_bytes=VMEM_LIMIT),
        cost_estimate=pl.CostEstimate(
            flops=2 * left.size * cols, bytes_accessed=2 * (left.size + right.size), transcendentals=0
        ),
    )(place, left, right)
    line = rounded(kept.astype(F32) + swap(sent, "dp", 1).astype(F32))
    total = line[0].astype(F32)
    for k in range(1, dp // 2):
        total = total + swap(line[k], "dp", 2 * k).astype(F32)
    return total


def lane_mask(shape, head):
    lanes = lax.broadcasted_iota(jnp.int32, shape, len(shape) - 1)
    return (lanes >= head * HD) & (lanes < (head + 1) * HD)


def transposed(value):
    return value.astype(F32).T


def block_bias(bias_ref, head, query_block, key_block):
    distance = query_block - key_block
    kept = bias_ref[head, jnp.clip(distance, 0, NB - 1)]
    return jnp.where(distance >= 0, kept, NEGATIVE)


def self_fwd_kernel(pos_ref, bias_ref, qkv_ref, o_ref, lse_ref, kh_ref, vt_ref, s_ref, acc_ref):
    heads = kh_ref.shape[0]
    width = heads * HD
    devs, _, rows = vt_ref.shape
    per = rows // BLOCK
    a = pl.program_id(0)
    pos = pos_ref[0]

    @pl.when(a == 0)
    def _():
        for h in range(heads):
            kh_ref[h] = qkv_ref[:, width + h * HD : width + (h + 1) * HD]
        for d in range(devs):
            vt_ref[d] = rounded(transposed(qkv_ref[d * rows : (d + 1) * rows, 2 * width :]))

    first = pl.multiple_of(((a // per) ^ pos) * rows + (a % per) * BLOCK, BLOCK)
    qt = rounded(transposed(qkv_ref[pl.ds(first, BLOCK), :width]) * HD**-0.5)

    def scores(d, tops):
        where = pl.multiple_of((d ^ pos) * rows, rows)
        out = []
        for h in range(heads):
            raw = dot(kh_ref[h, pl.ds(where, rows), :], qt[h * HD : (h + 1) * HD])
            top = tops[h]
            for half in range(per):
                c = block_bias(bias_ref, h, a, d * per + half)
                piece = raw[half * BLOCK : (half + 1) * BLOCK] + c
                s_ref[h, pl.ds(pl.multiple_of(d * rows + half * BLOCK, BLOCK), BLOCK), :] = piece
                top = jnp.maximum(top, jnp.max(piece.reshape(BLOCK // 8, 8, BLOCK), axis=0))
            out.append(top)
        return tuple(out)

    count = a // per + 1
    tops = lax.fori_loop(
        0, count, scores, tuple(jnp.full((8, BLOCK), NEGATIVE, F32) for _ in range(heads))
    )
    tops = [jnp.max(t, axis=0, keepdims=True) for t in tops]
    acc_ref[...] = jnp.zeros_like(acc_ref)

    def mix(d, sums):
        out = []
        slot = d ^ pos
        for h in range(heads):
            e = jnp.exp(s_ref[h, pl.ds(pl.multiple_of(d * rows, rows), rows), :] - tops[h])
            out.append(sums[h] + jnp.sum(e.reshape(rows // 8, 8, BLOCK), axis=0))
            acc_ref[h * HD : (h + 1) * HD, :] += dot(
                vt_ref[slot, h * HD : (h + 1) * HD, :], rounded(e)
            )
        return tuple(out)

    sums = lax.fori_loop(
        0, count, mix, tuple(jnp.zeros((8, BLOCK), F32) for _ in range(heads))
    )
    for h in range(heads):
        total = jnp.sum(sums[h], axis=0, keepdims=True)
        lse_ref[a, h : h + 1, :] = tops[h] + jnp.log(total)
        acc_ref[h * HD : (h + 1) * HD, :] = acc_ref[h * HD : (h + 1) * HD, :] / total
    o_ref[pl.ds(first, BLOCK), :] = rounded(acc_ref[...].T)


def self_fwd(pos, bias, qkv, rows):
    tokens, triple = qkv.shape
    width = triple // 3
    heads = width // HD
    blocks = tokens // BLOCK
    return pl.pallas_call(
        self_fwd_kernel,
        grid=(blocks,),
        in_specs=[smem_spec(), smem_spec(), vmem_spec()],
        out_specs=[vmem_spec(), vmem_spec()],
        out_shape=[
            jax.ShapeDtypeStruct((tokens, width), BF),
            jax.ShapeDtypeStruct((blocks, 8, BLOCK), F32),
        ],
        scratch_shapes=[
            pltpu.VMEM((heads, tokens, HD), BF),
            pltpu.VMEM((tokens // rows, width, rows), BF),
            pltpu.VMEM((heads, tokens, BLOCK), F32),
            pltpu.VMEM((width, BLOCK), F32),
        ],
        compiler_params=pltpu.CompilerParams(vmem_limit_bytes=VMEM_LIMIT),
        cost_estimate=pl.CostEstimate(
            flops=2 * tokens * tokens * width * 2, bytes_accessed=8 * tokens * width,
            transcendentals=tokens * tokens * heads // 2,
        ),
    )(pos.reshape(1), bias, qkv)


def self_bwd_kernel(
    pos_ref, bias_ref, qkv_ref, o_ref, go_ref, lse_ref, dqkv_ref, bsum_ref,
    kh_ref, vh_ref, kt_ref, qm_ref, gm_ref, p_ref, ds_ref, dst_ref, dq_ref, dk_ref, dv_ref,
):
    heads = kh_ref.shape[0]
    width = heads * HD
    devs, _, rows = kt_ref.shape
    per = rows // BLOCK
    a = pl.program_id(0)
    pos = pos_ref[0]

    @pl.when(a == 0)
    def _():
        for h in range(heads):
            kh_ref[h] = qkv_ref[:, width + h * HD : width + (h + 1) * HD]
            vh_ref[h] = qkv_ref[:, 2 * width + h * HD : 2 * width + (h + 1) * HD]
        for d in range(devs):
            kt_ref[d] = rounded(transposed(qkv_ref[d * rows : (d + 1) * rows, width : 2 * width]))
        dk_ref[...] = jnp.zeros_like(dk_ref)
        dv_ref[...] = jnp.zeros_like(dv_ref)
        bsum_ref[...] = jnp.zeros_like(bsum_ref)

    first = pl.multiple_of(((a // per) ^ pos) * rows + (a % per) * BLOCK, BLOCK)
    q = qkv_ref[pl.ds(first, BLOCK), :width] * jnp.asarray(HD**-0.5, BF)
    go = go_ref[pl.ds(first, BLOCK), :]
    qt = rounded(transposed(q))
    got = transposed(go)
    prod = got * transposed(o_ref[pl.ds(first, BLOCK), :])
    got = rounded(got)
    zero = jnp.zeros((BLOCK, width), BF)
    dots, lses = [], []
    for h in range(heads):
        mask = lane_mask((BLOCK, width), h)
        qm_ref[h * BLOCK : (h + 1) * BLOCK, :] = jnp.where(mask, q, zero)
        gm_ref[h * BLOCK : (h + 1) * BLOCK, :] = jnp.where(mask, go, zero)
        dots.append(jnp.sum(prod[h * HD : (h + 1) * HD], axis=0, keepdims=True))
        lses.append(lse_ref[a, h : h + 1, :])
    dq_ref[...] = jnp.zeros_like(dq_ref)

    def step(d, carry):
        where = pl.multiple_of((d ^ pos) * rows, rows)
        slot = d ^ pos
        for h in range(heads):
            lanes = slice(h * HD, (h + 1) * HD)
            cols = slice(h * BLOCK, (h + 1) * BLOCK)
            raw = dot(kh_ref[h, pl.ds(where, rows), :], qt[lanes])
            gp = dot(vh_ref[h, pl.ds(where, rows), :], got[lanes])
            for half in range(per):
                part = slice(half * BLOCK, (half + 1) * BLOCK)
                key_block = d * per + half
                c = block_bias(bias_ref, h, a, key_block)
                pf = jnp.exp(raw[part] + (c - lses[h]))
                p_ref[part, cols] = rounded(pf)
                ds = rounded(pf * (gp[part] - dots[h]))
                ds_ref[part, cols] = ds
                dst_ref[h, part, :] = ds
                bucket = jnp.clip(a - key_block, 0, NB - 1)
                bsum_ref[h, bucket] += jnp.sum(
                    ds.astype(F32).reshape(BLOCK // 8, 8, BLOCK), axis=0
                )
            dq_ref[lanes, :] += dot(kt_ref[slot, lanes, :], dst_ref[h])
        dv_ref[pl.ds(where, rows), :] += dot(p_ref[...], gm_ref[...])
        dk_ref[pl.ds(where, rows), :] += dot(ds_ref[...], qm_ref[...])
        return carry

    lax.fori_loop(0, a // per + 1, step, 0)
    dqkv_ref[pl.ds(first, BLOCK), :width] = rounded(dq_ref[...].T * HD**-0.5)

    @pl.when(a == pl.num_programs(0) - 1)
    def _():
        dqkv_ref[:, width : 2 * width] = rounded(dk_ref[...])
        dqkv_ref[:, 2 * width :] = rounded(dv_ref[...])


def self_bwd(pos, bias, qkv, mixed, grad, lse, rows):
    tokens, triple = qkv.shape
    width = triple // 3
    heads = width // HD
    blocks = tokens // BLOCK
    return pl.pallas_call(
        self_bwd_kernel,
        grid=(blocks,),
        in_specs=[smem_spec(), smem_spec()] + [vmem_spec()] * 4,
        out_specs=[vmem_spec(), vmem_spec()],
        out_shape=[
            jax.ShapeDtypeStruct((tokens, triple), BF),
            jax.ShapeDtypeStruct((heads, NB, 8, BLOCK), F32),
        ],
        scratch_shapes=[
            pltpu.VMEM((heads, tokens, HD), BF),
            pltpu.VMEM((heads, tokens, HD), BF),
            pltpu.VMEM((tokens // rows, width, rows), BF),
            pltpu.VMEM((heads * BLOCK, width), BF),
            pltpu.VMEM((heads * BLOCK, width), BF),
            pltpu.VMEM((rows, heads * BLOCK), BF),
            pltpu.VMEM((rows, heads * BLOCK), BF),
            pltpu.VMEM((heads, rows, BLOCK), BF),
            pltpu.VMEM((width, BLOCK), F32),
            pltpu.VMEM((tokens, width), F32),
            pltpu.VMEM((tokens, width), F32),
        ],
        compiler_params=pltpu.CompilerParams(vmem_limit_bytes=VMEM_LIMIT),
        cost_estimate=pl.CostEstimate(
            flops=5 * tokens * tokens * width * 2, bytes_accessed=16 * tokens * width,
            transcendentals=tokens * tokens * heads // 2,
        ),
    )(pos.reshape(1), bias, qkv, mixed, grad, lse)


def slotted(value, pad_ref):
    rows = value.shape[0]
    rolled = pltpu.roll(value.astype(F32), 1, 0)
    first = lax.broadcasted_iota(jnp.int32, rolled.shape, 0) == 0
    pad_ref[:rows] = rounded(jnp.where(first, 0.0, rolled))
    pad_ref[rows:] = rounded(jnp.where(first, rolled, 0.0)[:SEGMENT])


def unslotted(pad_ref, rows):
    value = pad_ref[:rows]
    first = lax.broadcasted_iota(jnp.int32, value.shape, 0) == 0
    value = jnp.where(first, jnp.broadcast_to(pad_ref[rows : rows + 1], value.shape), value)
    return pltpu.roll(value, rows - 1, 0)


def masked_stack(value, group):
    return jnp.concatenate(
        [jnp.where(lane_mask(value.shape, h), value, jnp.zeros_like(value)) for h in range(group)], 0
    )


def cross_soft(keys, stacked):
    s = dot(keys, stacked, 1, 1)
    top = jnp.max(s, axis=0, keepdims=True)
    e = jnp.exp(s - top)
    return e / jnp.sum(e, axis=0, keepdims=True)


def merged(tall, group):
    rows, width = tall.shape[0] // group, tall.shape[1]
    out = jnp.zeros((rows, width), F32)
    for h in range(group):
        out = jnp.where(lane_mask((rows, width), h), tall[h * rows : (h + 1) * rows], out)
    return out


def cross_fwd_kernel(q_ref, k_ref, v_ref, out_ref, qp_ref, op_ref):
    slot = pl.program_id(0)
    rows = q_ref.shape[0]
    lanes = 4 * HD

    @pl.when(slot == 0)
    def _():
        slotted(q_ref[...], qp_ref)

    here = pl.ds(pl.multiple_of(slot * SEGMENT, SEGMENT), SEGMENT)
    scaled = qp_ref[here, :] * jnp.asarray(HD**-0.5, BF)
    for g in range(q_ref.shape[1] // lanes):
        part = slice(g * lanes, (g + 1) * lanes)
        soft = rounded(cross_soft(k_ref[:, part], masked_stack(scaled[:, part], 4)))
        op_ref[here, part] = merged(dot(soft, v_ref[:, part], 0, 0), 4)

    @pl.when(slot == pl.num_programs(0) - 1)
    def _():
        out_ref[...] = rounded(unslotted(op_ref, rows))


def cross_fwd(queries, pairs, neigh_rows):
    rows, width = queries.shape
    slots = rows // SEGMENT + 1
    return pl.pallas_call(
        cross_fwd_kernel,
        grid=(slots,),
        in_specs=[
            vmem_spec(),
            pl.BlockSpec((neigh_rows, width), lambda i: (i, 0)),
            pl.BlockSpec((neigh_rows, width), lambda i: (i, 1)),
        ],
        out_specs=vmem_spec(),
        out_shape=jax.ShapeDtypeStruct((rows, width), BF),
        scratch_shapes=[
            pltpu.VMEM((slots * SEGMENT, width), BF),
            pltpu.VMEM((slots * SEGMENT, width), F32),
        ],
        compiler_params=pltpu.CompilerParams(vmem_limit_bytes=VMEM_LIMIT),
        cost_estimate=pl.CostEstimate(
            flops=16 * slots * SEGMENT * neigh_rows * width, bytes_accessed=2 * pairs.size,
            transcendentals=slots * neigh_rows * width,
        ),
    )(queries, pairs, pairs)


def cross_bwd_kernel(q_ref, g_ref, k_ref, v_ref, dq_ref, dkv_ref, qp_ref, gp_ref, op_ref):
    slot = pl.program_id(0)
    rows, width = q_ref.shape
    lanes = 4 * HD

    @pl.when(slot == 0)
    def _():
        slotted(q_ref[...], qp_ref)
        slotted(g_ref[...], gp_ref)

    here = pl.ds(pl.multiple_of(slot * SEGMENT, SEGMENT), SEGMENT)
    scaled = qp_ref[here, :] * jnp.asarray(HD**-0.5, BF)
    grads = gp_ref[here, :]
    for g in range(width // lanes):
        part = slice(g * lanes, (g + 1) * lanes)
        queries = masked_stack(scaled[:, part], 4)
        grad = masked_stack(grads[:, part], 4)
        soft = cross_soft(k_ref[:, part], queries)
        gp = dot(v_ref[:, part], grad, 1, 1)
        ds = rounded(soft * (gp - jnp.sum(soft * gp, axis=0, keepdims=True)))
        op_ref[here, part] = merged(dot(ds, k_ref[:, part], 0, 0), 4) * HD**-0.5
        dkv_ref[:, part] = rounded(dot(ds, queries))
        dkv_ref[:, width + g * lanes : width + (g + 1) * lanes] = rounded(dot(rounded(soft), grad))

    @pl.when(slot == pl.num_programs(0) - 1)
    def _():
        dq_ref[...] = rounded(unslotted(op_ref, rows))


def cross_bwd(queries, grads, pairs, neigh_rows):
    rows, width = queries.shape
    slots = rows // SEGMENT + 1
    return pl.pallas_call(
        cross_bwd_kernel,
        grid=(slots,),
        in_specs=[
            vmem_spec(),
            vmem_spec(),
            pl.BlockSpec((neigh_rows, width), lambda i: (i, 0)),
            pl.BlockSpec((neigh_rows, width), lambda i: (i, 1)),
        ],
        out_specs=[vmem_spec(), pl.BlockSpec((neigh_rows, 2 * width), lambda i: (i, 0))],
        out_shape=[
            jax.ShapeDtypeStruct((rows, width), BF),
            jax.ShapeDtypeStruct(pairs.shape, BF),
        ],
        scratch_shapes=[
            pltpu.VMEM((slots * SEGMENT, width), BF),
            pltpu.VMEM((slots * SEGMENT, width), BF),
            pltpu.VMEM((slots * SEGMENT, width), F32),
        ],
        compiler_params=pltpu.CompilerParams(vmem_limit_bytes=VMEM_LIMIT),
        cost_estimate=pl.CostEstimate(
            flops=40 * slots * SEGMENT * neigh_rows * width, bytes_accessed=4 * pairs.size,
            transcendentals=slots * neigh_rows * width,
        ),
    )(queries, grads, pairs, pairs)


def on_device(
    tokens, neighbours, norm_gains, position_bias, query_self, key_self, value_self, output_self,
    query_cross, key_cross, value_cross, output_cross, inner_weight, outer_weight, cotangent,
):
    dp, seq = lax.axis_size("dp"), lax.axis_size("seq")
    rows, model = tokens.shape[1], tokens.shape[2]
    heads = position_bias.shape[0]
    width = heads * HD
    segments = rows // SEGMENT
    neigh_rows = neighbours.shape[2] * neighbours.shape[3]
    span = min(seq, max(2, SEQ_MIN // rows))
    group_width = width // span
    group_heads = heads // span
    my_dp = lax.axis_index("dp")
    pos = lax.axis_index("seq") % span

    fast = seq == 4 and span == 4 and rows % (2 * BLOCK) == 0 and model == 896
    place = my_place() if fast else None

    def whole(shard):
        return assemble(lax.all_gather(shard, BOTH, axis=0, tiled=False), dp, seq)

    triple = jnp.concatenate([query_self, key_self, value_self], axis=1)
    if fast:
        near = {0: triple}
        for k in range(2, dp, 2):
            near[k] = swap(triple, "dp", k)
        for k in list(near):
            near[k + 1] = swap(near[k], "dp", 1)
        triple_full = reorder_rows(jnp.stack([near[k] for k in range(dp)]), my_dp)

        def turned(shard):
            flat = shard.T
            half = flat.shape[0] // 2
            return jnp.concatenate([flat[:half], flat[half:]], axis=1)

        packed = jnp.concatenate(
            [key_cross, value_cross, query_cross, turned(output_self), turned(output_cross)], axis=0
        )
        recall_full, query_full, output_turned, cross_turned = assemble_attention(
            gather_group(packed), place
        )
        part = outer_weight.shape[0] // 4
        line = [outer_weight[t * part : (t + 1) * part] for t in range(4)]
        packed = jnp.concatenate([inner_weight, jnp.concatenate(line, axis=1)], axis=0)
        inner_full, outer_full = assemble_feed(gather_group(packed), place)
    else:
        pieces = []
        for shard in (query_self, key_self, value_self):
            pieces.append(lax.dynamic_slice_in_dim(whole(shard), pos * group_width, group_width, 1))
        triple_full = jnp.concatenate(pieces, axis=1)
        recall_full = jnp.concatenate([whole(key_cross), whole(value_cross)], axis=1)
        query_full = whole(query_cross)
        output_turned, cross_turned = whole(output_self).T, whole(output_cross).T
        inner_full, outer_full = whole(inner_weight), whole(outer_weight)

    own_tokens = tokens.reshape(rows, model)
    pieces = {0: own_tokens}
    bit = span // 2
    while bit:
        for k in list(pieces):
            pieces[k | bit] = swap(pieces[k], "seq", bit)
        bit //= 2
    states = neighbours.reshape(segments * neigh_rows, model)
    forward_pairs = [(i, i + 1) for i in range(seq - 1) if (i + 1) % span]
    back_pairs = [(i + 1, i) for i in range(seq - 1) if (i + 1) % span]
    edge = lax.ppermute(states[(segments - 1) * neigh_rows :], "seq", forward_pairs)
    states_all = jnp.concatenate([edge, states], axis=0)

    inputs = own_tokens.astype(F32)
    upstream = cotangent.reshape(rows, model).astype(F32)
    first_normed = jnp.concatenate(
        [rounded(rms_apply(pieces[k].astype(F32), norm_gains[0])) for k in range(span)], axis=0
    )
    qkv = rounded(linear(first_normed, triple_full))
    bias = lax.dynamic_slice_in_dim(position_bias, pos * group_heads, group_heads, 0)
    mixed_group, lse = self_fwd(pos, bias, qkv, rows)

    def exchanged(stack):
        return [stack[0]] + [swap(stack[k], "seq", k) for k in range(1, span)]

    mixed_blocks = mixed_group.reshape(span, rows, group_width)
    mixed_self = columns_from_blocks(jnp.stack(exchanged(mixed_blocks)), pos)

    recall_pairs = rounded(linear(states_all, recall_full))

    after_self = inputs + input_grad(mixed_self, output_turned)
    second_normed = rounded(rms_apply(after_self, norm_gains[1]))
    cross_queries = rounded(linear(second_normed, query_full))
    mixed_cross = cross_fwd(cross_queries, recall_pairs, neigh_rows)
    after_cross = after_self + input_grad(mixed_cross, cross_turned)
    third_normed = rounded(rms_apply(after_cross, norm_gains[2]))
    gate_value = linear(third_normed, inner_full)
    activated, gelu_pull = jax.vjp(gelu_tanh, gate_value)
    hidden_act = rounded(activated)
    outcome = after_cross + linear(hidden_act, outer_full)

    grad_feed = rounded(upstream)
    grad_hidden = input_grad(grad_feed, outer_full)
    grad_gate = rounded(gelu_pull(grad_hidden)[0])
    if fast:
        pieces = group_grad("outer", place, hidden_act, grad_feed, 1, 2)
        pieces = group_grad("wide", place, third_normed, grad_gate, 0, 2, pieces)
        own = sum_group(pieces)
        part = own.shape[0] // 2
        sum_inner = own[:part]
        sum_outer = own[part:].reshape(part, 4, model // 4).transpose(1, 0, 2).reshape(4 * part, -1)
    else:
        sum_outer = block_sum(hidden_act, grad_feed)
        sum_inner = block_sum(third_normed, grad_gate)
    norm_grad, gain_three = norm_back(after_cross, norm_gains[2], input_grad(grad_gate, inner_full))
    grad_late = upstream + norm_grad

    grad_cross = rounded(grad_late)
    grad_mixed = rounded(linear(grad_cross, cross_turned))
    probe, pair_round = cross_bwd(cross_queries, grad_mixed, recall_pairs, neigh_rows)

    def turned_back(own):
        half = own.shape[1] // 2
        return jnp.concatenate([own[:, :half].T, own[:, half:].T], axis=1)

    if fast:
        pieces = group_grad("tall", place, mixed_cross, grad_cross, 3, 4)
        pieces = group_grad("wide", place, second_normed, probe, 2, 4, pieces)
        pieces = group_grad("wide", place, states_all, pair_round, 0, 4, pieces, 2)
        own = sum_group(pieces)
        part = own.shape[0] // 4
        sum_key, sum_value, sum_query = (own[i * part : (i + 1) * part] for i in range(3))
        sum_cross = turned_back(own[3 * part :])
    else:
        sum_cross = block_sum(mixed_cross, grad_cross)
        sum_key = block_sum(states_all, pair_round[:, :width])
        sum_value = block_sum(states_all, pair_round[:, width:])
        sum_query = block_sum(second_normed, probe)
    norm_grad, gain_two = norm_back(after_self, norm_gains[1], input_grad(probe, query_full))
    grad_early = grad_late + norm_grad
    states_round = rounded(input_grad(pair_round, recall_full))
    returned = lax.ppermute(states_round[:neigh_rows], "seq", back_pairs)
    last = states_round[segments * neigh_rows :].astype(F32) + returned.astype(F32)
    grad_states = jnp.concatenate(
        [states_round[neigh_rows : segments * neigh_rows], rounded(last)], axis=0
    )

    grad_self = rounded(grad_early)
    if fast:
        sum_output = turned_back(sum_group(group_grad("tall", place, mixed_self, grad_self, 0, 1)))
    else:
        sum_output = block_sum(mixed_self, grad_self)
    grad_attended = rounded(linear(grad_self, output_turned))
    group_grads = exchanged(blocks_from_columns(grad_attended, span, pos))
    grad_group = jnp.concatenate(group_grads, axis=0)
    triple_grad, bias_sums = self_bwd(pos, bias, qkv, mixed_group, grad_group, lse, rows)
    partial = rounded(input_grad(triple_grad, triple_full)).reshape(span, rows, model)
    blocks = {k: partial[k] for k in range(span)}
    bit = 1
    while bit < span:
        for k in sorted(blocks):
            if not k & bit:
                got = swap(blocks[k | bit], "seq", bit)
                blocks[k] = blocks[k].astype(F32) + got.astype(F32)
                if bit * 2 < span and k:
                    blocks[k] = rounded(blocks[k])
        blocks = {k: v for k, v in blocks.items() if not k & bit}
        bit *= 2
    norm_grad, gain_one = norm_back(inputs, norm_gains[0], blocks[0])
    grad_inputs = grad_early + norm_grad

    if fast:
        own = triple_sum(place, first_normed, triple_grad)
        own_self = [own[:, i * group_width : (i + 1) * group_width] for i in range(3)]
    else:
        own_self = []
        for i in range(3):
            columns = triple_grad[:, i * group_width : (i + 1) * group_width]
            wide = jnp.zeros((span * rows, width), BF)
            wide = lax.dynamic_update_slice_in_dim(wide, columns, pos * group_width, 1)
            own_self.append(block_sum(first_normed, wide))

    bias_local = jnp.sum(bias_sums, axis=(2, 3))
    bias_all = lax.dynamic_update_slice_in_dim(
        jnp.zeros((heads, NB), F32), bias_local, pos * group_heads, 0
    )
    gains, bias_total = lax.psum((jnp.stack([gain_one, gain_two, gain_three]), bias_all), BOTH)
    return (
        rounded(outcome).reshape(1, rows, model),
        rounded(grad_inputs).reshape(1, rows, model),
        grad_states.reshape(neighbours.shape),
        gains,
        bias_total,
        own_self[0],
        own_self[1],
        own_self[2],
        sum_output,
        sum_query,
        sum_key,
        sum_value,
        sum_cross,
        sum_inner,
        sum_outer,
    )


def solution(mesh):
    weight = P("dp", "seq")
    lane = P("dp", "seq", None)
    wide = P("dp", "seq", None, None, None)
    return jax.shard_map(
        on_device,
        mesh=mesh,
        in_specs=(lane, wide, P(), P()) + (weight,) * 10 + (lane,),
        out_specs=(lane, lane, wide, P(), P()) + (weight,) * 10,
        check_vma=False,
    )
```

```python
import functools

import jax
import jax.numpy as jnp
from jax import lax
from jax.experimental import pallas as pl
from jax.experimental.pallas import tpu as pltpu
from jax.sharding import PartitionSpec as P

HD = 64
SEGMENT = 64
BLOCK = 256
NB = 6
SEQ_MIN = 2048
EPSILON = 1e-06
NEGATIVE = -1e30
BF = jnp.bfloat16
F32 = jnp.float32
VMEM_LIMIT = 56 * 2**20
BOTH = ("dp", "seq")


def dot(a, b, ca=1, cb=0):
    return lax.dot_general(a, b, (((ca,), (cb,)), ((), ())), preferred_element_type=F32)


def linear(a, b):
    return dot(a, b)


def input_grad(a, b):
    return dot(a, b, 1, 1)


def weight_grad(a, b):
    return dot(a, b, 0, 0)


def rounded(v):
    return v.astype(BF)


def rms_apply(inputs, gain_row):
    factor = lax.rsqrt(jnp.mean(inputs * inputs, axis=-1, keepdims=True) + EPSILON)
    return inputs * factor * gain_row


def norm_back(inputs, gain_row, upstream):
    normed_value, pullback = jax.vjp(rms_apply, inputs, gain_row)
    return pullback(upstream)


def gelu_tanh(operand):
    return jax.nn.gelu(operand, approximate=True)


def swap(value, axis, by):
    peers = lax.axis_size(axis)
    return lax.ppermute(value, axis, [(i, i ^ by) for i in range(peers)])


def after(value, *others):
    return lax.optimization_barrier((value,) + others)[0]


def vmem_spec():
    return pl.BlockSpec(memory_space=pltpu.VMEM)


def smem_spec():
    return pl.BlockSpec(memory_space=pltpu.SMEM)


def copy_kernel(index_ref, in_ref, out_ref):
    out_ref[...] = in_ref[...].reshape(out_ref.shape)


def reorder_triple_kernel(place_ref, near_ref, far_ref, out_ref):
    count, rows, _ = near_ref.shape
    z, y = place_ref[0], place_ref[1]
    for ref, flip in ((near_ref, 0), (far_ref, 1)):
        for k in range(count):
            where = ((z ^ k) * 2 + (y ^ flip)) * rows
            out_ref[pl.ds(pl.multiple_of(where, rows), rows), :] = ref[k]


def reorder_triple(near, far, place):
    count, rows, cols = near.shape
    return pl.pallas_call(
        reorder_triple_kernel,
        in_specs=[smem_spec(), vmem_spec(), vmem_spec()],
        out_specs=vmem_spec(),
        out_shape=jax.ShapeDtypeStruct((2 * count * rows, cols), near.dtype),
    )(place, near, far)


def columns_from_blocks(stacked, mine):
    count, rows, cols = stacked.shape
    spec = pltpu.PrefetchScalarGridSpec(
        num_scalar_prefetch=1,
        grid=(count,),
        in_specs=[pl.BlockSpec((1, rows, cols), lambda i, m: (m[0] ^ i, 0, 0))],
        out_specs=pl.BlockSpec((rows, cols), lambda i, m: (0, i)),
    )
    return pl.pallas_call(
        copy_kernel,
        grid_spec=spec,
        out_shape=jax.ShapeDtypeStruct((rows, count * cols), stacked.dtype),
    )(mine.reshape(1), stacked)


def blocks_from_columns(flat, count, mine):
    rows, width = flat.shape
    cols = width // count
    spec = pltpu.PrefetchScalarGridSpec(
        num_scalar_prefetch=1,
        grid=(count,),
        in_specs=[pl.BlockSpec((rows, cols), lambda i, m: (0, m[0] ^ i))],
        out_specs=pl.BlockSpec((1, rows, cols), lambda i, m: (i, 0, 0)),
    )
    return pl.pallas_call(
        copy_kernel,
        grid_spec=spec,
        out_shape=jax.ShapeDtypeStruct((count, rows, cols), flat.dtype),
    )(mine.reshape(1), flat)


def assemble(blocks, dp, seq):
    _, rows, cols = blocks.shape
    return blocks.reshape(dp, seq, rows, cols).transpose(0, 2, 1, 3).reshape(dp * rows, seq * cols)


def block_sum(left, right):
    dp, seq = lax.axis_size("dp"), lax.axis_size("seq")
    rows, cols = left.shape[1] // dp, right.shape[1] // seq
    blocks = rounded(weight_grad(left, right)).reshape(dp, rows, seq, cols).transpose(0, 2, 1, 3)
    blocks = blocks.reshape(dp * seq, rows, cols)
    return lax.psum_scatter(blocks, BOTH, scatter_dimension=0, tiled=True)[0].astype(F32)


def device_pairs(target):
    dp, pairs = lax.axis_size("dp"), []
    for i in range(dp):
        for j in range(4):
            z, y, x, c = target(i // 2, i % 2, j // 2, j % 2)
            pairs.append((i * 4 + j, (z * 2 + y) * 4 + x * 2 + c))
    return pairs


def over_z(value, k):
    return lax.ppermute(value, BOTH, device_pairs(lambda z, y, x, c: (z ^ k, y, x, c)))


def over_a(value):
    return lax.ppermute(
        value, BOTH, device_pairs(lambda z, y, x, c: (z, y ^ c, x ^ (1 - c), c))
    )


def over_b(value):
    return lax.ppermute(
        value, BOTH, device_pairs(lambda z, y, x, c: (z, y ^ (1 - c), x ^ c, c))
    )


def over_core(value):
    return lax.ppermute(value, BOTH, device_pairs(lambda z, y, x, c: (z, y, x, 1 - c)))


def my_place():
    i, j = lax.axis_index("dp"), lax.axis_index("seq")
    return jnp.stack([i // 2, i % 2, j // 2, j % 2]).astype(jnp.int32)


def gather_group(shard):
    depth = lax.axis_size("dp") // 2
    near = jnp.stack([shard] + [over_z(shard, k) for k in range(1, depth)])
    both = jnp.concatenate([near, over_a(near)], axis=0)
    far = over_b(both)
    return [both, far, over_core(both), over_core(far)]


def piece_origin(place_ref, c, b, t, depth):
    z, y, x, core = (place_ref[i] for i in range(4))
    a, k = t // depth, t % depth
    core = core ^ c
    dx = jnp.where(core == 0, a, b)
    dy = jnp.where(core == 0, b, a)
    return (z ^ k) * 2 + (y ^ dy), (x ^ dx) * 2 + core


def assemble_attention_kernel(depth, place_ref, *refs):
    pieces, (recall, query, out_self, out_cross), sems = refs[:4], refs[4:8], refs[8]
    rows = query.shape[0] // (2 * depth)
    cols = query.shape[1] // 4
    half = cols // 2

    def step(t, carry):
        for i in range(4):
            i_dp, i_seq = piece_origin(place_ref, i // 2, i % 2, t, depth)
            down = pl.ds(pl.multiple_of(i_dp * rows, rows), rows)
            across = pl.multiple_of(i_seq * cols, cols)
            piece = pieces[i].at[t]

            def move(first, target, sem):
                pltpu.make_async_copy(piece.at[pl.ds(first, rows), :], target, sems.at[sem]).start()

            move(0, recall.at[down, pl.ds(across, cols)], 0)
            move(rows, recall.at[down, pl.ds(across + 4 * cols, cols)], 0)
            move(2 * rows, query.at[down, pl.ds(across, cols)], 1)
            lanes = pl.ds(pl.multiple_of(i_dp * half, half), half)
            for w, out in ((0, out_self), (1, out_cross)):
                for h in range(2):
                    top = pl.multiple_of((i_seq * 2 + h) * rows, rows)
                    pltpu.make_async_copy(
                        piece.at[pl.ds((3 + w) * rows, rows), pl.ds(h * half, half)],
                        out.at[pl.ds(top, rows), lanes],
                        sems.at[2 + w],
                    ).start()
        return carry

    lax.fori_loop(0, 2 * depth, step, 0)
    for sem, out in enumerate((recall, query, out_self, out_cross)):
        pltpu.make_async_copy(out, out, sems.at[sem]).wait()


def assemble_attention(pieces, place):
    count, packed, cols = pieces[0].shape
    rows = packed // 5
    model, width = rows * count, cols * 4
    shapes = [(model, 2 * width), (model, width), (8 * rows, width), (8 * rows, width)]
    return pl.pallas_call(
        functools.partial(assemble_attention_kernel, count // 2),
        in_specs=[smem_spec()] + [pl.BlockSpec(memory_space=pl.ANY)] * 4,
        out_specs=[vmem_spec()] * 4,
        out_shape=[jax.ShapeDtypeStruct(s, BF) for s in shapes],
        scratch_shapes=[pltpu.SemaphoreType.DMA((4,))],
        compiler_params=pltpu.CompilerParams(vmem_limit_bytes=VMEM_LIMIT),
    )(place, *pieces)


def assemble_feed_kernel(blocks, inner, outer, stage, sems):
    count = blocks.shape[0]
    rows = inner.shape[0] // (count // 4)
    cols = inner.shape[1] // 4
    part = cols // 4

    def step(i, carry):
        for j in range(4):
            piece = blocks.at[i * 4 + j]
            down = pl.ds(pl.multiple_of(i * rows, rows), rows)
            pltpu.make_async_copy(
                piece.at[pl.ds(rows, rows), :], stage.at[i, j], sems.at[1]
            ).start()
            pltpu.make_async_copy(
                piece.at[pl.ds(0, rows), :], inner.at[down, pl.ds(j * cols, cols)], sems.at[0]
            ).start()
        return carry

    lax.fori_loop(0, count // 4, step, 0)
    pltpu.make_async_copy(stage, stage, sems.at[1]).wait()

    def spread(i, carry):
        for t in range(4):
            line = [stage[i, j, :, t * part : (t + 1) * part] for j in range(4)]
            where = pl.multiple_of((i * 4 + t) * rows, rows)
            outer[pl.ds(where, rows), :] = jnp.concatenate(line, axis=1)
        return carry

    lax.fori_loop(0, count // 4, spread, 0)
    pltpu.make_async_copy(inner, inner, sems.at[0]).wait()


def assemble_feed(blocks):
    count, packed, cols = blocks.shape
    rows, deep = packed // 2, count // 4
    return pl.pallas_call(
        assemble_feed_kernel,
        in_specs=[pl.BlockSpec(memory_space=pl.ANY)],
        out_specs=[vmem_spec()] * 2,
        out_shape=[
            jax.ShapeDtypeStruct((rows * deep, cols * 4), BF),
            jax.ShapeDtypeStruct((4 * rows * deep, cols), BF),
        ],
        scratch_shapes=[
            pltpu.VMEM((deep, 4, rows, cols), BF),
            pltpu.SemaphoreType.DMA((2,)),
        ],
        compiler_params=pltpu.CompilerParams(vmem_limit_bytes=VMEM_LIMIT),
    )(blocks)


def put_block(place_ref, out_ref, core, i_dp, flip, value):
    z, y = place_ref[0], place_ref[1]
    dy = (i_dp % 2) ^ y
    b = jnp.where(core == 0, dy, flip)
    a = jnp.where(core == 0, flip, dy)
    out_ref[b, a, (i_dp // 2) ^ z] = value


def wide_grad_kernel(*refs):
    place_ref, left, kept_right, sent_right = refs[:4]
    kept, sent = refs[-2:]
    flip = pl.program_id(1)
    rows = kept.shape[3]
    core = place_ref[3]
    for right, out, c in ((kept_right, kept, core), (sent_right, sent, 1 - core)):
        value = rounded(dot(left[...], right[...], 0, 0))
        for i_dp in range(value.shape[0] // rows):
            put_block(place_ref, out, c, i_dp, flip, value[i_dp * rows : (i_dp + 1) * rows])


def tall_grad_kernel(*refs):
    place_ref, left, right = refs[:3]
    kept, sent = refs[-2:]
    rows, cols = kept.shape[3], kept.shape[4]
    half = cols // 2
    x, core = place_ref[2], place_ref[3]
    for j in range(4):
        value = rounded(dot(right[:, 2 * j * rows : 2 * (j + 1) * rows], left[...], 0, 0))
        for out, mine in ((kept, core == j % 2), (sent, core != j % 2)):

            @pl.when(mine)
            def _():
                for i_dp in range(value.shape[1] // half):
                    lanes = slice(i_dp * half, (i_dp + 1) * half)
                    block = jnp.concatenate([value[:rows, lanes], value[rows:, lanes]], axis=1)
                    put_block(place_ref, out, j % 2, i_dp, (j // 2) ^ x, block)


def outer_grad_kernel(left, right, out_ref):
    rows, cols = out_ref.shape[2], out_ref.shape[3]
    part = cols // 4
    value = rounded(dot(left[...], right[...], 0, 0))
    for i_y in range(2):
        for j in range(4):
            base = i_y * 4 * rows
            lanes = slice(j * part, (j + 1) * part)
            line = [value[base + t * rows : base + (t + 1) * rows, lanes] for t in range(4)]
            out_ref[i_y, j] = jnp.concatenate(line, axis=1)


def inner_grad_kernel(left, right, before, out_ref):
    value = rounded(dot(left[...], right[...], 0, 0))
    out_ref[...] = value.reshape(out_ref.shape)


def feed_grad(normed, grad_gate, hidden, grad_feed):
    dp = lax.axis_size("dp")
    tokens, model = normed.shape
    inner = grad_gate.shape[1]
    rows, cols = model // dp, inner // 4
    shape = jax.ShapeDtypeStruct((dp, 4, 2 * rows, cols), BF)
    params = pltpu.CompilerParams(vmem_limit_bytes=VMEM_LIMIT)
    cost = pl.CostEstimate(
        flops=2 * tokens * model * inner,
        bytes_accessed=2 * (tokens * (model + inner) + model * inner),
        transcendentals=0,
    )
    outer = pl.pallas_call(
        outer_grad_kernel,
        grid=(dp // 2,),
        in_specs=[
            pl.BlockSpec((tokens, 2 * inner // dp), lambda i: (0, i)),
            pl.BlockSpec((tokens, model), lambda i: (0, 0)),
        ],
        out_specs=pl.BlockSpec((2, 4, rows, cols), lambda i: (i, 0, 1, 0)),
        out_shape=shape,
        compiler_params=params,
        cost_estimate=cost,
    )(hidden, grad_feed)
    return pl.pallas_call(
        inner_grad_kernel,
        grid=(4,),
        in_specs=[
            pl.BlockSpec((tokens, model), lambda i: (0, 0)),
            pl.BlockSpec((tokens, cols), lambda i: (0, i)),
            pl.BlockSpec(memory_space=pl.ANY),
        ],
        out_specs=pl.BlockSpec((dp, 1, rows, cols), lambda i: (0, i, 0, 0)),
        out_shape=shape,
        input_output_aliases={2: 0},
        compiler_params=params,
        cost_estimate=cost,
    )(normed, grad_gate, outer)


def group_grad(kind, place, left, right, first, total, before=None, parts=1):
    dp = lax.axis_size("dp")
    depth = dp // 2
    tokens, height = left.shape
    width = right.shape[1]
    if kind == "tall":
        rows, cols = width // 8, 2 * height // dp
    else:
        rows, cols = height // dp, width // 4 // parts
    whole = jax.ShapeDtypeStruct((2, 2, depth, total * rows, cols), BF)
    block = (2, 2, depth, rows, cols)
    if kind == "wide":
        kernel, grid, operands = wide_grad_kernel, (parts, 2), [left, right, right]
        specs = [
            pl.BlockSpec((tokens, height), lambda p, i, m: (0, 0)),
            pl.BlockSpec((tokens, cols), lambda p, i, m: (0, p * 4 + (m[2] ^ i) * 2 + m[3])),
            pl.BlockSpec((tokens, cols), lambda p, i, m: (0, p * 4 + (m[2] ^ i) * 2 + 1 - m[3])),
        ]
        out_spec = pl.BlockSpec(block, lambda p, i, m: (0, 0, 0, first + p, 0))
    else:
        kernel, grid, operands = tall_grad_kernel, (1,), [left, right]
        specs = [
            pl.BlockSpec((tokens, height), lambda i, m: (0, 0)),
            pl.BlockSpec((tokens, width), lambda i, m: (0, 0)),
        ]
        out_spec = pl.BlockSpec(block, lambda i, m: (0, 0, 0, first, 0))
    aliases = {}
    if before is not None:
        aliases = {1 + len(operands): 0, 2 + len(operands): 1}
        operands = operands + list(before)
        specs = specs + [pl.BlockSpec(memory_space=pl.ANY)] * 2
    return pl.pallas_call(
        kernel,
        grid_spec=pltpu.PrefetchScalarGridSpec(
            num_scalar_prefetch=1, grid=grid, in_specs=specs, out_specs=[out_spec] * 2
        ),
        out_shape=[whole, whole],
        input_output_aliases=aliases,
        compiler_params=pltpu.CompilerParams(vmem_limit_bytes=VMEM_LIMIT),
        cost_estimate=pl.CostEstimate(
            flops=2 * tokens * height * width,
            bytes_accessed=2 * (left.size + right.size + height * width),
            transcendentals=0,
        ),
    )(place, *operands)


def wide_sum(*values):
    total = values[0].astype(F32)
    for value in values[1:]:
        total = total + value.astype(F32)
    return total


def sum_group(pieces):
    kept, sent = pieces
    got = over_core(sent)
    out_b = rounded(wide_sum(kept[1], got[1]))
    yield out_b
    got_b = over_b(out_b)
    out_a = rounded(wide_sum(kept[0, 1], got[0, 1], got_b[1]))
    yield out_a
    got_a = over_a(out_a)
    line = rounded(wide_sum(kept[0, 0], got[0, 0], got_b[0], got_a))
    yield line
    yield wide_sum(line[0], *[over_z(line[k], k) for k in range(1, line.shape[0])])


def butterfly(value):
    k = 1
    while k < lax.axis_size("dp") // 2:
        value = value + over_z(value, k)
        k *= 2
    for step in (over_a, over_b, over_core):
        value = value + step(value)
    return value


def triple_grad_kernel(place_ref, left, right, kept, sent):
    value = rounded(dot(left[...], right[...], 0, 0))
    rows = kept.shape[1]
    z, y = place_ref[0], place_ref[1]
    for out, flip in ((kept, 0), (sent, 1)):
        for i_y in range(2):

            @pl.when((y ^ i_y) == flip)
            def _():
                for i_z in range(kept.shape[0]):
                    top = (i_z * 2 + i_y) * rows
                    out[i_z ^ z] = value[top : top + rows]


def triple_sum(place, left, right):
    dp = lax.axis_size("dp")
    rows, cols = left.shape[1] // dp, right.shape[1]
    shape = jax.ShapeDtypeStruct((dp // 2, rows, cols), BF)
    kept, sent = pl.pallas_call(
        triple_grad_kernel,
        in_specs=[smem_spec(), vmem_spec(), vmem_spec()],
        out_specs=[vmem_spec()] * 2,
        out_shape=[shape, shape],
        compiler_params=pltpu.CompilerParams(vmem_limit_bytes=VMEM_LIMIT),
        cost_estimate=pl.CostEstimate(
            flops=2 * left.size * cols, bytes_accessed=2 * (left.size + right.size), transcendentals=0
        ),
    )(place, left, right)
    line = rounded(wide_sum(kept, swap(sent, "dp", 1)))
    return wide_sum(line[0], *[swap(line[k], "dp", 2 * k) for k in range(1, dp // 2)])


def lane_mask(shape, head):
    lanes = lax.broadcasted_iota(jnp.int32, shape, len(shape) - 1)
    return (lanes >= head * HD) & (lanes < (head + 1) * HD)


def transposed(value):
    return value.astype(F32).T


def block_bias(bias_ref, head, query_block, key_block):
    distance = query_block - key_block
    kept = bias_ref[head, jnp.clip(distance, 0, NB - 1)]
    return jnp.where(distance >= 0, kept, NEGATIVE)


def self_fwd_kernel(pos_ref, bias_ref, qkv_ref, o_ref, lse_ref, kh_ref, vt_ref, s_ref, acc_ref):
    heads = kh_ref.shape[0]
    width = heads * HD
    devs, _, rows = vt_ref.shape
    per = rows // BLOCK
    a = pl.program_id(0)
    pos = pos_ref[0]

    @pl.when(a == 0)
    def _():
        for h in range(heads):
            kh_ref[h] = qkv_ref[:, width + h * HD : width + (h + 1) * HD]
        for d in range(devs):
            vt_ref[d] = rounded(transposed(qkv_ref[d * rows : (d + 1) * rows, 2 * width :]))

    first = pl.multiple_of(((a // per) ^ pos) * rows + (a % per) * BLOCK, BLOCK)
    qt = rounded(transposed(qkv_ref[pl.ds(first, BLOCK), :width]) * HD**-0.5)

    def scores(d, tops):
        where = pl.multiple_of((d ^ pos) * rows, rows)
        out = []
        for h in range(heads):
            raw = dot(kh_ref[h, pl.ds(where, rows), :], qt[h * HD : (h + 1) * HD])
            top = tops[h]
            for half in range(per):
                c = block_bias(bias_ref, h, a, d * per + half)
                piece = raw[half * BLOCK : (half + 1) * BLOCK] + c
                s_ref[h, pl.ds(pl.multiple_of(d * rows + half * BLOCK, BLOCK), BLOCK), :] = piece
                top = jnp.maximum(top, jnp.max(piece.reshape(BLOCK // 8, 8, BLOCK), axis=0))
            out.append(top)
        return tuple(out)

    count = a // per + 1
    tops = lax.fori_loop(
        0, count, scores, tuple(jnp.full((8, BLOCK), NEGATIVE, F32) for _ in range(heads))
    )
    tops = [jnp.max(t, axis=0, keepdims=True) for t in tops]
    acc_ref[...] = jnp.zeros_like(acc_ref)

    def mix(d, sums):
        out = []
        slot = d ^ pos
        for h in range(heads):
            e = jnp.exp(s_ref[h, pl.ds(pl.multiple_of(d * rows, rows), rows), :] - tops[h])
            out.append(sums[h] + jnp.sum(e.reshape(rows // 8, 8, BLOCK), axis=0))
            acc_ref[h * HD : (h + 1) * HD, :] += dot(
                vt_ref[slot, h * HD : (h + 1) * HD, :], rounded(e)
            )
        return tuple(out)

    sums = lax.fori_loop(
        0, count, mix, tuple(jnp.zeros((8, BLOCK), F32) for _ in range(heads))
    )
    for h in range(heads):
        total = jnp.sum(sums[h], axis=0, keepdims=True)
        lse_ref[a, h : h + 1, :] = tops[h] + jnp.log(total)
        acc_ref[h * HD : (h + 1) * HD, :] = acc_ref[h * HD : (h + 1) * HD, :] / total
    o_ref[pl.ds(first, BLOCK), :] = rounded(acc_ref[...].T)


def self_fwd(pos, bias, qkv, rows):
    tokens, triple = qkv.shape
    width = triple // 3
    heads = width // HD
    blocks = tokens // BLOCK
    return pl.pallas_call(
        self_fwd_kernel,
        grid=(blocks,),
        in_specs=[smem_spec(), smem_spec(), vmem_spec()],
        out_specs=[vmem_spec(), vmem_spec()],
        out_shape=[
            jax.ShapeDtypeStruct((tokens, width), BF),
            jax.ShapeDtypeStruct((blocks, 8, BLOCK), F32),
        ],
        scratch_shapes=[
            pltpu.VMEM((heads, tokens, HD), BF),
            pltpu.VMEM((tokens // rows, width, rows), BF),
            pltpu.VMEM((heads, tokens, BLOCK), F32),
            pltpu.VMEM((width, BLOCK), F32),
        ],
        compiler_params=pltpu.CompilerParams(vmem_limit_bytes=VMEM_LIMIT),
        cost_estimate=pl.CostEstimate(
            flops=2 * tokens * tokens * width * 2, bytes_accessed=8 * tokens * width,
            transcendentals=tokens * tokens * heads // 2,
        ),
    )(pos.reshape(1), bias, qkv)


def self_bwd_kernel(
    pos_ref, bias_ref, qkv_ref, o_ref, go_ref, lse_ref, dqkv_ref, bsum_ref,
    kh_ref, vh_ref, kt_ref, qm_ref, gm_ref, p_ref, ds_ref, dst_ref, dq_ref, dk_ref, dv_ref,
):
    heads = kh_ref.shape[0]
    width = heads * HD
    devs, _, rows = kt_ref.shape
    per = rows // BLOCK
    a = pl.program_id(0)
    pos = pos_ref[0]

    @pl.when(a == 0)
    def _():
        for h in range(heads):
            kh_ref[h] = qkv_ref[:, width + h * HD : width + (h + 1) * HD]
            vh_ref[h] = qkv_ref[:, 2 * width + h * HD : 2 * width + (h + 1) * HD]
        for d in range(devs):
            kt_ref[d] = rounded(transposed(qkv_ref[d * rows : (d + 1) * rows, width : 2 * width]))
        dk_ref[...] = jnp.zeros_like(dk_ref)
        dv_ref[...] = jnp.zeros_like(dv_ref)
        bsum_ref[...] = jnp.zeros_like(bsum_ref)

    first = pl.multiple_of(((a // per) ^ pos) * rows + (a % per) * BLOCK, BLOCK)
    q = qkv_ref[pl.ds(first, BLOCK), :width] * jnp.asarray(HD**-0.5, BF)
    go = go_ref[pl.ds(first, BLOCK), :]
    qt = rounded(transposed(q))
    got = transposed(go)
    prod = got * transposed(o_ref[pl.ds(first, BLOCK), :])
    got = rounded(got)
    zero = jnp.zeros((BLOCK, width), BF)
    dots, lses = [], []
    for h in range(heads):
        mask = lane_mask((BLOCK, width), h)
        qm_ref[h * BLOCK : (h + 1) * BLOCK, :] = jnp.where(mask, q, zero)
        gm_ref[h * BLOCK : (h + 1) * BLOCK, :] = jnp.where(mask, go, zero)
        dots.append(jnp.sum(prod[h * HD : (h + 1) * HD], axis=0, keepdims=True))
        lses.append(lse_ref[a, h : h + 1, :])
    dq_ref[...] = jnp.zeros_like(dq_ref)

    def step(d, carry):
        where = pl.multiple_of((d ^ pos) * rows, rows)
        slot = d ^ pos
        for h in range(heads):
            lanes = slice(h * HD, (h + 1) * HD)
            cols = slice(h * BLOCK, (h + 1) * BLOCK)
            raw = dot(kh_ref[h, pl.ds(where, rows), :], qt[lanes])
            gp = dot(vh_ref[h, pl.ds(where, rows), :], got[lanes])
            for half in range(per):
                part = slice(half * BLOCK, (half + 1) * BLOCK)
                key_block = d * per + half
                c = block_bias(bias_ref, h, a, key_block)
                pf = jnp.exp(raw[part] + (c - lses[h]))
                p_ref[part, cols] = rounded(pf)
                ds = rounded(pf * (gp[part] - dots[h]))
                ds_ref[part, cols] = ds
                dst_ref[h, part, :] = ds
                bucket = jnp.clip(a - key_block, 0, NB - 1)
                bsum_ref[h, bucket] += jnp.sum(
                    ds.astype(F32).reshape(BLOCK // 8, 8, BLOCK), axis=0
                )
            dq_ref[lanes, :] += dot(kt_ref[slot, lanes, :], dst_ref[h])
        dv_ref[pl.ds(where, rows), :] += dot(p_ref[...], gm_ref[...])
        dk_ref[pl.ds(where, rows), :] += dot(ds_ref[...], qm_ref[...])
        return carry

    lax.fori_loop(0, a // per + 1, step, 0)
    dqkv_ref[pl.ds(first, BLOCK), :width] = rounded(dq_ref[...].T * HD**-0.5)

    @pl.when(a == pl.num_programs(0) - 1)
    def _():
        dqkv_ref[:, width : 2 * width] = rounded(dk_ref[...])
        dqkv_ref[:, 2 * width :] = rounded(dv_ref[...])


def self_bwd(pos, bias, qkv, mixed, grad, lse, rows):
    tokens, triple = qkv.shape
    width = triple // 3
    heads = width // HD
    blocks = tokens // BLOCK
    return pl.pallas_call(
        self_bwd_kernel,
        grid=(blocks,),
        in_specs=[smem_spec(), smem_spec()] + [vmem_spec()] * 4,
        out_specs=[vmem_spec(), vmem_spec()],
        out_shape=[
            jax.ShapeDtypeStruct((tokens, triple), BF),
            jax.ShapeDtypeStruct((heads, NB, 8, BLOCK), F32),
        ],
        scratch_shapes=[
            pltpu.VMEM((heads, tokens, HD), BF),
            pltpu.VMEM((heads, tokens, HD), BF),
            pltpu.VMEM((tokens // rows, width, rows), BF),
            pltpu.VMEM((heads * BLOCK, width), BF),
            pltpu.VMEM((heads * BLOCK, width), BF),
            pltpu.VMEM((rows, heads * BLOCK), BF),
            pltpu.VMEM((rows, heads * BLOCK), BF),
            pltpu.VMEM((heads, rows, BLOCK), BF),
            pltpu.VMEM((width, BLOCK), F32),
            pltpu.VMEM((tokens, width), F32),
            pltpu.VMEM((tokens, width), F32),
        ],
        compiler_params=pltpu.CompilerParams(vmem_limit_bytes=VMEM_LIMIT),
        cost_estimate=pl.CostEstimate(
            flops=5 * tokens * tokens * width * 2, bytes_accessed=16 * tokens * width,
            transcendentals=tokens * tokens * heads // 2,
        ),
    )(pos.reshape(1), bias, qkv, mixed, grad, lse)


def slotted(value, pad_ref):
    rows = value.shape[0]
    rolled = pltpu.roll(value.astype(F32), 1, 0)
    first = lax.broadcasted_iota(jnp.int32, rolled.shape, 0) == 0
    pad_ref[:rows] = rounded(jnp.where(first, 0.0, rolled))
    pad_ref[rows:] = rounded(jnp.where(first, rolled, 0.0)[:SEGMENT])


def unslotted(pad_ref, rows):
    value = pad_ref[:rows]
    first = lax.broadcasted_iota(jnp.int32, value.shape, 0) == 0
    value = jnp.where(first, jnp.broadcast_to(pad_ref[rows : rows + 1], value.shape), value)
    return pltpu.roll(value, rows - 1, 0)


def masked_stack(value, group):
    return jnp.concatenate(
        [jnp.where(lane_mask(value.shape, h), value, jnp.zeros_like(value)) for h in range(group)], 0
    )


def cross_soft(keys, stacked):
    s = dot(keys, stacked, 1, 1)
    top = jnp.max(s, axis=0, keepdims=True)
    e = jnp.exp(s - top)
    return e / jnp.sum(e, axis=0, keepdims=True)


def merged(tall, group):
    rows, width = tall.shape[0] // group, tall.shape[1]
    out = jnp.zeros((rows, width), F32)
    for h in range(group):
        out = jnp.where(lane_mask((rows, width), h), tall[h * rows : (h + 1) * rows], out)
    return out


def cross_fwd_kernel(q_ref, k_ref, v_ref, out_ref, qp_ref, op_ref):
    slot = pl.program_id(0)
    rows = q_ref.shape[0]
    lanes = 4 * HD

    @pl.when(slot == 0)
    def _():
        slotted(q_ref[...], qp_ref)

    here = pl.ds(pl.multiple_of(slot * SEGMENT, SEGMENT), SEGMENT)
    scaled = qp_ref[here, :] * jnp.asarray(HD**-0.5, BF)
    for g in range(q_ref.shape[1] // lanes):
        part = slice(g * lanes, (g + 1) * lanes)
        soft = rounded(cross_soft(k_ref[:, part], masked_stack(scaled[:, part], 4)))
        op_ref[here, part] = merged(dot(soft, v_ref[:, part], 0, 0), 4)

    @pl.when(slot == pl.num_programs(0) - 1)
    def _():
        out_ref[...] = rounded(unslotted(op_ref, rows))


def cross_fwd(queries, pairs, neigh_rows):
    rows, width = queries.shape
    slots = rows // SEGMENT + 1
    return pl.pallas_call(
        cross_fwd_kernel,
        grid=(slots,),
        in_specs=[
            vmem_spec(),
            pl.BlockSpec((neigh_rows, width), lambda i: (i, 0)),
            pl.BlockSpec((neigh_rows, width), lambda i: (i, 1)),
        ],
        out_specs=vmem_spec(),
        out_shape=jax.ShapeDtypeStruct((rows, width), BF),
        scratch_shapes=[
            pltpu.VMEM((slots * SEGMENT, width), BF),
            pltpu.VMEM((slots * SEGMENT, width), F32),
        ],
        compiler_params=pltpu.CompilerParams(vmem_limit_bytes=VMEM_LIMIT),
        cost_estimate=pl.CostEstimate(
            flops=16 * slots * SEGMENT * neigh_rows * width, bytes_accessed=2 * pairs.size,
            transcendentals=slots * neigh_rows * width,
        ),
    )(queries, pairs, pairs)


def cross_bwd_kernel(q_ref, g_ref, k_ref, v_ref, dq_ref, dkv_ref, qp_ref, gp_ref, op_ref):
    slot = pl.program_id(0)
    rows, width = q_ref.shape
    lanes = 4 * HD

    @pl.when(slot == 0)
    def _():
        slotted(q_ref[...], qp_ref)
        slotted(g_ref[...], gp_ref)

    here = pl.ds(pl.multiple_of(slot * SEGMENT, SEGMENT), SEGMENT)
    scaled = qp_ref[here, :] * jnp.asarray(HD**-0.5, BF)
    grads = gp_ref[here, :]
    for g in range(width // lanes):
        part = slice(g * lanes, (g + 1) * lanes)
        queries = masked_stack(scaled[:, part], 4)
        grad = masked_stack(grads[:, part], 4)
        soft = cross_soft(k_ref[:, part], queries)
        gp = dot(v_ref[:, part], grad, 1, 1)
        ds = rounded(soft * (gp - jnp.sum(soft * gp, axis=0, keepdims=True)))
        op_ref[here, part] = merged(dot(ds, k_ref[:, part], 0, 0), 4) * HD**-0.5
        dkv_ref[:, part] = rounded(dot(ds, queries))
        dkv_ref[:, width + g * lanes : width + (g + 1) * lanes] = rounded(dot(rounded(soft), grad))

    @pl.when(slot == pl.num_programs(0) - 1)
    def _():
        dq_ref[...] = rounded(unslotted(op_ref, rows))


def cross_bwd(queries, grads, pairs, neigh_rows):
    rows, width = queries.shape
    slots = rows // SEGMENT + 1
    return pl.pallas_call(
        cross_bwd_kernel,
        grid=(slots,),
        in_specs=[
            vmem_spec(),
            vmem_spec(),
            pl.BlockSpec((neigh_rows, width), lambda i: (i, 0)),
            pl.BlockSpec((neigh_rows, width), lambda i: (i, 1)),
        ],
        out_specs=[vmem_spec(), pl.BlockSpec((neigh_rows, 2 * width), lambda i: (i, 0))],
        out_shape=[
            jax.ShapeDtypeStruct((rows, width), BF),
            jax.ShapeDtypeStruct(pairs.shape, BF),
        ],
        scratch_shapes=[
            pltpu.VMEM((slots * SEGMENT, width), BF),
            pltpu.VMEM((slots * SEGMENT, width), BF),
            pltpu.VMEM((slots * SEGMENT, width), F32),
        ],
        compiler_params=pltpu.CompilerParams(vmem_limit_bytes=VMEM_LIMIT),
        cost_estimate=pl.CostEstimate(
            flops=40 * slots * SEGMENT * neigh_rows * width, bytes_accessed=4 * pairs.size,
            transcendentals=slots * neigh_rows * width,
        ),
    )(queries, grads, pairs, pairs)


def on_device(
    tokens, neighbours, norm_gains, position_bias, query_self, key_self, value_self, output_self,
    query_cross, key_cross, value_cross, output_cross, inner_weight, outer_weight, cotangent,
):
    dp, seq = lax.axis_size("dp"), lax.axis_size("seq")
    rows, model = tokens.shape[1], tokens.shape[2]
    heads = position_bias.shape[0]
    width = heads * HD
    segments = rows // SEGMENT
    neigh_rows = neighbours.shape[2] * neighbours.shape[3]
    span = min(seq, max(2, SEQ_MIN // rows))
    group_width = width // span
    group_heads = heads // span
    my_dp = lax.axis_index("dp")
    pos = lax.axis_index("seq") % span

    fast = seq == 4 and span == 4 and rows % (2 * BLOCK) == 0 and model == 896
    place = my_place() if fast else None

    def whole(shard):
        return assemble(lax.all_gather(shard, BOTH, axis=0, tiled=False), dp, seq)

    triple = jnp.concatenate([query_self, key_self, value_self], axis=1)
    if fast:
        line = jnp.stack([triple] + [swap(triple, "dp", 2 * k) for k in range(1, dp // 2)])
        triple_full = reorder_triple(line, swap(line, "dp", 1), place)

        def turned(shard):
            flat = shard.T
            half = flat.shape[0] // 2
            return jnp.concatenate([flat[:half], flat[half:]], axis=1)

        packed = jnp.concatenate(
            [key_cross, value_cross, query_cross, turned(output_self), turned(output_cross)], axis=0
        )
        recall_full, query_full, output_turned, cross_turned = assemble_attention(
            gather_group(after(packed, line)), place
        )
        part = outer_weight.shape[0] // 4
        line = [outer_weight[t * part : (t + 1) * part] for t in range(4)]
        packed = jnp.concatenate([inner_weight, jnp.concatenate(line, axis=1)], axis=0)
        feed_blocks = lax.all_gather(packed, BOTH, axis=0, tiled=False)
        inner_full, outer_full = assemble_feed(feed_blocks)
    else:
        pieces = []
        for shard in (query_self, key_self, value_self):
            pieces.append(lax.dynamic_slice_in_dim(whole(shard), pos * group_width, group_width, 1))
        triple_full = jnp.concatenate(pieces, axis=1)
        recall_full = jnp.concatenate([whole(key_cross), whole(value_cross)], axis=1)
        query_full = whole(query_cross)
        output_turned, cross_turned = whole(output_self).T, whole(output_cross).T
        inner_full, outer_full = whole(inner_weight), whole(outer_weight)

    own_tokens = tokens.reshape(rows, model)
    pieces_tok = {0: own_tokens}
    bit = span // 2
    while bit:
        for k in list(pieces_tok):
            pieces_tok[k | bit] = swap(pieces_tok[k], "seq", bit)
        bit //= 2
    states = neighbours.reshape(segments * neigh_rows, model)
    forward_pairs = [(i, i + 1) for i in range(seq - 1) if (i + 1) % span]
    back_pairs = [(i + 1, i) for i in range(seq - 1) if (i + 1) % span]
    edge = lax.ppermute(states[(segments - 1) * neigh_rows :], "seq", forward_pairs)
    states_all = lax.optimization_barrier(jnp.concatenate([edge, states], axis=0))

    inputs = own_tokens.astype(F32)
    upstream = cotangent.reshape(rows, model).astype(F32)
    first_normed = jnp.concatenate(
        [rounded(rms_apply(pieces_tok[k].astype(F32), norm_gains[0])) for k in range(span)], axis=0
    )
    qkv = rounded(linear(first_normed, triple_full))
    bias = lax.dynamic_slice_in_dim(position_bias, pos * group_heads, group_heads, 0)
    mixed_group, lse = self_fwd(pos, bias, qkv, rows)

    def exchanged(stack):
        return [stack[0]] + [swap(stack[k], "seq", k) for k in range(1, span)]

    mixed_blocks = mixed_group.reshape(span, rows, group_width)
    mixed_self = columns_from_blocks(jnp.stack(exchanged(mixed_blocks)), pos)

    recall_pairs = rounded(linear(states_all, recall_full))

    after_self = inputs + input_grad(mixed_self, output_turned)
    second_normed = rounded(rms_apply(after_self, norm_gains[1]))
    cross_queries = rounded(linear(second_normed, query_full))
    mixed_cross = cross_fwd(cross_queries, recall_pairs, neigh_rows)
    after_cross = after_self + input_grad(mixed_cross, cross_turned)
    third_normed = rounded(rms_apply(after_cross, norm_gains[2]))
    gate_value = linear(third_normed, inner_full)
    activated, gelu_pull = jax.vjp(gelu_tanh, gate_value)
    hidden_act = rounded(activated)
    outcome = after_cross + linear(hidden_act, outer_full)

    grad_feed = rounded(upstream)
    grad_hidden = input_grad(grad_feed, outer_full)
    grad_gate = rounded(gelu_pull(grad_hidden)[0])
    if fast:
        blocks = feed_grad(third_normed, grad_gate, hidden_act, grad_feed)
        blocks = blocks.reshape((dp * seq,) + blocks.shape[2:])
        own = lax.psum_scatter(blocks, BOTH, scatter_dimension=0, tiled=True)[0].astype(F32)
        part = own.shape[0] // 2
        sum_inner = own[:part]
        sum_outer = own[part:].reshape(part, 4, model // 4).transpose(1, 0, 2).reshape(4 * part, -1)
    else:
        sum_outer = block_sum(hidden_act, grad_feed)
        sum_inner = block_sum(third_normed, grad_gate)
    norm_grad, gain_three = norm_back(after_cross, norm_gains[2], input_grad(grad_gate, inner_full))
    grad_late = upstream + norm_grad

    grad_cross = rounded(grad_late)
    grad_mixed = rounded(linear(grad_cross, cross_turned))
    probe, pair_round = cross_bwd(cross_queries, grad_mixed, recall_pairs, neigh_rows)

    def turned_back(own):
        half = own.shape[1] // 2
        return jnp.concatenate([own[:, :half].T, own[:, half:].T], axis=1)

    if fast:
        pieces = group_grad("tall", place, mixed_cross, grad_cross, 3, 5)
        pieces = group_grad("wide", place, second_normed, probe, 2, 5, pieces)
        pieces = group_grad("wide", place, states_all, pair_round, 0, 5, pieces, 2)
    else:
        sum_cross = block_sum(mixed_cross, grad_cross)
        sum_key = block_sum(states_all, pair_round[:, :width])
        sum_value = block_sum(states_all, pair_round[:, width:])
        sum_query = block_sum(second_normed, probe)
    norm_grad, gain_two = norm_back(after_self, norm_gains[1], input_grad(probe, query_full))
    grad_early = grad_late + norm_grad
    states_round = rounded(input_grad(pair_round, recall_full))
    returned = lax.ppermute(states_round[:neigh_rows], "seq", back_pairs)
    last = states_round[segments * neigh_rows :].astype(F32) + returned.astype(F32)
    grad_states = jnp.concatenate(
        [states_round[neigh_rows : segments * neigh_rows], rounded(last)], axis=0
    )

    grad_self = rounded(grad_early)
    if fast:
        steps = sum_group(group_grad("tall", place, mixed_self, grad_self, 4, 5, pieces))
        sent_b = next(steps)
        sent_a = next(steps)
        sent_z = next(steps)
        own = next(steps)
        part = own.shape[0] // 5
        sum_key, sum_value, sum_query = (own[i * part : (i + 1) * part] for i in range(3))
        sum_cross = turned_back(own[3 * part : 4 * part])
        sum_output = turned_back(own[4 * part :])
    else:
        sum_output = block_sum(mixed_self, grad_self)
    grad_attended = rounded(linear(grad_self, output_turned))
    group_grads = exchanged(blocks_from_columns(grad_attended, span, pos))
    grad_group = jnp.concatenate(group_grads, axis=0)
    if fast:
        grad_group = after(grad_group, sent_b)
    triple_grad, bias_sums = self_bwd(pos, bias, qkv, mixed_group, grad_group, lse, rows)
    partial = input_grad(triple_grad, triple_full)
    all_tokens = jnp.concatenate([pieces_tok[k] for k in range(span)], axis=0).astype(F32)
    factor = lax.rsqrt(jnp.mean(all_tokens * all_tokens, axis=-1, keepdims=True) + EPSILON)
    gain_one = jnp.sum(partial * all_tokens * factor, axis=0)
    partial = rounded(partial).reshape(span, rows, model)
    blocks = {k: partial[k] for k in range(span)}
    bit = 1
    while bit < span:
        for k in sorted(blocks):
            if not k & bit:
                got = swap(blocks[k | bit], "seq", bit)
                blocks[k] = blocks[k].astype(F32) + got.astype(F32)
                if bit * 2 < span and k:
                    blocks[k] = rounded(blocks[k])
        blocks = {k: v for k, v in blocks.items() if not k & bit}
        bit *= 2
    norm_grad, _ = norm_back(inputs, norm_gains[0], blocks[0])
    grad_inputs = grad_early + norm_grad

    if fast:
        own = triple_sum(place, first_normed, triple_grad)
        own_self = [own[:, i * group_width : (i + 1) * group_width] for i in range(3)]
    else:
        own_self = []
        for i in range(3):
            columns = triple_grad[:, i * group_width : (i + 1) * group_width]
            wide = jnp.zeros((span * rows, width), BF)
            wide = lax.dynamic_update_slice_in_dim(wide, columns, pos * group_width, 1)
            own_self.append(block_sum(first_normed, wide))

    bias_local = jnp.sum(bias_sums, axis=(2, 3))
    bias_all = lax.dynamic_update_slice_in_dim(
        jnp.zeros((heads, NB), F32), bias_local, pos * group_heads, 0
    )
    small = jnp.concatenate([gain_one, gain_two, gain_three, bias_all.reshape(-1)])
    if fast:
        size = small.shape[0]
        small = jnp.pad(small, (0, -size % 1024)).reshape(-1, 128)
        small = butterfly(small).reshape(-1)[:size]
    else:
        small = lax.psum(small, BOTH)
    gains = small[: 3 * model].reshape(3, model)
    bias_total = small[3 * model :].reshape(heads, NB)
    return (
        rounded(outcome).reshape(1, rows, model),
        rounded(grad_inputs).reshape(1, rows, model),
        grad_states.reshape(neighbours.shape),
        gains,
        bias_total,
        own_self[0],
        own_self[1],
        own_self[2],
        sum_output,
        sum_query,
        sum_key,
        sum_value,
        sum_cross,
        sum_inner,
        sum_outer,
    )


def solution(mesh):
    weight = P("dp", "seq")
    lane = P("dp", "seq", None)
    wide = P("dp", "seq", None, None, None)
    return jax.shard_map(
        on_device,
        mesh=mesh,
        in_specs=(lane, wide, P(), P()) + (weight,) * 10 + (lane,),
        out_specs=(lane, lane, wide, P(), P()) + (weight,) * 10,
        check_vma=False,
    )
```

```python
import functools

import jax
import jax.numpy as jnp
from jax import lax
from jax.experimental import pallas as pl
from jax.experimental.pallas import tpu as pltpu
from jax.sharding import PartitionSpec as P

HD = 64
SEGMENT = 64
BLOCK = 256
NB = 6
SEQ_MIN = 2048
EPSILON = 1e-06
NEGATIVE = -1e30
BF = jnp.bfloat16
F32 = jnp.float32
VMEM_LIMIT = 56 * 2**20
BOTH = ("dp", "seq")


def dot(a, b, ca=1, cb=0):
    return lax.dot_general(a, b, (((ca,), (cb,)), ((), ())), preferred_element_type=F32)


def linear(a, b):
    return dot(a, b)


def input_grad(a, b):
    return dot(a, b, 1, 1)


def weight_grad(a, b):
    return dot(a, b, 0, 0)


def rounded(v):
    return v.astype(BF)


def rms_apply(inputs, gain_row):
    factor = lax.rsqrt(jnp.mean(inputs * inputs, axis=-1, keepdims=True) + EPSILON)
    return inputs * factor * gain_row


def norm_back(inputs, gain_row, upstream):
    normed_value, pullback = jax.vjp(rms_apply, inputs, gain_row)
    return pullback(upstream)


def gelu_tanh(operand):
    return jax.nn.gelu(operand, approximate=True)


def swap(value, axis, by):
    peers = lax.axis_size(axis)
    return lax.ppermute(value, axis, [(i, i ^ by) for i in range(peers)])


def after(value, *others):
    return lax.optimization_barrier((value,) + others)[0]


def estimate(flops, bytes_accessed, transcendentals):
    return pl.CostEstimate(
        flops=flops // 50, bytes_accessed=bytes_accessed // 50, transcendentals=transcendentals // 50
    )


def vmem_spec():
    return pl.BlockSpec(memory_space=pltpu.VMEM)


def smem_spec():
    return pl.BlockSpec(memory_space=pltpu.SMEM)


def reorder_triple_kernel(place_ref, near_ref, far_ref, out_ref):
    count, rows, _ = near_ref.shape
    z, y = place_ref[0], place_ref[1]
    for ref, flip in ((near_ref, 0), (far_ref, 1)):
        for k in range(count):
            where = ((z ^ k) * 2 + (y ^ flip)) * rows
            out_ref[pl.ds(pl.multiple_of(where, rows), rows), :] = ref[k]


def project_kernel(place_ref, near_ref, far_ref, gain_ref, *refs):
    tokens, (normed_ref, qkv_ref, full_ref) = refs[:-3], refs[-3:]
    reorder_triple_kernel(place_ref, near_ref, far_ref, full_ref)
    rows = tokens[0].shape[0]
    part = rows // 2
    for k, ref in enumerate(tokens):

        def step(i, carry):
            here = pl.ds(pl.multiple_of(i * part, part), part)
            there = pl.ds(pl.multiple_of(k * rows + i * part, part), part)
            normed = rounded(rms_apply(ref[here, :].astype(F32), gain_ref[...]))
            normed_ref[there, :] = normed
            qkv_ref[there, :] = rounded(dot(normed, full_ref[...]))
            return carry

        lax.fori_loop(0, 2, step, 0)


def project(near, far, gain, tokens, place):
    count, height, cols = near.shape
    rows, model = tokens[0].shape
    total = rows * len(tokens)
    return pl.pallas_call(
        project_kernel,
        in_specs=[smem_spec()] + [vmem_spec()] * (3 + len(tokens)),
        out_specs=[vmem_spec()] * 3,
        out_shape=[
            jax.ShapeDtypeStruct((total, model), BF),
            jax.ShapeDtypeStruct((total, cols), BF),
            jax.ShapeDtypeStruct((2 * count * height, cols), BF),
        ],
        compiler_params=pltpu.CompilerParams(vmem_limit_bytes=VMEM_LIMIT),
        cost_estimate=estimate(
            flops=2 * total * model * cols, bytes_accessed=8 * total * model, transcendentals=0
        ),
    )(place, near, far, gain, *tokens)


def join_kernel(mine_ref, *refs):
    out_ref = refs[-1]
    cols = refs[0].shape[1]
    for k, ref in enumerate(refs[:-1]):
        out_ref[:, pl.ds(pl.multiple_of((mine_ref[0] ^ k) * cols, cols), cols)] = ref[...]


def join_columns(pieces, mine):
    rows, cols = pieces[0].shape
    return pl.pallas_call(
        join_kernel,
        in_specs=[smem_spec()] + [vmem_spec()] * len(pieces),
        out_specs=vmem_spec(),
        out_shape=jax.ShapeDtypeStruct((rows, cols * len(pieces)), pieces[0].dtype),
    )(mine.reshape(1), *pieces)


def split_kernel(mine_ref, in_ref, *outs):
    cols = outs[0].shape[1]
    for k, ref in enumerate(outs):
        ref[...] = in_ref[:, pl.ds(pl.multiple_of((mine_ref[0] ^ k) * cols, cols), cols)]


def split_columns(flat, count, mine):
    rows, width = flat.shape
    return pl.pallas_call(
        split_kernel,
        in_specs=[smem_spec(), vmem_spec()],
        out_specs=[vmem_spec()] * count,
        out_shape=[jax.ShapeDtypeStruct((rows, width // count), flat.dtype)] * count,
    )(mine.reshape(1), flat)


def assemble(blocks, dp, seq):
    _, rows, cols = blocks.shape
    return blocks.reshape(dp, seq, rows, cols).transpose(0, 2, 1, 3).reshape(dp * rows, seq * cols)


def block_sum(left, right):
    dp, seq = lax.axis_size("dp"), lax.axis_size("seq")
    rows, cols = left.shape[1] // dp, right.shape[1] // seq
    blocks = rounded(weight_grad(left, right)).reshape(dp, rows, seq, cols).transpose(0, 2, 1, 3)
    blocks = blocks.reshape(dp * seq, rows, cols)
    return lax.psum_scatter(blocks, BOTH, scatter_dimension=0, tiled=True)[0].astype(F32)


def device_pairs(target):
    dp, pairs = lax.axis_size("dp"), []
    for i in range(dp):
        for j in range(4):
            z, y, x, c = target(i // 2, i % 2, j // 2, j % 2)
            pairs.append((i * 4 + j, (z * 2 + y) * 4 + x * 2 + c))
    return pairs


def over_z(value, k):
    return lax.ppermute(value, BOTH, device_pairs(lambda z, y, x, c: (z ^ k, y, x, c)))


def over_a(value):
    return lax.ppermute(
        value, BOTH, device_pairs(lambda z, y, x, c: (z, y ^ c, x ^ (1 - c), c))
    )


def over_b(value):
    return lax.ppermute(
        value, BOTH, device_pairs(lambda z, y, x, c: (z, y ^ (1 - c), x ^ c, c))
    )


def over_core(value):
    return lax.ppermute(value, BOTH, device_pairs(lambda z, y, x, c: (z, y, x, 1 - c)))


def my_place():
    i, j = lax.axis_index("dp"), lax.axis_index("seq")
    return jnp.stack([i // 2, i % 2, j // 2, j % 2]).astype(jnp.int32)


def gather_near(shard):
    depth = lax.axis_size("dp") // 2
    return [shard] + [over_z(shard, k) for k in range(1, depth)]


def piece_origin(place_ref, c, b, t, depth):
    z, y, x, core = (place_ref[i] for i in range(4))
    a, k = t // depth, t % depth
    core = core ^ c
    dx = jnp.where(core == 0, a, b)
    dy = jnp.where(core == 0, b, a)
    return (z ^ k) * 2 + (y ^ dy), (x ^ dx) * 2 + core


def assemble_attention_kernel(depth, place_ref, *refs):
    pieces, (recall, query, out_self, out_cross), sems = refs[:4], refs[4:8], refs[8]
    rows = query.shape[0] // (2 * depth)
    cols = query.shape[1] // 4
    half = cols // 2

    def step(t, carry):
        for i in range(4):
            i_dp, i_seq = piece_origin(place_ref, i // 2, i % 2, t, depth)
            down = pl.ds(pl.multiple_of(i_dp * rows, rows), rows)
            across = pl.multiple_of(i_seq * cols, cols)
            piece = pieces[i].at[t]

            def move(first, target, sem):
                pltpu.make_async_copy(piece.at[pl.ds(first, rows), :], target, sems.at[sem]).start()

            move(0, recall.at[down, pl.ds(across, cols)], 0)
            move(rows, recall.at[down, pl.ds(across + 4 * cols, cols)], 0)
            move(2 * rows, query.at[down, pl.ds(across, cols)], 1)
            lanes = pl.ds(pl.multiple_of(i_dp * half, half), half)
            for w, out in ((0, out_self), (1, out_cross)):
                for h in range(2):
                    top = pl.multiple_of((i_seq * 2 + h) * rows, rows)
                    pltpu.make_async_copy(
                        piece.at[pl.ds((3 + w) * rows, rows), pl.ds(h * half, half)],
                        out.at[pl.ds(top, rows), lanes],
                        sems.at[2 + w],
                    ).start()
        return carry

    lax.fori_loop(0, 2 * depth, step, 0)
    for sem, out in enumerate((recall, query, out_self, out_cross)):
        pltpu.make_async_copy(out, out, sems.at[sem]).wait()


def assemble_attention(pieces, place):
    count, packed, cols = pieces[0].shape
    rows = packed // 5
    model, width = rows * count, cols * 4
    shapes = [(model, 2 * width), (model, width), (8 * rows, width), (8 * rows, width)]
    return pl.pallas_call(
        functools.partial(assemble_attention_kernel, count // 2),
        in_specs=[smem_spec()] + [pl.BlockSpec(memory_space=pl.ANY)] * 4,
        out_specs=[vmem_spec()] * 4,
        out_shape=[jax.ShapeDtypeStruct(s, BF) for s in shapes],
        scratch_shapes=[pltpu.SemaphoreType.DMA((4,))],
        compiler_params=pltpu.CompilerParams(vmem_limit_bytes=VMEM_LIMIT),
    )(place, *pieces)


def assemble_feed_kernel(depth, place_ref, *refs):
    pieces, (inner, outer, stage, sems) = refs[:4], refs[4:]
    rows, cols = stage.shape[2:]
    part = cols // 4

    def step(t, carry):
        for i in range(4):
            i_dp, i_seq = piece_origin(place_ref, i // 2, i % 2, t, depth)
            piece = pieces[i].at[t]
            down = pl.ds(pl.multiple_of(i_dp * rows, rows), rows)
            across = pl.ds(pl.multiple_of(i_seq * cols, cols), cols)
            pltpu.make_async_copy(
                piece.at[pl.ds(rows, rows), :], stage.at[i_dp, i_seq], sems.at[1]
            ).start()
            pltpu.make_async_copy(
                piece.at[pl.ds(0, rows), :], inner.at[down, across], sems.at[0]
            ).start()
        return carry

    lax.fori_loop(0, 2 * depth, step, 0)
    pltpu.make_async_copy(stage, stage, sems.at[1]).wait()

    def spread(i, carry):
        for t in range(4):
            line = [stage[i, j, :, t * part : (t + 1) * part] for j in range(4)]
            where = pl.multiple_of((i * 4 + t) * rows, rows)
            outer[pl.ds(where, rows), :] = jnp.concatenate(line, axis=1)
        return carry

    lax.fori_loop(0, 2 * depth, spread, 0)
    pltpu.make_async_copy(inner, inner, sems.at[0]).wait()


def assemble_feed(pieces, place):
    deep, packed, cols = pieces[0].shape
    rows = packed // 2
    return pl.pallas_call(
        functools.partial(assemble_feed_kernel, deep // 2),
        in_specs=[smem_spec()] + [pl.BlockSpec(memory_space=pl.ANY)] * 4,
        out_specs=[vmem_spec()] * 2,
        out_shape=[
            jax.ShapeDtypeStruct((rows * deep, cols * 4), BF),
            jax.ShapeDtypeStruct((4 * rows * deep, cols), BF),
        ],
        scratch_shapes=[
            pltpu.VMEM((deep, 4, rows, cols), BF),
            pltpu.SemaphoreType.DMA((2,)),
        ],
        compiler_params=pltpu.CompilerParams(vmem_limit_bytes=VMEM_LIMIT),
    )(place, *pieces)


def put_block(place_ref, out_ref, core, i_dp, flip, value):
    z, y = place_ref[0], place_ref[1]
    dy = (i_dp % 2) ^ y
    b = jnp.where(core == 0, dy, flip)
    a = jnp.where(core == 0, flip, dy)
    out_ref[b, a, (i_dp // 2) ^ z] = value


def wide_grad_kernel(*refs):
    place_ref, left, kept_right, sent_right = refs[:4]
    kept, sent = refs[-2:]
    flip = pl.program_id(1)
    rows = kept.shape[3]
    core = place_ref[3]
    for right, out, c in ((kept_right, kept, core), (sent_right, sent, 1 - core)):
        value = rounded(dot(left[...], right[...], 0, 0))
        for i_dp in range(value.shape[0] // rows):
            put_block(place_ref, out, c, i_dp, flip, value[i_dp * rows : (i_dp + 1) * rows])


def tall_grad_kernel(*refs):
    place_ref, left, right = refs[:3]
    kept, sent = refs[-2:]
    rows, cols = kept.shape[3], kept.shape[4]
    half = cols // 2
    x, core = place_ref[2], place_ref[3]
    for j in range(4):
        value = rounded(dot(right[:, 2 * j * rows : 2 * (j + 1) * rows], left[...], 0, 0))
        for out, mine in ((kept, core == j % 2), (sent, core != j % 2)):

            @pl.when(mine)
            def _():
                for i_dp in range(value.shape[1] // half):
                    lanes = slice(i_dp * half, (i_dp + 1) * half)
                    block = jnp.concatenate([value[:rows, lanes], value[rows:, lanes]], axis=1)
                    put_block(place_ref, out, j % 2, i_dp, (j // 2) ^ x, block)


def feed_outer_kernel(place_ref, left, right, kept, sent):
    rows, cols = kept.shape[3:]
    part = cols // 4
    y, x, core = place_ref[1], place_ref[2], place_ref[3]
    value = rounded(dot(left[...], right[...], 0, 0))
    for j in range(4):
        for out, mine in ((kept, core == j % 2), (sent, core != j % 2)):

            @pl.when(mine)
            def _():
                for i_y in range(2):
                    base = i_y * 4 * rows
                    lanes = slice(j * part, (j + 1) * part)
                    line = [value[base + t * rows : base + (t + 1) * rows, lanes] for t in range(4)]
                    dy, flip = i_y ^ y, (j // 2) ^ x
                    b, a = (dy, flip) if j % 2 == 0 else (flip, dy)
                    out[b, a, 0] = jnp.concatenate(line, axis=1)


def feed_grad(place, normed, grad_gate, hidden, grad_feed):
    dp = lax.axis_size("dp")
    depth = dp // 2
    tokens, model = normed.shape
    inner = grad_gate.shape[1]
    rows, cols = model // dp, inner // 4
    shape = jax.ShapeDtypeStruct((2, 2, depth, 2 * rows, cols), BF)
    out_spec = pl.BlockSpec((2, 2, 1, rows, cols), lambda i, m: (0, 0, m[0] ^ i, 1, 0))
    pieces = pl.pallas_call(
        feed_outer_kernel,
        grid_spec=pltpu.PrefetchScalarGridSpec(
            num_scalar_prefetch=1,
            grid=(depth,),
            in_specs=[
                pl.BlockSpec((tokens, inner // depth), lambda i, m: (0, i)),
                pl.BlockSpec((tokens, model), lambda i, m: (0, 0)),
            ],
            out_specs=[out_spec] * 2,
        ),
        out_shape=[shape, shape],
        compiler_params=pltpu.CompilerParams(vmem_limit_bytes=VMEM_LIMIT),
        cost_estimate=estimate(
            flops=2 * tokens * model * inner,
            bytes_accessed=2 * (tokens * (model + inner) + model * inner),
            transcendentals=0,
        ),
    )(place, hidden, grad_feed)
    return group_grad("wide", place, normed, grad_gate, 0, 2, pieces)


def group_grad(kind, place, left, right, first, total, before=None, parts=1):
    dp = lax.axis_size("dp")
    depth = dp // 2
    tokens, height = left.shape
    width = right.shape[1]
    if kind == "tall":
        rows, cols = width // 8, 2 * height // dp
    else:
        rows, cols = height // dp, width // 4 // parts
    whole = jax.ShapeDtypeStruct((2, 2, depth, total * rows, cols), BF)
    block = (2, 2, depth, rows, cols)
    if kind == "wide":
        kernel, grid, operands = wide_grad_kernel, (parts, 2), [left, right, right]
        specs = [
            pl.BlockSpec((tokens, height), lambda p, i, m: (0, 0)),
            pl.BlockSpec((tokens, cols), lambda p, i, m: (0, p * 4 + (m[2] ^ i) * 2 + m[3])),
            pl.BlockSpec((tokens, cols), lambda p, i, m: (0, p * 4 + (m[2] ^ i) * 2 + 1 - m[3])),
        ]
        out_spec = pl.BlockSpec(block, lambda p, i, m: (0, 0, 0, first + p, 0))
    else:
        kernel, grid, operands = tall_grad_kernel, (1,), [left, right]
        specs = [
            pl.BlockSpec((tokens, height), lambda i, m: (0, 0)),
            pl.BlockSpec((tokens, width), lambda i, m: (0, 0)),
        ]
        out_spec = pl.BlockSpec(block, lambda i, m: (0, 0, 0, first, 0))
    aliases = {}
    if before is not None:
        aliases = {1 + len(operands): 0, 2 + len(operands): 1}
        operands = operands + list(before)
        specs = specs + [pl.BlockSpec(memory_space=pl.ANY)] * 2
    return pl.pallas_call(
        kernel,
        grid_spec=pltpu.PrefetchScalarGridSpec(
            num_scalar_prefetch=1, grid=grid, in_specs=specs, out_specs=[out_spec] * 2
        ),
        out_shape=[whole, whole],
        input_output_aliases=aliases,
        compiler_params=pltpu.CompilerParams(vmem_limit_bytes=VMEM_LIMIT),
        cost_estimate=estimate(
            flops=2 * tokens * height * width,
            bytes_accessed=2 * (left.size + right.size + height * width),
            transcendentals=0,
        ),
    )(place, *operands)


def wide_sum(*values):
    total = values[0].astype(F32)
    for value in values[1:]:
        total = total + value.astype(F32)
    return total


def sum_second(kept, got, got_b):
    return rounded(wide_sum(kept[0, 1], got[0, 1], got_b[1]))


def sum_third(kept, got, got_b, got_a):
    return rounded(wide_sum(kept[0, 0], got[0, 0], got_b[0], got_a))


def sum_over_z(line):
    return wide_sum(line[0], *[over_z(line[k], k) for k in range(1, line.shape[0])])


def butterfly(value):
    k = 1
    while k < lax.axis_size("dp") // 2:
        value = value + over_z(value, k)
        k *= 2
    for step in (over_a, over_b, over_core):
        value = value + step(value)
    return value


def triple_grad_kernel(place_ref, left, right, kept, sent):
    value = rounded(dot(left[...], right[...], 0, 0))
    rows = kept.shape[1]
    z, y = place_ref[0], place_ref[1]
    for out, flip in ((kept, 0), (sent, 1)):
        for i_y in range(2):

            @pl.when((y ^ i_y) == flip)
            def _():
                for i_z in range(kept.shape[0]):
                    top = (i_z * 2 + i_y) * rows
                    out[i_z ^ z] = value[top : top + rows]


def triple_pieces(place, left, right):
    dp = lax.axis_size("dp")
    rows, cols = left.shape[1] // dp, right.shape[1]
    shape = jax.ShapeDtypeStruct((dp // 2, rows, cols), BF)
    return pl.pallas_call(
        triple_grad_kernel,
        in_specs=[smem_spec(), vmem_spec(), vmem_spec()],
        out_specs=[vmem_spec()] * 2,
        out_shape=[shape, shape],
        compiler_params=pltpu.CompilerParams(vmem_limit_bytes=VMEM_LIMIT),
        cost_estimate=estimate(
            flops=2 * left.size * cols, bytes_accessed=2 * (left.size + right.size), transcendentals=0
        ),
    )(place, left, right)


def lane_mask(shape, head):
    lanes = lax.broadcasted_iota(jnp.int32, shape, len(shape) - 1)
    return (lanes >= head * HD) & (lanes < (head + 1) * HD)


def transposed(value):
    return value.astype(F32).T


def block_bias(bias_ref, head, query_block, key_block):
    distance = query_block - key_block
    kept = bias_ref[head, jnp.clip(distance, 0, NB - 1)]
    return jnp.where(distance >= 0, kept, NEGATIVE)


def self_fwd_kernel(pos_ref, bias_ref, qkv_ref, o_ref, lse_ref, kh_ref, vt_ref, s_ref, acc_ref):
    heads = kh_ref.shape[0]
    width = heads * HD
    devs, _, rows = vt_ref.shape
    per = rows // BLOCK
    a = pl.program_id(0)
    pos = pos_ref[0]

    @pl.when(a == 0)
    def _():
        for h in range(heads):
            kh_ref[h] = qkv_ref[:, width + h * HD : width + (h + 1) * HD]
        for d in range(devs):
            vt_ref[d] = rounded(transposed(qkv_ref[d * rows : (d + 1) * rows, 2 * width :]))

    first = pl.multiple_of(((a // per) ^ pos) * rows + (a % per) * BLOCK, BLOCK)
    qt = rounded(transposed(qkv_ref[pl.ds(first, BLOCK), :width]) * HD**-0.5)

    def scores(d, tops):
        where = pl.multiple_of((d ^ pos) * rows, rows)
        out = []
        for h in range(heads):
            raw = dot(kh_ref[h, pl.ds(where, rows), :], qt[h * HD : (h + 1) * HD])
            top = tops[h]
            for half in range(per):
                c = block_bias(bias_ref, h, a, d * per + half)
                piece = raw[half * BLOCK : (half + 1) * BLOCK] + c
                s_ref[h, pl.ds(pl.multiple_of(d * rows + half * BLOCK, BLOCK), BLOCK), :] = piece
                top = jnp.maximum(top, jnp.max(piece.reshape(BLOCK // 8, 8, BLOCK), axis=0))
            out.append(top)
        return tuple(out)

    count = a // per + 1
    tops = lax.fori_loop(
        0, count, scores, tuple(jnp.full((8, BLOCK), NEGATIVE, F32) for _ in range(heads))
    )
    tops = [jnp.max(t, axis=0, keepdims=True) for t in tops]
    acc_ref[...] = jnp.zeros_like(acc_ref)

    def mix(d, sums):
        out = []
        slot = d ^ pos
        for h in range(heads):
            e = jnp.exp(s_ref[h, pl.ds(pl.multiple_of(d * rows, rows), rows), :] - tops[h])
            out.append(sums[h] + jnp.sum(e.reshape(rows // 8, 8, BLOCK), axis=0))
            acc_ref[h * HD : (h + 1) * HD, :] += dot(
                vt_ref[slot, h * HD : (h + 1) * HD, :], rounded(e)
            )
        return tuple(out)

    sums = lax.fori_loop(
        0, count, mix, tuple(jnp.zeros((8, BLOCK), F32) for _ in range(heads))
    )
    for h in range(heads):
        total = jnp.sum(sums[h], axis=0, keepdims=True)
        lse_ref[a, h : h + 1, :] = tops[h] + jnp.log(total)
        acc_ref[h * HD : (h + 1) * HD, :] = acc_ref[h * HD : (h + 1) * HD, :] / total
    o_ref[pl.ds(first, BLOCK), :] = rounded(acc_ref[...].T)


def self_fwd(pos, bias, qkv, rows):
    tokens, triple = qkv.shape
    width = triple // 3
    heads = width // HD
    blocks = tokens // BLOCK
    return pl.pallas_call(
        self_fwd_kernel,
        grid=(blocks,),
        in_specs=[smem_spec(), smem_spec(), vmem_spec()],
        out_specs=[vmem_spec(), vmem_spec()],
        out_shape=[
            jax.ShapeDtypeStruct((tokens, width), BF),
            jax.ShapeDtypeStruct((blocks, 8, BLOCK), F32),
        ],
        scratch_shapes=[
            pltpu.VMEM((heads, tokens, HD), BF),
            pltpu.VMEM((tokens // rows, width, rows), BF),
            pltpu.VMEM((heads, tokens, BLOCK), F32),
            pltpu.VMEM((width, BLOCK), F32),
        ],
        compiler_params=pltpu.CompilerParams(vmem_limit_bytes=VMEM_LIMIT),
        cost_estimate=estimate(
            flops=2 * tokens * tokens * width * 2, bytes_accessed=8 * tokens * width,
            transcendentals=tokens * tokens * heads // 2,
        ),
    )(pos.reshape(1), bias, qkv)


def self_bwd_kernel(
    pos_ref, bias_ref, qkv_ref, o_ref, go_ref, lse_ref, dqkv_ref, bsum_ref,
    kh_ref, vh_ref, kt_ref, qm_ref, gm_ref, p_ref, ds_ref, dst_ref, dq_ref, dk_ref, dv_ref,
):
    heads = kh_ref.shape[0]
    width = heads * HD
    devs, _, rows = kt_ref.shape
    per = rows // BLOCK
    a = pl.program_id(0)
    pos = pos_ref[0]

    @pl.when(a == 0)
    def _():
        for h in range(heads):
            kh_ref[h] = qkv_ref[:, width + h * HD : width + (h + 1) * HD]
            vh_ref[h] = qkv_ref[:, 2 * width + h * HD : 2 * width + (h + 1) * HD]
        for d in range(devs):
            kt_ref[d] = rounded(transposed(qkv_ref[d * rows : (d + 1) * rows, width : 2 * width]))
        dk_ref[...] = jnp.zeros_like(dk_ref)
        dv_ref[...] = jnp.zeros_like(dv_ref)
        bsum_ref[...] = jnp.zeros_like(bsum_ref)

    first = pl.multiple_of(((a // per) ^ pos) * rows + (a % per) * BLOCK, BLOCK)
    q = qkv_ref[pl.ds(first, BLOCK), :width] * jnp.asarray(HD**-0.5, BF)
    go = go_ref[pl.ds(first, BLOCK), :]
    qt = rounded(transposed(q))
    got = transposed(go)
    prod = got * transposed(o_ref[pl.ds(first, BLOCK), :])
    got = rounded(got)
    zero = jnp.zeros((BLOCK, width), BF)
    dots, lses = [], []
    for h in range(heads):
        mask = lane_mask((BLOCK, width), h)
        qm_ref[h * BLOCK : (h + 1) * BLOCK, :] = jnp.where(mask, q, zero)
        gm_ref[h * BLOCK : (h + 1) * BLOCK, :] = jnp.where(mask, go, zero)
        dots.append(jnp.sum(prod[h * HD : (h + 1) * HD], axis=0, keepdims=True))
        lses.append(lse_ref[a, h : h + 1, :])
    dq_ref[...] = jnp.zeros_like(dq_ref)

    def step(d, carry):
        where = pl.multiple_of((d ^ pos) * rows, rows)
        slot = d ^ pos
        for h in range(heads):
            lanes = slice(h * HD, (h + 1) * HD)
            cols = slice(h * BLOCK, (h + 1) * BLOCK)
            raw = dot(kh_ref[h, pl.ds(where, rows), :], qt[lanes])
            gp = dot(vh_ref[h, pl.ds(where, rows), :], got[lanes])
            for half in range(per):
                part = slice(half * BLOCK, (half + 1) * BLOCK)
                key_block = d * per + half
                c = block_bias(bias_ref, h, a, key_block)
                pf = jnp.exp(raw[part] + (c - lses[h]))
                p_ref[part, cols] = rounded(pf)
                ds = rounded(pf * (gp[part] - dots[h]))
                ds_ref[part, cols] = ds
                dst_ref[h, part, :] = ds
                bucket = jnp.clip(a - key_block, 0, NB - 1)
                bsum_ref[h, bucket] += jnp.sum(
                    ds.astype(F32).reshape(BLOCK // 8, 8, BLOCK), axis=0
                )
            dq_ref[lanes, :] += dot(kt_ref[slot, lanes, :], dst_ref[h])
        dv_ref[pl.ds(where, rows), :] += dot(p_ref[...], gm_ref[...])
        dk_ref[pl.ds(where, rows), :] += dot(ds_ref[...], qm_ref[...])
        return carry

    lax.fori_loop(0, a // per + 1, step, 0)
    dqkv_ref[pl.ds(first, BLOCK), :width] = rounded(dq_ref[...].T * HD**-0.5)

    @pl.when(a == pl.num_programs(0) - 1)
    def _():
        dqkv_ref[:, width : 2 * width] = rounded(dk_ref[...])
        dqkv_ref[:, 2 * width :] = rounded(dv_ref[...])


def self_bwd(pos, bias, qkv, mixed, grad, lse, rows):
    tokens, triple = qkv.shape
    width = triple // 3
    heads = width // HD
    blocks = tokens // BLOCK
    return pl.pallas_call(
        self_bwd_kernel,
        grid=(blocks,),
        in_specs=[smem_spec(), smem_spec()] + [vmem_spec()] * 4,
        out_specs=[vmem_spec(), vmem_spec()],
        out_shape=[
            jax.ShapeDtypeStruct((tokens, triple), BF),
            jax.ShapeDtypeStruct((heads, NB, 8, BLOCK), F32),
        ],
        scratch_shapes=[
            pltpu.VMEM((heads, tokens, HD), BF),
            pltpu.VMEM((heads, tokens, HD), BF),
            pltpu.VMEM((tokens // rows, width, rows), BF),
            pltpu.VMEM((heads * BLOCK, width), BF),
            pltpu.VMEM((heads * BLOCK, width), BF),
            pltpu.VMEM((rows, heads * BLOCK), BF),
            pltpu.VMEM((rows, heads * BLOCK), BF),
            pltpu.VMEM((heads, rows, BLOCK), BF),
            pltpu.VMEM((width, BLOCK), F32),
            pltpu.VMEM((tokens, width), F32),
            pltpu.VMEM((tokens, width), F32),
        ],
        compiler_params=pltpu.CompilerParams(vmem_limit_bytes=VMEM_LIMIT),
        cost_estimate=estimate(
            flops=5 * tokens * tokens * width * 2, bytes_accessed=16 * tokens * width,
            transcendentals=tokens * tokens * heads // 2,
        ),
    )(pos.reshape(1), bias, qkv, mixed, grad, lse)


def slotted(value, pad_ref):
    rows = value.shape[0]
    rolled = pltpu.roll(value.astype(F32), 1, 0)
    first = lax.broadcasted_iota(jnp.int32, rolled.shape, 0) == 0
    pad_ref[:rows] = rounded(jnp.where(first, 0.0, rolled))
    pad_ref[rows:] = rounded(jnp.where(first, rolled, 0.0)[:SEGMENT])


def unslotted(pad_ref, rows):
    value = pad_ref[:rows]
    first = lax.broadcasted_iota(jnp.int32, value.shape, 0) == 0
    value = jnp.where(first, jnp.broadcast_to(pad_ref[rows : rows + 1], value.shape), value)
    return pltpu.roll(value, rows - 1, 0)


def masked_stack(value, group):
    return jnp.concatenate(
        [jnp.where(lane_mask(value.shape, h), value, jnp.zeros_like(value)) for h in range(group)], 0
    )


def cross_soft(keys, stacked):
    s = dot(keys, stacked, 1, 1)
    top = jnp.max(s, axis=0, keepdims=True)
    e = jnp.exp(s - top)
    return e / jnp.sum(e, axis=0, keepdims=True)


def merged(tall, group):
    rows, width = tall.shape[0] // group, tall.shape[1]
    out = jnp.zeros((rows, width), F32)
    for h in range(group):
        out = jnp.where(lane_mask((rows, width), h), tall[h * rows : (h + 1) * rows], out)
    return out


def cross_fwd_kernel(q_ref, k_ref, v_ref, out_ref, qp_ref, op_ref):
    slot = pl.program_id(0)
    rows = q_ref.shape[0]
    lanes = 4 * HD

    @pl.when(slot == 0)
    def _():
        slotted(q_ref[...], qp_ref)

    here = pl.ds(pl.multiple_of(slot * SEGMENT, SEGMENT), SEGMENT)
    scaled = qp_ref[here, :] * jnp.asarray(HD**-0.5, BF)
    for g in range(q_ref.shape[1] // lanes):
        part = slice(g * lanes, (g + 1) * lanes)
        soft = rounded(cross_soft(k_ref[:, part], masked_stack(scaled[:, part], 4)))
        op_ref[here, part] = merged(dot(soft, v_ref[:, part], 0, 0), 4)

    @pl.when(slot == pl.num_programs(0) - 1)
    def _():
        out_ref[...] = rounded(unslotted(op_ref, rows))


def cross_fwd(queries, pairs, neigh_rows):
    rows, width = queries.shape
    slots = rows // SEGMENT + 1
    return pl.pallas_call(
        cross_fwd_kernel,
        grid=(slots,),
        in_specs=[
            vmem_spec(),
            pl.BlockSpec((neigh_rows, width), lambda i: (i, 0)),
            pl.BlockSpec((neigh_rows, width), lambda i: (i, 1)),
        ],
        out_specs=vmem_spec(),
        out_shape=jax.ShapeDtypeStruct((rows, width), BF),
        scratch_shapes=[
            pltpu.VMEM((slots * SEGMENT, width), BF),
            pltpu.VMEM((slots * SEGMENT, width), F32),
        ],
        compiler_params=pltpu.CompilerParams(vmem_limit_bytes=VMEM_LIMIT),
        cost_estimate=estimate(
            flops=16 * slots * SEGMENT * neigh_rows * width, bytes_accessed=2 * pairs.size,
            transcendentals=slots * neigh_rows * width,
        ),
    )(queries, pairs, pairs)


def cross_bwd_kernel(q_ref, g_ref, k_ref, v_ref, dq_ref, dkv_ref, qp_ref, gp_ref, op_ref):
    slot = pl.program_id(0)
    rows, width = q_ref.shape
    lanes = 4 * HD

    @pl.when(slot == 0)
    def _():
        slotted(q_ref[...], qp_ref)
        slotted(g_ref[...], gp_ref)

    here = pl.ds(pl.multiple_of(slot * SEGMENT, SEGMENT), SEGMENT)
    scaled = qp_ref[here, :] * jnp.asarray(HD**-0.5, BF)
    grads = gp_ref[here, :]
    for g in range(width // lanes):
        part = slice(g * lanes, (g + 1) * lanes)
        queries = masked_stack(scaled[:, part], 4)
        grad = masked_stack(grads[:, part], 4)
        soft = cross_soft(k_ref[:, part], queries)
        gp = dot(v_ref[:, part], grad, 1, 1)
        ds = rounded(soft * (gp - jnp.sum(soft * gp, axis=0, keepdims=True)))
        op_ref[here, part] = merged(dot(ds, k_ref[:, part], 0, 0), 4) * HD**-0.5
        dkv_ref[:, part] = rounded(dot(ds, queries))
        dkv_ref[:, width + g * lanes : width + (g + 1) * lanes] = rounded(dot(rounded(soft), grad))

    @pl.when(slot == pl.num_programs(0) - 1)
    def _():
        dq_ref[...] = rounded(unslotted(op_ref, rows))


def cross_bwd(queries, grads, pairs, neigh_rows):
    rows, width = queries.shape
    slots = rows // SEGMENT + 1
    return pl.pallas_call(
        cross_bwd_kernel,
        grid=(slots,),
        in_specs=[
            vmem_spec(),
            vmem_spec(),
            pl.BlockSpec((neigh_rows, width), lambda i: (i, 0)),
            pl.BlockSpec((neigh_rows, width), lambda i: (i, 1)),
        ],
        out_specs=[vmem_spec(), pl.BlockSpec((neigh_rows, 2 * width), lambda i: (i, 0))],
        out_shape=[
            jax.ShapeDtypeStruct((rows, width), BF),
            jax.ShapeDtypeStruct(pairs.shape, BF),
        ],
        scratch_shapes=[
            pltpu.VMEM((slots * SEGMENT, width), BF),
            pltpu.VMEM((slots * SEGMENT, width), BF),
            pltpu.VMEM((slots * SEGMENT, width), F32),
        ],
        compiler_params=pltpu.CompilerParams(vmem_limit_bytes=VMEM_LIMIT),
        cost_estimate=estimate(
            flops=40 * slots * SEGMENT * neigh_rows * width, bytes_accessed=4 * pairs.size,
            transcendentals=slots * neigh_rows * width,
        ),
    )(queries, grads, pairs, pairs)


def on_device(
    tokens, neighbours, norm_gains, position_bias, query_self, key_self, value_self, output_self,
    query_cross, key_cross, value_cross, output_cross, inner_weight, outer_weight, cotangent,
):
    dp, seq = lax.axis_size("dp"), lax.axis_size("seq")
    rows, model = tokens.shape[1], tokens.shape[2]
    heads = position_bias.shape[0]
    width = heads * HD
    segments = rows // SEGMENT
    neigh_rows = neighbours.shape[2] * neighbours.shape[3]
    span = min(seq, max(2, SEQ_MIN // rows))
    group_width = width // span
    group_heads = heads // span
    my_dp = lax.axis_index("dp")
    pos = lax.axis_index("seq") % span

    fast = seq == 4 and span == 4 and rows % (2 * BLOCK) == 0 and model == 896
    place = my_place() if fast else None

    def whole(shard):
        return assemble(lax.all_gather(shard, BOTH, axis=0, tiled=False), dp, seq)

    own_tokens = tokens.reshape(rows, model)
    states = neighbours.reshape(segments * neigh_rows, model)
    forward_pairs = [(i, i + 1) for i in range(seq - 1) if (i + 1) % span]
    back_pairs = [(i + 1, i) for i in range(seq - 1) if (i + 1) % span]
    inputs = own_tokens.astype(F32)
    upstream = cotangent.reshape(rows, model).astype(F32)
    bias = lax.dynamic_slice_in_dim(position_bias, pos * group_heads, group_heads, 0)
    triple = jnp.concatenate([query_self, key_self, value_self], axis=1)

    pieces_tok = {0: own_tokens}
    bit = span // 2
    while bit:
        for k in list(pieces_tok):
            pieces_tok[k | bit] = swap(pieces_tok[k], "seq", bit)
        bit //= 2
    lane_tokens = [pieces_tok[k] for k in range(span)]

    if fast:
        near = jnp.stack([triple] + [swap(triple, "dp", 2 * k) for k in range(1, dp // 2)])
        far = swap(near, "dp", 1)
        lane_tokens = list(lax.optimization_barrier(tuple(lane_tokens) + (far,)))
        far = lane_tokens.pop()

        def turned(shard):
            flat = shard.T
            half = flat.shape[0] // 2
            return jnp.concatenate([flat[:half], flat[half:]], axis=1)

        packed = jnp.concatenate(
            [key_cross, value_cross, query_cross, turned(output_self), turned(output_cross)], axis=0
        )
        part = outer_weight.shape[0] // 4
        line = [outer_weight[t * part : (t + 1) * part] for t in range(4)]
        feed = jnp.concatenate([inner_weight, jnp.concatenate(line, axis=1)], axis=0)
        group_near = jnp.stack(gather_near(packed))
        feed_line = gather_near(after(feed, group_near))
        edge_source = after(states[(segments - 1) * neigh_rows :], far)
        group_near = after(group_near, far)
        group_both = jnp.concatenate([group_near, over_a(group_near)], axis=0)
        first_normed, qkv, triple_full = project(near, far, norm_gains[:1], lane_tokens, place)
        group_both = after(group_both, qkv)
        group_far = over_b(group_both)
    else:
        edge_source = states[(segments - 1) * neigh_rows :]
        pieces = []
        for shard in (query_self, key_self, value_self):
            pieces.append(lax.dynamic_slice_in_dim(whole(shard), pos * group_width, group_width, 1))
        triple_full = jnp.concatenate(pieces, axis=1)
        recall_full = jnp.concatenate([whole(key_cross), whole(value_cross)], axis=1)
        query_full = whole(query_cross)
        output_turned, cross_turned = whole(output_self).T, whole(output_cross).T
        inner_full, outer_full = whole(inner_weight), whole(outer_weight)
        first_normed = jnp.concatenate(
            [rounded(rms_apply(v.astype(F32), norm_gains[0])) for v in lane_tokens], axis=0
        )
        qkv = rounded(linear(first_normed, triple_full))

    edge = lax.ppermute(edge_source, "seq", forward_pairs)
    mixed_group, lse = self_fwd(pos, bias, qkv, rows)
    if fast:
        feed_line = list(lax.optimization_barrier(tuple(feed_line) + (edge, mixed_group, group_far)))
        group_far, mixed_group, edge = feed_line.pop(), feed_line.pop(), feed_line.pop()

    states_all = lax.optimization_barrier(jnp.concatenate([edge, states], axis=0))

    def exchanged(blocks):
        return [blocks[0]] + [swap(blocks[k], "seq", k) for k in range(1, span)]

    mixed_blocks = [mixed_group[k * rows : (k + 1) * rows] for k in range(span)]
    mixed_self = join_columns(exchanged(mixed_blocks), pos)
    if fast:
        feed_near = after(jnp.stack(feed_line), mixed_self)
        feed_next = over_a(feed_near)
        recall_full, query_full, output_turned, cross_turned = assemble_attention(
            [group_both, group_far, over_core(group_both), over_core(group_far)], place
        )

    recall_pairs = rounded(linear(states_all, recall_full))

    after_self = inputs + input_grad(mixed_self, output_turned)
    second_normed = rounded(rms_apply(after_self, norm_gains[1]))
    if fast:
        feed_both = jnp.concatenate([feed_near, after(feed_next, second_normed)], axis=0)
        feed_far = over_b(feed_both)
    cross_queries = rounded(linear(second_normed, query_full))
    mixed_cross = cross_fwd(cross_queries, recall_pairs, neigh_rows)
    if fast:
        mixed_cross, feed_far = lax.optimization_barrier((mixed_cross, feed_far))
    after_cross = after_self + input_grad(mixed_cross, cross_turned)
    third_normed = rounded(rms_apply(after_cross, norm_gains[2]))
    if fast:
        inner_full, outer_full = assemble_feed(
            [feed_both, feed_far, over_core(feed_both), over_core(feed_far)], place
        )
    gate_value = linear(third_normed, inner_full)
    activated, gelu_pull = jax.vjp(gelu_tanh, gate_value)
    hidden_act = rounded(activated)
    outcome = after_cross + linear(hidden_act, outer_full)

    grad_feed = rounded(upstream)
    grad_hidden = input_grad(grad_feed, outer_full)
    grad_gate = rounded(gelu_pull(grad_hidden)[0])
    if fast:
        kept, sent = feed_grad(place, third_normed, grad_gate, hidden_act, grad_feed)
        got = over_core(sent)
    else:
        sum_outer = block_sum(hidden_act, grad_feed)
        sum_inner = block_sum(third_normed, grad_gate)
    norm_grad, gain_three = norm_back(after_cross, norm_gains[2], input_grad(grad_gate, inner_full))
    grad_late = upstream + norm_grad

    grad_cross = rounded(grad_late)
    grad_mixed = rounded(linear(grad_cross, cross_turned))
    if fast:
        got = after(got, grad_mixed)
        sent_b = rounded(wide_sum(kept[1], got[1]))
        grad_mixed = after(grad_mixed, sent_b)
        got_b = over_b(sent_b)
    probe, pair_round = cross_bwd(cross_queries, grad_mixed, recall_pairs, neigh_rows)

    def turned_back(own):
        half = own.shape[1] // 2
        return jnp.concatenate([own[:, :half].T, own[:, half:].T], axis=1)

    if fast:
        pieces = group_grad("tall", place, mixed_cross, grad_cross, 3, 5)
        pieces = group_grad("wide", place, second_normed, probe, 2, 5, pieces)
        pieces = group_grad("wide", place, states_all, pair_round, 0, 5, pieces, 2)
        probe, got_b = lax.optimization_barrier((probe, got_b, pieces[0]))[:2]
        sent_a = sum_second(kept, got, got_b)
        got_a = over_a(sent_a)
    else:
        sum_cross = block_sum(mixed_cross, grad_cross)
        sum_key = block_sum(states_all, pair_round[:, :width])
        sum_value = block_sum(states_all, pair_round[:, width:])
        sum_query = block_sum(second_normed, probe)
    norm_grad, gain_two = norm_back(after_self, norm_gains[1], input_grad(probe, query_full))
    grad_early = grad_late + norm_grad
    states_round = rounded(input_grad(pair_round, recall_full))

    grad_self = rounded(grad_early)
    if fast:
        last_kept, last_sent = group_grad("tall", place, mixed_self, grad_self, 4, 5, pieces)
        last_got = over_core(last_sent)
    else:
        sum_output = block_sum(mixed_self, grad_self)
    grad_attended = rounded(linear(grad_self, output_turned))
    if fast:
        grad_attended = after(grad_attended, sent_a)
    grad_parts = exchanged(split_columns(grad_attended, span, pos))
    if fast:
        grad_parts = list(lax.optimization_barrier(tuple(grad_parts) + (states_round, last_got)))
        last_got, states_round = grad_parts.pop(), grad_parts.pop()
        line = sum_third(kept, got, got_b, after(got_a, grad_parts[-1]))
        last_b = rounded(wide_sum(last_kept[1], last_got[1]))
        grad_parts[0] = after(grad_parts[0], line, last_b)
        last_far = over_b(last_b)
        feed_own = sum_over_z(line)
        part = feed_own.shape[0] // 2
        sum_inner = feed_own[:part]
        sum_outer = feed_own[part:].reshape(part, 4, model // 4)
        sum_outer = sum_outer.transpose(1, 0, 2).reshape(4 * part, -1)
    grad_group = jnp.concatenate(grad_parts, axis=0)
    returned = lax.ppermute(states_round[:neigh_rows], "seq", back_pairs)
    last = states_round[segments * neigh_rows :].astype(F32) + returned.astype(F32)
    grad_states = jnp.concatenate(
        [states_round[neigh_rows : segments * neigh_rows], rounded(last)], axis=0
    )
    triple_grad, bias_sums = self_bwd(pos, bias, qkv, mixed_group, grad_group, lse, rows)
    if fast:
        triple_grad, last_far = lax.optimization_barrier((triple_grad, last_far, feed_own))[:2]
        last_a = sum_second(last_kept, last_got, last_far)
        last_near = over_a(last_a)
        own_y, other_y = triple_pieces(place, first_normed, after(triple_grad, last_a))
        got_y = swap(other_y, "dp", 1)
        triple_grad = after(triple_grad, other_y)
    partial = input_grad(triple_grad, triple_full)
    gain_one = jnp.sum(partial * first_normed.astype(F32), axis=0) / norm_gains[0]
    partial = rounded(partial)
    if fast:
        partial, last_near = lax.optimization_barrier((partial, last_near))
        line = sum_third(last_kept, last_got, last_far, last_near)
        own = sum_over_z(line)
        part = own.shape[0] // 5
        sum_key, sum_value, sum_query = (own[i * part : (i + 1) * part] for i in range(3))
        sum_cross = turned_back(own[3 * part : 4 * part])
        sum_output = turned_back(own[4 * part :])
    partial = partial.reshape(span, rows, model)
    blocks = {k: partial[k] for k in range(span)}
    bit = 1
    while bit < span:
        for k in sorted(blocks):
            if not k & bit:
                leaves = blocks[k | bit]
                if fast and bit == 2:
                    leaves, got_y = lax.optimization_barrier((leaves, got_y))
                got = swap(leaves, "seq", bit)
                blocks[k] = blocks[k].astype(F32) + got.astype(F32)
                if bit * 2 < span and k:
                    blocks[k] = rounded(blocks[k])
        blocks = {k: v for k, v in blocks.items() if not k & bit}
        bit *= 2
    if fast:
        own = sum_over_z(rounded(wide_sum(own_y, got_y)))
        own_self = [own[:, i * group_width : (i + 1) * group_width] for i in range(3)]
    norm_grad, _ = norm_back(inputs, norm_gains[0], blocks[0])
    grad_inputs = grad_early + norm_grad

    if not fast:
        own_self = []
        for i in range(3):
            columns = triple_grad[:, i * group_width : (i + 1) * group_width]
            wide = jnp.zeros((span * rows, width), BF)
            wide = lax.dynamic_update_slice_in_dim(wide, columns, pos * group_width, 1)
            own_self.append(block_sum(first_normed, wide))

    bias_local = jnp.sum(bias_sums, axis=(2, 3))
    bias_all = lax.dynamic_update_slice_in_dim(
        jnp.zeros((heads, NB), F32), bias_local, pos * group_heads, 0
    )
    small = jnp.concatenate([gain_one, gain_two, gain_three, bias_all.reshape(-1)])
    if fast:
        size = small.shape[0]
        small = jnp.pad(small, (0, -size % 1024)).reshape(-1, 128)
        small = butterfly(small).reshape(-1)[:size]
    else:
        small = lax.psum(small, BOTH)
    gains = small[: 3 * model].reshape(3, model)
    bias_total = small[3 * model :].reshape(heads, NB)
    return (
        rounded(outcome).reshape(1, rows, model),
        rounded(grad_inputs).reshape(1, rows, model),
        grad_states.reshape(neighbours.shape),
        gains,
        bias_total,
        own_self[0],
        own_self[1],
        own_self[2],
        sum_output,
        sum_query,
        sum_key,
        sum_value,
        sum_cross,
        sum_inner,
        sum_outer,
    )


def solution(mesh):
    weight = P("dp", "seq")
    lane = P("dp", "seq", None)
    wide = P("dp", "seq", None, None, None)
    return jax.shard_map(
        on_device,
        mesh=mesh,
        in_specs=(lane, wide, P(), P()) + (weight,) * 10 + (lane,),
        out_specs=(lane, lane, wide, P(), P()) + (weight,) * 10,
        check_vma=False,
    )
```

```python
import functools

import jax
import jax.numpy as jnp
from jax import lax
from jax.experimental import pallas as pl
from jax.experimental.pallas import tpu as pltpu
from jax.sharding import PartitionSpec as P

HD = 64
SEGMENT = 64
BLOCK = 256
NB = 6
SEQ_MIN = 2048
EPSILON = 1e-06
NEGATIVE = -1e30
BF = jnp.bfloat16
F32 = jnp.float32
VMEM_LIMIT = 56 * 2**20
BOTH = ("dp", "seq")


def dot(a, b, ca=1, cb=0):
    return lax.dot_general(a, b, (((ca,), (cb,)), ((), ())), preferred_element_type=F32)


def linear(a, b):
    return dot(a, b)


def input_grad(a, b):
    return dot(a, b, 1, 1)


def weight_grad(a, b):
    return dot(a, b, 0, 0)


def rounded(v):
    return v.astype(BF)


def rms_apply(inputs, gain_row):
    factor = lax.rsqrt(jnp.mean(inputs * inputs, axis=-1, keepdims=True) + EPSILON)
    return inputs * factor * gain_row


def norm_back(inputs, gain_row, upstream):
    normed_value, pullback = jax.vjp(rms_apply, inputs, gain_row)
    return pullback(upstream)


def gelu_tanh(operand):
    return jax.nn.gelu(operand, approximate=True)


def swap(value, axis, by):
    peers = lax.axis_size(axis)
    return lax.ppermute(value, axis, [(i, i ^ by) for i in range(peers)])


def after(value, *others):
    return lax.optimization_barrier((value,) + others)[0]


def estimate(flops, bytes_accessed, transcendentals):
    return pl.CostEstimate(
        flops=flops // 50, bytes_accessed=bytes_accessed // 50, transcendentals=transcendentals // 50
    )


def vmem_spec():
    return pl.BlockSpec(memory_space=pltpu.VMEM)


def smem_spec():
    return pl.BlockSpec(memory_space=pltpu.SMEM)


def reorder_triple_kernel(place_ref, near_ref, far_ref, out_ref):
    count, rows, _ = near_ref.shape
    z, y = place_ref[0], place_ref[1]
    for ref, flip in ((near_ref, 0), (far_ref, 1)):
        for k in range(count):
            where = ((z ^ k) * 2 + (y ^ flip)) * rows
            out_ref[pl.ds(pl.multiple_of(where, rows), rows), :] = ref[k]


def project_kernel(place_ref, near_ref, far_ref, gain_ref, *refs):
    tokens, (normed_ref, qkv_ref, full_ref) = refs[:-3], refs[-3:]
    reorder_triple_kernel(place_ref, near_ref, far_ref, full_ref)
    rows = tokens[0].shape[0]
    part = rows // 2
    for k, ref in enumerate(tokens):

        def step(i, carry):
            here = pl.ds(pl.multiple_of(i * part, part), part)
            there = pl.ds(pl.multiple_of(k * rows + i * part, part), part)
            normed = rounded(rms_apply(ref[here, :].astype(F32), gain_ref[...]))
            normed_ref[there, :] = normed
            qkv_ref[there, :] = rounded(dot(normed, full_ref[...]))
            return carry

        lax.fori_loop(0, 2, step, 0)


def project(near, far, gain, tokens, place):
    count, height, cols = near.shape
    rows, model = tokens[0].shape
    total = rows * len(tokens)
    return pl.pallas_call(
        project_kernel,
        in_specs=[smem_spec()] + [vmem_spec()] * (3 + len(tokens)),
        out_specs=[vmem_spec()] * 3,
        out_shape=[
            jax.ShapeDtypeStruct((total, model), BF),
            jax.ShapeDtypeStruct((total, cols), BF),
            jax.ShapeDtypeStruct((2 * count * height, cols), BF),
        ],
        compiler_params=pltpu.CompilerParams(vmem_limit_bytes=VMEM_LIMIT),
        cost_estimate=estimate(
            flops=2 * total * model * cols, bytes_accessed=8 * total * model, transcendentals=0
        ),
    )(place, near, far, gain, *tokens)


def join_kernel(mine_ref, *refs):
    out_ref = refs[-1]
    cols = refs[0].shape[1]
    for k, ref in enumerate(refs[:-1]):
        out_ref[:, pl.ds(pl.multiple_of((mine_ref[0] ^ k) * cols, cols), cols)] = ref[...]


def join_columns(pieces, mine):
    rows, cols = pieces[0].shape
    return pl.pallas_call(
        join_kernel,
        in_specs=[smem_spec()] + [vmem_spec()] * len(pieces),
        out_specs=vmem_spec(),
        out_shape=jax.ShapeDtypeStruct((rows, cols * len(pieces)), pieces[0].dtype),
    )(mine.reshape(1), *pieces)


def split_kernel(mine_ref, in_ref, *outs):
    cols = outs[0].shape[1]
    for k, ref in enumerate(outs):
        ref[...] = in_ref[:, pl.ds(pl.multiple_of((mine_ref[0] ^ k) * cols, cols), cols)]


def split_columns(flat, count, mine):
    rows, width = flat.shape
    return pl.pallas_call(
        split_kernel,
        in_specs=[smem_spec(), vmem_spec()],
        out_specs=[vmem_spec()] * count,
        out_shape=[jax.ShapeDtypeStruct((rows, width // count), flat.dtype)] * count,
    )(mine.reshape(1), flat)


def assemble(blocks, dp, seq):
    _, rows, cols = blocks.shape
    return blocks.reshape(dp, seq, rows, cols).transpose(0, 2, 1, 3).reshape(dp * rows, seq * cols)


def block_sum(left, right):
    dp, seq = lax.axis_size("dp"), lax.axis_size("seq")
    rows, cols = left.shape[1] // dp, right.shape[1] // seq
    blocks = rounded(weight_grad(left, right)).reshape(dp, rows, seq, cols).transpose(0, 2, 1, 3)
    blocks = blocks.reshape(dp * seq, rows, cols)
    return lax.psum_scatter(blocks, BOTH, scatter_dimension=0, tiled=True)[0].astype(F32)


def device_pairs(target):
    dp, pairs = lax.axis_size("dp"), []
    for i in range(dp):
        for j in range(4):
            z, y, x, c = target(i // 2, i % 2, j // 2, j % 2)
            pairs.append((i * 4 + j, (z * 2 + y) * 4 + x * 2 + c))
    return pairs


def over_z(value, k):
    return lax.ppermute(value, BOTH, device_pairs(lambda z, y, x, c: (z ^ k, y, x, c)))


def over_a(value):
    return lax.ppermute(
        value, BOTH, device_pairs(lambda z, y, x, c: (z, y ^ c, x ^ (1 - c), c))
    )


def over_b(value):
    return lax.ppermute(
        value, BOTH, device_pairs(lambda z, y, x, c: (z, y ^ (1 - c), x ^ c, c))
    )


def over_core(value):
    return lax.ppermute(value, BOTH, device_pairs(lambda z, y, x, c: (z, y, x, 1 - c)))


def my_place():
    i, j = lax.axis_index("dp"), lax.axis_index("seq")
    return jnp.stack([i // 2, i % 2, j // 2, j % 2]).astype(jnp.int32)


def gather_near(shard):
    depth = lax.axis_size("dp") // 2
    return [shard] + [over_z(shard, k) for k in range(1, depth)]


def piece_origin(place_ref, c, b, t, depth):
    z, y, x, core = (place_ref[i] for i in range(4))
    a, k = t // depth, t % depth
    core = core ^ c
    dx = jnp.where(core == 0, a, b)
    dy = jnp.where(core == 0, b, a)
    return (z ^ k) * 2 + (y ^ dy), (x ^ dx) * 2 + core


def assemble_attention_kernel(depth, place_ref, *refs):
    pieces, (recall, query, out_self, out_cross), sems = refs[:4], refs[4:8], refs[8]
    rows = query.shape[0] // (2 * depth)
    cols = query.shape[1] // 4
    half = cols // 2

    def step(t, carry):
        for i in range(4):
            i_dp, i_seq = piece_origin(place_ref, i // 2, i % 2, t, depth)
            down = pl.ds(pl.multiple_of(i_dp * rows, rows), rows)
            across = pl.multiple_of(i_seq * cols, cols)
            piece = pieces[i].at[t]

            def move(first, target, sem):
                pltpu.make_async_copy(piece.at[pl.ds(first, rows), :], target, sems.at[sem]).start()

            move(0, recall.at[down, pl.ds(across, cols)], 0)
            move(rows, recall.at[down, pl.ds(across + 4 * cols, cols)], 0)
            move(2 * rows, query.at[down, pl.ds(across, cols)], 1)
            lanes = pl.ds(pl.multiple_of(i_dp * half, half), half)
            for w, out in ((0, out_self), (1, out_cross)):
                for h in range(2):
                    top = pl.multiple_of((i_seq * 2 + h) * rows, rows)
                    pltpu.make_async_copy(
                        piece.at[pl.ds((3 + w) * rows, rows), pl.ds(h * half, half)],
                        out.at[pl.ds(top, rows), lanes],
                        sems.at[2 + w],
                    ).start()
        return carry

    lax.fori_loop(0, 2 * depth, step, 0)
    for sem, out in enumerate((recall, query, out_self, out_cross)):
        pltpu.make_async_copy(out, out, sems.at[sem]).wait()


def assemble_attention(pieces, place):
    count, packed, cols = pieces[0].shape
    rows = packed // 5
    model, width = rows * count, cols * 4
    shapes = [(model, 2 * width), (model, width), (8 * rows, width), (8 * rows, width)]
    return pl.pallas_call(
        functools.partial(assemble_attention_kernel, count // 2),
        in_specs=[smem_spec()] + [pl.BlockSpec(memory_space=pl.ANY)] * 4,
        out_specs=[vmem_spec()] * 4,
        out_shape=[jax.ShapeDtypeStruct(s, BF) for s in shapes],
        scratch_shapes=[pltpu.SemaphoreType.DMA((4,))],
        compiler_params=pltpu.CompilerParams(vmem_limit_bytes=VMEM_LIMIT),
    )(place, *pieces)


def assemble_feed_kernel(depth, place_ref, *refs):
    pieces, (inner, outer, stage, sems) = refs[:4], refs[4:]
    rows, cols = stage.shape[2:]
    part = cols // 4

    def step(t, carry):
        for i in range(4):
            i_dp, i_seq = piece_origin(place_ref, i // 2, i % 2, t, depth)
            piece = pieces[i].at[t]
            down = pl.ds(pl.multiple_of(i_dp * rows, rows), rows)
            across = pl.ds(pl.multiple_of(i_seq * cols, cols), cols)
            pltpu.make_async_copy(
                piece.at[pl.ds(rows, rows), :], stage.at[i_dp, i_seq], sems.at[1]
            ).start()
            pltpu.make_async_copy(
                piece.at[pl.ds(0, rows), :], inner.at[down, across], sems.at[0]
            ).start()
        return carry

    lax.fori_loop(0, 2 * depth, step, 0)
    pltpu.make_async_copy(stage, stage, sems.at[1]).wait()

    def spread(i, carry):
        for t in range(4):
            line = [stage[i, j, :, t * part : (t + 1) * part] for j in range(4)]
            where = pl.multiple_of((i * 4 + t) * rows, rows)
            outer[pl.ds(where, rows), :] = jnp.concatenate(line, axis=1)
        return carry

    lax.fori_loop(0, 2 * depth, spread, 0)
    pltpu.make_async_copy(inner, inner, sems.at[0]).wait()


def assemble_feed(pieces, place):
    deep, packed, cols = pieces[0].shape
    rows = packed // 2
    return pl.pallas_call(
        functools.partial(assemble_feed_kernel, deep // 2),
        in_specs=[smem_spec()] + [pl.BlockSpec(memory_space=pl.ANY)] * 4,
        out_specs=[vmem_spec()] * 2,
        out_shape=[
            jax.ShapeDtypeStruct((rows * deep, cols * 4), BF),
            jax.ShapeDtypeStruct((4 * rows * deep, cols), BF),
        ],
        scratch_shapes=[
            pltpu.VMEM((deep, 4, rows, cols), BF),
            pltpu.SemaphoreType.DMA((2,)),
        ],
        compiler_params=pltpu.CompilerParams(vmem_limit_bytes=VMEM_LIMIT),
    )(place, *pieces)


def put_block(place_ref, out_ref, core, i_dp, flip, value):
    z, y = place_ref[0], place_ref[1]
    dy = (i_dp % 2) ^ y
    b = jnp.where(core == 0, dy, flip)
    a = jnp.where(core == 0, flip, dy)
    out_ref[b, a, (i_dp // 2) ^ z] = value


def wide_grad_kernel(*refs):
    place_ref, left, kept_right, sent_right = refs[:4]
    kept, sent = refs[-2:]
    flip = pl.program_id(1)
    rows = kept.shape[3]
    core = place_ref[3]
    for right, out, c in ((kept_right, kept, core), (sent_right, sent, 1 - core)):
        value = rounded(dot(left[...], right[...], 0, 0))
        for i_dp in range(value.shape[0] // rows):
            put_block(place_ref, out, c, i_dp, flip, value[i_dp * rows : (i_dp + 1) * rows])


def tall_grad_kernel(*refs):
    place_ref, left, right = refs[:3]
    kept, sent = refs[-2:]
    rows, cols = kept.shape[3], kept.shape[4]
    half = cols // 2
    x, core = place_ref[2], place_ref[3]
    for j in range(4):
        value = rounded(dot(right[:, 2 * j * rows : 2 * (j + 1) * rows], left[...], 0, 0))
        for out, mine in ((kept, core == j % 2), (sent, core != j % 2)):

            @pl.when(mine)
            def _():
                for i_dp in range(value.shape[1] // half):
                    lanes = slice(i_dp * half, (i_dp + 1) * half)
                    block = jnp.concatenate([value[:rows, lanes], value[rows:, lanes]], axis=1)
                    put_block(place_ref, out, j % 2, i_dp, (j // 2) ^ x, block)


def feed_outer_kernel(place_ref, left, right, kept, sent):
    rows, cols = kept.shape[3:]
    part = cols // 4
    y, x, core = place_ref[1], place_ref[2], place_ref[3]
    value = rounded(dot(left[...], right[...], 0, 0))
    for j in range(4):
        for out, mine in ((kept, core == j % 2), (sent, core != j % 2)):

            @pl.when(mine)
            def _():
                for i_y in range(2):
                    base = i_y * 4 * rows
                    lanes = slice(j * part, (j + 1) * part)
                    line = [value[base + t * rows : base + (t + 1) * rows, lanes] for t in range(4)]
                    dy, flip = i_y ^ y, (j // 2) ^ x
                    b, a = (dy, flip) if j % 2 == 0 else (flip, dy)
                    out[b, a, 0] = jnp.concatenate(line, axis=1)


def feed_grad(place, normed, grad_gate, hidden, grad_feed):
    dp = lax.axis_size("dp")
    depth = dp // 2
    tokens, model = normed.shape
    inner = grad_gate.shape[1]
    rows, cols = model // dp, inner // 4
    shape = jax.ShapeDtypeStruct((2, 2, depth, 2 * rows, cols), BF)
    out_spec = pl.BlockSpec((2, 2, 1, rows, cols), lambda i, m: (0, 0, m[0] ^ i, 1, 0))
    pieces = pl.pallas_call(
        feed_outer_kernel,
        grid_spec=pltpu.PrefetchScalarGridSpec(
            num_scalar_prefetch=1,
            grid=(depth,),
            in_specs=[
                pl.BlockSpec((tokens, inner // depth), lambda i, m: (0, i)),
                pl.BlockSpec((tokens, model), lambda i, m: (0, 0)),
            ],
            out_specs=[out_spec] * 2,
        ),
        out_shape=[shape, shape],
        compiler_params=pltpu.CompilerParams(vmem_limit_bytes=VMEM_LIMIT),
        cost_estimate=estimate(
            flops=2 * tokens * model * inner,
            bytes_accessed=2 * (tokens * (model + inner) + model * inner),
            transcendentals=0,
        ),
    )(place, hidden, grad_feed)
    return group_grad("wide", place, normed, grad_gate, 0, 2, pieces)


def group_grad(kind, place, left, right, first, total, before=None, parts=1):
    dp = lax.axis_size("dp")
    depth = dp // 2
    tokens, height = left.shape
    width = right.shape[1]
    if kind == "tall":
        rows, cols = width // 8, 2 * height // dp
    else:
        rows, cols = height // dp, width // 4 // parts
    whole = jax.ShapeDtypeStruct((2, 2, depth, total * rows, cols), BF)
    block = (2, 2, depth, rows, cols)
    if kind == "wide":
        kernel, grid, operands = wide_grad_kernel, (parts, 2), [left, right, right]
        specs = [
            pl.BlockSpec((tokens, height), lambda p, i, m: (0, 0)),
            pl.BlockSpec((tokens, cols), lambda p, i, m: (0, p * 4 + (m[2] ^ i) * 2 + m[3])),
            pl.BlockSpec((tokens, cols), lambda p, i, m: (0, p * 4 + (m[2] ^ i) * 2 + 1 - m[3])),
        ]
        out_spec = pl.BlockSpec(block, lambda p, i, m: (0, 0, 0, first + p, 0))
    else:
        kernel, grid, operands = tall_grad_kernel, (1,), [left, right]
        specs = [
            pl.BlockSpec((tokens, height), lambda i, m: (0, 0)),
            pl.BlockSpec((tokens, width), lambda i, m: (0, 0)),
        ]
        out_spec = pl.BlockSpec(block, lambda i, m: (0, 0, 0, first, 0))
    aliases = {}
    if before is not None:
        aliases = {1 + len(operands): 0, 2 + len(operands): 1}
        operands = operands + list(before)
        specs = specs + [pl.BlockSpec(memory_space=pl.ANY)] * 2
    return pl.pallas_call(
        kernel,
        grid_spec=pltpu.PrefetchScalarGridSpec(
            num_scalar_prefetch=1, grid=grid, in_specs=specs, out_specs=[out_spec] * 2
        ),
        out_shape=[whole, whole],
        input_output_aliases=aliases,
        compiler_params=pltpu.CompilerParams(vmem_limit_bytes=VMEM_LIMIT),
        cost_estimate=estimate(
            flops=2 * tokens * height * width,
            bytes_accessed=2 * (left.size + right.size + height * width),
            transcendentals=0,
        ),
    )(place, *operands)


def wide_sum(*values):
    total = values[0].astype(F32)
    for value in values[1:]:
        total = total + value.astype(F32)
    return total


def sum_second(kept, got, got_b):
    return rounded(wide_sum(kept[0, 1], got[0, 1], got_b[1]))


def sum_third(kept, got, got_b, got_a):
    return rounded(wide_sum(kept[0, 0], got[0, 0], got_b[0], got_a))


def all_over_z(line):
    return [over_z(line[k], k) for k in range(1, line.shape[0])]


def joint(values, *others):
    out = lax.optimization_barrier(tuple(values) + others)
    return list(out[: len(values)]), *out[len(values) :]


def small_sum_kernel(dp, seq, in_ref, out_ref, slots, send_sems, recv_sems):
    count = dp * seq
    me = lax.axis_index("dp") * seq + lax.axis_index("seq")
    barrier = pltpu.get_barrier_semaphore()

    def peer(d):
        other = lax.rem(me + d, count)
        return lax.div(other, seq), lax.rem(other, seq)

    def greet(d, carry):
        pl.semaphore_signal(
            barrier, inc=1, device_id=peer(d), device_id_type=pl.DeviceIdType.MESH
        )
        return carry

    lax.fori_loop(1, count, greet, 0)
    pl.semaphore_wait(barrier, count - 1)

    def copy(d):
        return pltpu.make_async_remote_copy(
            src_ref=in_ref,
            dst_ref=slots.at[d - 1],
            send_sem=send_sems.at[d - 1],
            recv_sem=recv_sems.at[d - 1],
            device_id=peer(d),
            device_id_type=pl.DeviceIdType.MESH,
        )

    def start(d, carry):
        copy(d).start()
        return carry

    def wait(d, carry):
        copy(d).wait()
        return carry

    lax.fori_loop(1, count, start, 0)
    lax.fori_loop(1, count, wait, 0)
    total = in_ref[...]
    for d in range(count - 1):
        total = total + slots[d]
    out_ref[...] = total


def small_sum(value):
    dp, seq = lax.axis_size("dp"), lax.axis_size("seq")
    others = dp * seq - 1
    return pl.pallas_call(
        functools.partial(small_sum_kernel, dp, seq),
        in_specs=[vmem_spec()],
        out_specs=vmem_spec(),
        out_shape=jax.ShapeDtypeStruct(value.shape, value.dtype),
        scratch_shapes=[
            pltpu.VMEM((others,) + value.shape, value.dtype),
            pltpu.SemaphoreType.DMA((others,)),
            pltpu.SemaphoreType.DMA((others,)),
        ],
        compiler_params=pltpu.CompilerParams(collective_id=0, has_side_effects=True),
    )(value)


def triple_grad_kernel(place_ref, left, right, kept, sent):
    value = rounded(dot(left[...], right[...], 0, 0))
    rows = kept.shape[1]
    z, y = place_ref[0], place_ref[1]
    for out, flip in ((kept, 0), (sent, 1)):
        for i_y in range(2):

            @pl.when((y ^ i_y) == flip)
            def _():
                for i_z in range(kept.shape[0]):
                    top = (i_z * 2 + i_y) * rows
                    out[i_z ^ z] = value[top : top + rows]


def triple_pieces(place, left, right):
    dp = lax.axis_size("dp")
    rows, cols = left.shape[1] // dp, right.shape[1]
    shape = jax.ShapeDtypeStruct((dp // 2, rows, cols), BF)
    return pl.pallas_call(
        triple_grad_kernel,
        in_specs=[smem_spec(), vmem_spec(), vmem_spec()],
        out_specs=[vmem_spec()] * 2,
        out_shape=[shape, shape],
        compiler_params=pltpu.CompilerParams(vmem_limit_bytes=VMEM_LIMIT),
        cost_estimate=estimate(
            flops=2 * left.size * cols, bytes_accessed=2 * (left.size + right.size), transcendentals=0
        ),
    )(place, left, right)


def lane_mask(shape, head):
    lanes = lax.broadcasted_iota(jnp.int32, shape, len(shape) - 1)
    return (lanes >= head * HD) & (lanes < (head + 1) * HD)


def transposed(value):
    return value.astype(F32).T


def block_bias(bias_ref, head, query_block, key_block):
    distance = query_block - key_block
    kept = bias_ref[head, jnp.clip(distance, 0, NB - 1)]
    return jnp.where(distance >= 0, kept, NEGATIVE)


def self_fwd_kernel(pos_ref, bias_ref, qkv_ref, o_ref, lse_ref, kh_ref, vt_ref, s_ref, acc_ref):
    heads = kh_ref.shape[0]
    width = heads * HD
    devs, _, rows = vt_ref.shape
    per = rows // BLOCK
    a = pl.program_id(0)
    pos = pos_ref[0]

    @pl.when(a == 0)
    def _():
        for h in range(heads):
            kh_ref[h] = qkv_ref[:, width + h * HD : width + (h + 1) * HD]
        for d in range(devs):
            vt_ref[d] = rounded(transposed(qkv_ref[d * rows : (d + 1) * rows, 2 * width :]))

    first = pl.multiple_of(((a // per) ^ pos) * rows + (a % per) * BLOCK, BLOCK)
    qt = rounded(transposed(qkv_ref[pl.ds(first, BLOCK), :width]) * HD**-0.5)

    def scores(d, tops):
        where = pl.multiple_of((d ^ pos) * rows, rows)
        out = []
        for h in range(heads):
            raw = dot(kh_ref[h, pl.ds(where, rows), :], qt[h * HD : (h + 1) * HD])
            top = tops[h]
            for half in range(per):
                c = block_bias(bias_ref, h, a, d * per + half)
                piece = raw[half * BLOCK : (half + 1) * BLOCK] + c
                s_ref[h, pl.ds(pl.multiple_of(d * rows + half * BLOCK, BLOCK), BLOCK), :] = piece
                top = jnp.maximum(top, jnp.max(piece.reshape(BLOCK // 8, 8, BLOCK), axis=0))
            out.append(top)
        return tuple(out)

    count = a // per + 1
    tops = lax.fori_loop(
        0, count, scores, tuple(jnp.full((8, BLOCK), NEGATIVE, F32) for _ in range(heads))
    )
    tops = [jnp.max(t, axis=0, keepdims=True) for t in tops]
    acc_ref[...] = jnp.zeros_like(acc_ref)

    def mix(d, sums):
        out = []
        slot = d ^ pos
        for h in range(heads):
            e = jnp.exp(s_ref[h, pl.ds(pl.multiple_of(d * rows, rows), rows), :] - tops[h])
            out.append(sums[h] + jnp.sum(e.reshape(rows // 8, 8, BLOCK), axis=0))
            acc_ref[h * HD : (h + 1) * HD, :] += dot(
                vt_ref[slot, h * HD : (h + 1) * HD, :], rounded(e)
            )
        return tuple(out)

    sums = lax.fori_loop(
        0, count, mix, tuple(jnp.zeros((8, BLOCK), F32) for _ in range(heads))
    )
    for h in range(heads):
        total = jnp.sum(sums[h], axis=0, keepdims=True)
        lse_ref[a, h : h + 1, :] = tops[h] + jnp.log(total)
        acc_ref[h * HD : (h + 1) * HD, :] = acc_ref[h * HD : (h + 1) * HD, :] / total
    o_ref[pl.ds(first, BLOCK), :] = rounded(acc_ref[...].T)


def self_fwd(pos, bias, qkv, rows):
    tokens, triple = qkv.shape
    width = triple // 3
    heads = width // HD
    blocks = tokens // BLOCK
    return pl.pallas_call(
        self_fwd_kernel,
        grid=(blocks,),
        in_specs=[smem_spec(), smem_spec(), vmem_spec()],
        out_specs=[vmem_spec(), vmem_spec()],
        out_shape=[
            jax.ShapeDtypeStruct((tokens, width), BF),
            jax.ShapeDtypeStruct((blocks, 8, BLOCK), F32),
        ],
        scratch_shapes=[
            pltpu.VMEM((heads, tokens, HD), BF),
            pltpu.VMEM((tokens // rows, width, rows), BF),
            pltpu.VMEM((heads, tokens, BLOCK), F32),
            pltpu.VMEM((width, BLOCK), F32),
        ],
        compiler_params=pltpu.CompilerParams(vmem_limit_bytes=VMEM_LIMIT),
        cost_estimate=estimate(
            flops=2 * tokens * tokens * width * 2, bytes_accessed=8 * tokens * width,
            transcendentals=tokens * tokens * heads // 2,
        ),
    )(pos.reshape(1), bias, qkv)


def self_bwd_kernel(
    pos_ref, bias_ref, qkv_ref, o_ref, go_ref, lse_ref, dqkv_ref, bsum_ref,
    kh_ref, vh_ref, kt_ref, qm_ref, gm_ref, p_ref, ds_ref, dst_ref, dq_ref, dk_ref, dv_ref,
):
    heads = kh_ref.shape[0]
    width = heads * HD
    devs, _, rows = kt_ref.shape
    per = rows // BLOCK
    a = pl.program_id(0)
    pos = pos_ref[0]

    @pl.when(a == 0)
    def _():
        for h in range(heads):
            kh_ref[h] = qkv_ref[:, width + h * HD : width + (h + 1) * HD]
            vh_ref[h] = qkv_ref[:, 2 * width + h * HD : 2 * width + (h + 1) * HD]
        for d in range(devs):
            kt_ref[d] = rounded(transposed(qkv_ref[d * rows : (d + 1) * rows, width : 2 * width]))
        dk_ref[...] = jnp.zeros_like(dk_ref)
        dv_ref[...] = jnp.zeros_like(dv_ref)
        bsum_ref[...] = jnp.zeros_like(bsum_ref)

    first = pl.multiple_of(((a // per) ^ pos) * rows + (a % per) * BLOCK, BLOCK)
    q = qkv_ref[pl.ds(first, BLOCK), :width] * jnp.asarray(HD**-0.5, BF)
    go = go_ref[pl.ds(first, BLOCK), :]
    qt = rounded(transposed(q))
    got = transposed(go)
    prod = got * transposed(o_ref[pl.ds(first, BLOCK), :])
    got = rounded(got)
    zero = jnp.zeros((BLOCK, width), BF)
    dots, lses = [], []
    for h in range(heads):
        mask = lane_mask((BLOCK, width), h)
        qm_ref[h * BLOCK : (h + 1) * BLOCK, :] = jnp.where(mask, q, zero)
        gm_ref[h * BLOCK : (h + 1) * BLOCK, :] = jnp.where(mask, go, zero)
        dots.append(jnp.sum(prod[h * HD : (h + 1) * HD], axis=0, keepdims=True))
        lses.append(lse_ref[a, h : h + 1, :])
    dq_ref[...] = jnp.zeros_like(dq_ref)

    def step(d, carry):
        where = pl.multiple_of((d ^ pos) * rows, rows)
        slot = d ^ pos
        for h in range(heads):
            lanes = slice(h * HD, (h + 1) * HD)
            cols = slice(h * BLOCK, (h + 1) * BLOCK)
            raw = dot(kh_ref[h, pl.ds(where, rows), :], qt[lanes])
            gp = dot(vh_ref[h, pl.ds(where, rows), :], got[lanes])
            for half in range(per):
                part = slice(half * BLOCK, (half + 1) * BLOCK)
                key_block = d * per + half
                c = block_bias(bias_ref, h, a, key_block)
                pf = jnp.exp(raw[part] + (c - lses[h]))
                p_ref[part, cols] = rounded(pf)
                ds = rounded(pf * (gp[part] - dots[h]))
                ds_ref[part, cols] = ds
                dst_ref[h, part, :] = ds
                bucket = jnp.clip(a - key_block, 0, NB - 1)
                bsum_ref[h, bucket] += jnp.sum(
                    ds.astype(F32).reshape(BLOCK // 8, 8, BLOCK), axis=0
                )
            dq_ref[lanes, :] += dot(kt_ref[slot, lanes, :], dst_ref[h])
        dv_ref[pl.ds(where, rows), :] += dot(p_ref[...], gm_ref[...])
        dk_ref[pl.ds(where, rows), :] += dot(ds_ref[...], qm_ref[...])
        return carry

    lax.fori_loop(0, a // per + 1, step, 0)
    dqkv_ref[pl.ds(first, BLOCK), :width] = rounded(dq_ref[...].T * HD**-0.5)

    @pl.when(a == pl.num_programs(0) - 1)
    def _():
        dqkv_ref[:, width : 2 * width] = rounded(dk_ref[...])
        dqkv_ref[:, 2 * width :] = rounded(dv_ref[...])


def self_bwd(pos, bias, qkv, mixed, grad, lse, rows):
    tokens, triple = qkv.shape
    width = triple // 3
    heads = width // HD
    blocks = tokens // BLOCK
    return pl.pallas_call(
        self_bwd_kernel,
        grid=(blocks,),
        in_specs=[smem_spec(), smem_spec()] + [vmem_spec()] * 4,
        out_specs=[vmem_spec(), vmem_spec()],
        out_shape=[
            jax.ShapeDtypeStruct((tokens, triple), BF),
            jax.ShapeDtypeStruct((heads, NB, 8, BLOCK), F32),
        ],
        scratch_shapes=[
            pltpu.VMEM((heads, tokens, HD), BF),
            pltpu.VMEM((heads, tokens, HD), BF),
            pltpu.VMEM((tokens // rows, width, rows), BF),
            pltpu.VMEM((heads * BLOCK, width), BF),
            pltpu.VMEM((heads * BLOCK, width), BF),
            pltpu.VMEM((rows, heads * BLOCK), BF),
            pltpu.VMEM((rows, heads * BLOCK), BF),
            pltpu.VMEM((heads, rows, BLOCK), BF),
            pltpu.VMEM((width, BLOCK), F32),
            pltpu.VMEM((tokens, width), F32),
            pltpu.VMEM((tokens, width), F32),
        ],
        compiler_params=pltpu.CompilerParams(vmem_limit_bytes=VMEM_LIMIT),
        cost_estimate=estimate(
            flops=5 * tokens * tokens * width * 2, bytes_accessed=16 * tokens * width,
            transcendentals=tokens * tokens * heads // 2,
        ),
    )(pos.reshape(1), bias, qkv, mixed, grad, lse)


def slotted(value, pad_ref):
    rows = value.shape[0]
    rolled = pltpu.roll(value.astype(F32), 1, 0)
    first = lax.broadcasted_iota(jnp.int32, rolled.shape, 0) == 0
    pad_ref[:rows] = rounded(jnp.where(first, 0.0, rolled))
    pad_ref[rows:] = rounded(jnp.where(first, rolled, 0.0)[:SEGMENT])


def unslotted(pad_ref, rows):
    value = pad_ref[:rows]
    first = lax.broadcasted_iota(jnp.int32, value.shape, 0) == 0
    value = jnp.where(first, jnp.broadcast_to(pad_ref[rows : rows + 1], value.shape), value)
    return pltpu.roll(value, rows - 1, 0)


def masked_stack(value, group):
    return jnp.concatenate(
        [jnp.where(lane_mask(value.shape, h), value, jnp.zeros_like(value)) for h in range(group)], 0
    )


def cross_soft(keys, stacked):
    s = dot(keys, stacked, 1, 1)
    top = jnp.max(s, axis=0, keepdims=True)
    e = jnp.exp(s - top)
    return e / jnp.sum(e, axis=0, keepdims=True)


def merged(tall, group):
    rows, width = tall.shape[0] // group, tall.shape[1]
    out = jnp.zeros((rows, width), F32)
    for h in range(group):
        out = jnp.where(lane_mask((rows, width), h), tall[h * rows : (h + 1) * rows], out)
    return out


def cross_fwd_kernel(q_ref, k_ref, v_ref, out_ref, qp_ref, op_ref):
    slot = pl.program_id(0)
    rows = q_ref.shape[0]
    lanes = 4 * HD

    @pl.when(slot == 0)
    def _():
        slotted(q_ref[...], qp_ref)

    here = pl.ds(pl.multiple_of(slot * SEGMENT, SEGMENT), SEGMENT)
    scaled = qp_ref[here, :] * jnp.asarray(HD**-0.5, BF)
    for g in range(q_ref.shape[1] // lanes):
        part = slice(g * lanes, (g + 1) * lanes)
        soft = rounded(cross_soft(k_ref[:, part], masked_stack(scaled[:, part], 4)))
        op_ref[here, part] = merged(dot(soft, v_ref[:, part], 0, 0), 4)

    @pl.when(slot == pl.num_programs(0) - 1)
    def _():
        out_ref[...] = rounded(unslotted(op_ref, rows))


def cross_fwd(queries, pairs, neigh_rows):
    rows, width = queries.shape
    slots = rows // SEGMENT + 1
    return pl.pallas_call(
        cross_fwd_kernel,
        grid=(slots,),
        in_specs=[
            vmem_spec(),
            pl.BlockSpec((neigh_rows, width), lambda i: (i, 0)),
            pl.BlockSpec((neigh_rows, width), lambda i: (i, 1)),
        ],
        out_specs=vmem_spec(),
        out_shape=jax.ShapeDtypeStruct((rows, width), BF),
        scratch_shapes=[
            pltpu.VMEM((slots * SEGMENT, width), BF),
            pltpu.VMEM((slots * SEGMENT, width), F32),
        ],
        compiler_params=pltpu.CompilerParams(vmem_limit_bytes=VMEM_LIMIT),
        cost_estimate=estimate(
            flops=16 * slots * SEGMENT * neigh_rows * width, bytes_accessed=2 * pairs.size,
            transcendentals=slots * neigh_rows * width,
        ),
    )(queries, pairs, pairs)


def cross_bwd_kernel(q_ref, g_ref, k_ref, v_ref, dq_ref, dkv_ref, qp_ref, gp_ref, op_ref):
    slot = pl.program_id(0)
    rows, width = q_ref.shape
    lanes = 4 * HD

    @pl.when(slot == 0)
    def _():
        slotted(q_ref[...], qp_ref)
        slotted(g_ref[...], gp_ref)

    here = pl.ds(pl.multiple_of(slot * SEGMENT, SEGMENT), SEGMENT)
    scaled = qp_ref[here, :] * jnp.asarray(HD**-0.5, BF)
    grads = gp_ref[here, :]
    for g in range(width // lanes):
        part = slice(g * lanes, (g + 1) * lanes)
        queries = masked_stack(scaled[:, part], 4)
        grad = masked_stack(grads[:, part], 4)
        soft = cross_soft(k_ref[:, part], queries)
        gp = dot(v_ref[:, part], grad, 1, 1)
        ds = rounded(soft * (gp - jnp.sum(soft * gp, axis=0, keepdims=True)))
        op_ref[here, part] = merged(dot(ds, k_ref[:, part], 0, 0), 4) * HD**-0.5
        dkv_ref[:, part] = rounded(dot(ds, queries))
        dkv_ref[:, width + g * lanes : width + (g + 1) * lanes] = rounded(dot(rounded(soft), grad))

    @pl.when(slot == pl.num_programs(0) - 1)
    def _():
        dq_ref[...] = rounded(unslotted(op_ref, rows))


def cross_bwd(queries, grads, pairs, neigh_rows):
    rows, width = queries.shape
    slots = rows // SEGMENT + 1
    return pl.pallas_call(
        cross_bwd_kernel,
        grid=(slots,),
        in_specs=[
            vmem_spec(),
            vmem_spec(),
            pl.BlockSpec((neigh_rows, width), lambda i: (i, 0)),
            pl.BlockSpec((neigh_rows, width), lambda i: (i, 1)),
        ],
        out_specs=[vmem_spec(), pl.BlockSpec((neigh_rows, 2 * width), lambda i: (i, 0))],
        out_shape=[
            jax.ShapeDtypeStruct((rows, width), BF),
            jax.ShapeDtypeStruct(pairs.shape, BF),
        ],
        scratch_shapes=[
            pltpu.VMEM((slots * SEGMENT, width), BF),
            pltpu.VMEM((slots * SEGMENT, width), BF),
            pltpu.VMEM((slots * SEGMENT, width), F32),
        ],
        compiler_params=pltpu.CompilerParams(vmem_limit_bytes=VMEM_LIMIT),
        cost_estimate=estimate(
            flops=40 * slots * SEGMENT * neigh_rows * width, bytes_accessed=4 * pairs.size,
            transcendentals=slots * neigh_rows * width,
        ),
    )(queries, grads, pairs, pairs)


def on_device(
    tokens, neighbours, norm_gains, position_bias, query_self, key_self, value_self, output_self,
    query_cross, key_cross, value_cross, output_cross, inner_weight, outer_weight, cotangent,
):
    dp, seq = lax.axis_size("dp"), lax.axis_size("seq")
    rows, model = tokens.shape[1], tokens.shape[2]
    heads = position_bias.shape[0]
    width = heads * HD
    segments = rows // SEGMENT
    neigh_rows = neighbours.shape[2] * neighbours.shape[3]
    span = min(seq, max(2, SEQ_MIN // rows))
    group_width = width // span
    group_heads = heads // span
    my_dp = lax.axis_index("dp")
    pos = lax.axis_index("seq") % span

    fast = seq == 4 and span == 4 and rows % (2 * BLOCK) == 0 and model == 896
    place = my_place() if fast else None

    def whole(shard):
        return assemble(lax.all_gather(shard, BOTH, axis=0, tiled=False), dp, seq)

    own_tokens = tokens.reshape(rows, model)
    states = neighbours.reshape(segments * neigh_rows, model)
    forward_pairs = [(i, i + 1) for i in range(seq - 1) if (i + 1) % span]
    back_pairs = [(i + 1, i) for i in range(seq - 1) if (i + 1) % span]
    inputs = own_tokens.astype(F32)
    upstream = cotangent.reshape(rows, model).astype(F32)
    bias = lax.dynamic_slice_in_dim(position_bias, pos * group_heads, group_heads, 0)
    triple = jnp.concatenate([query_self, key_self, value_self], axis=1)

    pieces_tok = {0: own_tokens}
    bit = span // 2
    while bit:
        for k in list(pieces_tok):
            pieces_tok[k | bit] = swap(pieces_tok[k], "seq", bit)
        bit //= 2
    lane_tokens = [pieces_tok[k] for k in range(span)]

    if fast:
        near = jnp.stack([triple] + [swap(triple, "dp", 2 * k) for k in range(1, dp // 2)])
        far = swap(near, "dp", 1)
        lane_tokens = list(lax.optimization_barrier(tuple(lane_tokens) + (far,)))
        far = lane_tokens.pop()

        def turned(shard):
            flat = shard.T
            half = flat.shape[0] // 2
            return jnp.concatenate([flat[:half], flat[half:]], axis=1)

        packed = jnp.concatenate(
            [key_cross, value_cross, query_cross, turned(output_self), turned(output_cross)], axis=0
        )
        part = outer_weight.shape[0] // 4
        line = [outer_weight[t * part : (t + 1) * part] for t in range(4)]
        feed = jnp.concatenate([inner_weight, jnp.concatenate(line, axis=1)], axis=0)
        group_near = jnp.stack(gather_near(packed))
        feed_line = gather_near(after(feed, group_near))
        edge_source = after(states[(segments - 1) * neigh_rows :], far)
        group_near = after(group_near, far)
        group_both = jnp.concatenate([group_near, over_a(group_near)], axis=0)
        first_normed, qkv, triple_full = project(near, far, norm_gains[:1], lane_tokens, place)
        group_both = after(group_both, qkv)
        group_far = over_b(group_both)
    else:
        edge_source = states[(segments - 1) * neigh_rows :]
        pieces = []
        for shard in (query_self, key_self, value_self):
            pieces.append(lax.dynamic_slice_in_dim(whole(shard), pos * group_width, group_width, 1))
        triple_full = jnp.concatenate(pieces, axis=1)
        recall_full = jnp.concatenate([whole(key_cross), whole(value_cross)], axis=1)
        query_full = whole(query_cross)
        output_turned, cross_turned = whole(output_self).T, whole(output_cross).T
        inner_full, outer_full = whole(inner_weight), whole(outer_weight)
        first_normed = jnp.concatenate(
            [rounded(rms_apply(v.astype(F32), norm_gains[0])) for v in lane_tokens], axis=0
        )
        qkv = rounded(linear(first_normed, triple_full))

    edge = lax.ppermute(edge_source, "seq", forward_pairs)
    mixed_group, lse = self_fwd(pos, bias, qkv, rows)
    if fast:
        feed_line = list(lax.optimization_barrier(tuple(feed_line) + (edge, mixed_group, group_far)))
        group_far, mixed_group, edge = feed_line.pop(), feed_line.pop(), feed_line.pop()

    states_all = lax.optimization_barrier(jnp.concatenate([edge, states], axis=0))

    def exchanged(blocks):
        return [blocks[0]] + [swap(blocks[k], "seq", k) for k in range(1, span)]

    mixed_blocks = [mixed_group[k * rows : (k + 1) * rows] for k in range(span)]
    mixed_self = join_columns(exchanged(mixed_blocks), pos)
    if fast:
        feed_near = after(jnp.stack(feed_line), mixed_self)
        feed_next = over_a(feed_near)
        recall_full, query_full, output_turned, cross_turned = assemble_attention(
            [group_both, group_far, over_core(group_both), over_core(group_far)], place
        )

    recall_pairs = rounded(linear(states_all, recall_full))

    after_self = inputs + input_grad(mixed_self, output_turned)
    second_normed = rounded(rms_apply(after_self, norm_gains[1]))
    if fast:
        feed_both = jnp.concatenate([feed_near, after(feed_next, second_normed)], axis=0)
        feed_far = over_b(feed_both)
    cross_queries = rounded(linear(second_normed, query_full))
    mixed_cross = cross_fwd(cross_queries, recall_pairs, neigh_rows)
    if fast:
        mixed_cross, feed_far = lax.optimization_barrier((mixed_cross, feed_far))
    after_cross = after_self + input_grad(mixed_cross, cross_turned)
    third_normed = rounded(rms_apply(after_cross, norm_gains[2]))
    if fast:
        inner_full, outer_full = assemble_feed(
            [feed_both, feed_far, over_core(feed_both), over_core(feed_far)], place
        )
    gate_value = linear(third_normed, inner_full)
    activated, gelu_pull = jax.vjp(gelu_tanh, gate_value)
    hidden_act = rounded(activated)

    grad_feed = rounded(upstream)
    grad_hidden = input_grad(grad_feed, outer_full)
    grad_gate = rounded(gelu_pull(grad_hidden)[0])
    if fast:
        kept, sent = feed_grad(place, third_normed, grad_gate, hidden_act, grad_feed)
        got = over_core(sent)
    else:
        sum_outer = block_sum(hidden_act, grad_feed)
        sum_inner = block_sum(third_normed, grad_gate)
    norm_grad, gain_three = norm_back(after_cross, norm_gains[2], input_grad(grad_gate, inner_full))
    grad_late = upstream + norm_grad

    grad_cross = rounded(grad_late)
    grad_mixed = rounded(linear(grad_cross, cross_turned))
    if fast:
        got = after(got, grad_mixed)
        sent_b = rounded(wide_sum(kept[1], got[1]))
        grad_mixed = after(grad_mixed, sent_b)
        got_b = over_b(sent_b)
    probe, pair_round = cross_bwd(cross_queries, grad_mixed, recall_pairs, neigh_rows)

    def turned_back(own):
        half = own.shape[1] // 2
        return jnp.concatenate([own[:, :half].T, own[:, half:].T], axis=1)

    if fast:
        pieces = group_grad("tall", place, mixed_cross, grad_cross, 3, 5)
        pieces = group_grad("wide", place, second_normed, probe, 2, 5, pieces)
        pieces = group_grad("wide", place, states_all, pair_round, 0, 5, pieces, 2)
        probe, got_b = lax.optimization_barrier((probe, got_b, pieces[0]))[:2]
        sent_a = sum_second(kept, got, got_b)
        got_a = over_a(sent_a)
    else:
        sum_cross = block_sum(mixed_cross, grad_cross)
        sum_key = block_sum(states_all, pair_round[:, :width])
        sum_value = block_sum(states_all, pair_round[:, width:])
        sum_query = block_sum(second_normed, probe)
    norm_grad, gain_two = norm_back(after_self, norm_gains[1], input_grad(probe, query_full))
    grad_early = grad_late + norm_grad

    grad_self = rounded(grad_early)
    if fast:
        last_kept, last_sent = group_grad("tall", place, mixed_self, grad_self, 4, 5, pieces)
        last_got = over_core(last_sent)
    else:
        sum_output = block_sum(mixed_self, grad_self)
    grad_attended = rounded(linear(grad_self, output_turned))
    if fast:
        grad_attended = after(grad_attended, sent_a)
    grad_parts = exchanged(split_columns(grad_attended, span, pos))
    if fast:
        pair_round = after(pair_round, grad_attended)
    states_round = rounded(input_grad(pair_round, recall_full))
    if fast:
        grad_parts = list(lax.optimization_barrier(tuple(grad_parts) + (states_round, last_got)))
        last_got, states_round = grad_parts.pop(), grad_parts.pop()
        line = sum_third(kept, got, got_b, after(got_a, grad_parts[-1]))
        last_b = rounded(wide_sum(last_kept[1], last_got[1]))
        grad_parts[0] = after(grad_parts[0], line, last_b)
        last_far = over_b(last_b)
        feed_own = [line[0]] + all_over_z(line)
    grad_group = jnp.concatenate(grad_parts, axis=0)
    def joined_states(whole_round, edge_round):
        last = whole_round[segments * neigh_rows :].astype(F32) + edge_round.astype(F32)
        return jnp.concatenate(
            [whole_round[neigh_rows : segments * neigh_rows], rounded(last)], axis=0
        )

    returned = lax.ppermute(states_round[:neigh_rows], "seq", back_pairs)
    triple_grad, bias_sums = self_bwd(pos, bias, qkv, mixed_group, grad_group, lse, rows)
    if fast:
        feed_own, triple_grad, last_far, returned = joint(feed_own, triple_grad, last_far, returned)
        last_a = sum_second(last_kept, last_got, last_far)
        last_near = over_a(last_a)
        own_y, other_y = triple_pieces(place, first_normed, after(triple_grad, last_a))
        other_y, last_near, triple_grad = lax.optimization_barrier((other_y, last_near, triple_grad))
        got_y = swap(other_y, "dp", 1)
    else:
        grad_states = joined_states(states_round, returned)
    partial = input_grad(triple_grad, triple_full)
    gain_one = jnp.sum(partial * first_normed.astype(F32), axis=0) / norm_gains[0]
    partial = rounded(partial)
    if fast:
        last_near = after(last_near, partial)
        line = sum_third(last_kept, last_got, last_far, last_near)
        last_own = [line[0]] + all_over_z(line)
    partial = partial.reshape(span, rows, model)
    blocks = {k: partial[k] for k in range(span)}
    if fast:
        near_zero, near_two = swap(partial[1], "seq", 1), swap(partial[3], "seq", 1)
        leaves = rounded(wide_sum(partial[2], near_two))
        last_own[1:-1], leaves, got_y, near_zero = joint(last_own[1:-1], leaves, got_y, near_zero)
        arrived = swap(leaves, "seq", 2)
        line = rounded(wide_sum(own_y, got_y))
        own = [line[0]] + all_over_z(line)
        feed_own, returned, hidden_act, _ = joint(feed_own, returned, hidden_act, own[1])
        outcome = rounded(after_cross + linear(hidden_act, outer_full))
        feed_own = wide_sum(*feed_own)
        part = feed_own.shape[0] // 2
        sum_inner = feed_own[:part]
        sum_outer = feed_own[part:].reshape(part, 4, model // 4)
        sum_outer = sum_outer.transpose(1, 0, 2).reshape(4 * part, -1)
        grad_states = joined_states(states_round, returned)
    else:
        outcome = rounded(after_cross + linear(hidden_act, outer_full))
        bit = 1
        while bit < span:
            for k in sorted(blocks):
                if not k & bit:
                    got = swap(blocks[k | bit], "seq", bit)
                    blocks[k] = blocks[k].astype(F32) + got.astype(F32)
                    if bit * 2 < span and k:
                        blocks[k] = rounded(blocks[k])
            blocks = {k: v for k, v in blocks.items() if not k & bit}
            bit *= 2
    bias_local = jnp.sum(bias_sums, axis=(2, 3))
    bias_all = lax.dynamic_update_slice_in_dim(
        jnp.zeros((heads, NB), F32), bias_local, pos * group_heads, 0
    )
    small = jnp.concatenate([gain_one, gain_two, gain_three, bias_all.reshape(-1)])
    if fast:
        size = small.shape[0]
        small = jnp.pad(small, (0, -size % 1024)).reshape(-1, 128)
        small = small_sum(after(small, own[1], outcome, grad_states, sum_inner, sum_outer))
        rest, small = joint(own[1:] + last_own[-1:] + [arrived], small)
        own[1:], last_own[-1], arrived = rest[:-2], rest[-2], rest[-1]
        blocks[0] = wide_sum(partial[0], near_zero, arrived)
        small = small.reshape(-1)[:size]
    else:
        small = lax.psum(small, BOTH)
    if fast:
        own_sum = wide_sum(*own)
        own_self = [own_sum[:, i * group_width : (i + 1) * group_width] for i in range(3)]
        last_own = wide_sum(*last_own)
        part = last_own.shape[0] // 5
        sum_key, sum_value, sum_query = (last_own[i * part : (i + 1) * part] for i in range(3))
        sum_cross = turned_back(last_own[3 * part : 4 * part])
        sum_output = turned_back(last_own[4 * part :])
    norm_grad, _ = norm_back(inputs, norm_gains[0], blocks[0])
    grad_inputs = grad_early + norm_grad

    if not fast:
        own_self = []
        for i in range(3):
            columns = triple_grad[:, i * group_width : (i + 1) * group_width]
            wide = jnp.zeros((span * rows, width), BF)
            wide = lax.dynamic_update_slice_in_dim(wide, columns, pos * group_width, 1)
            own_self.append(block_sum(first_normed, wide))

    gains = small[: 3 * model].reshape(3, model)
    bias_total = small[3 * model :].reshape(heads, NB)
    return (
        outcome.reshape(1, rows, model),
        rounded(grad_inputs).reshape(1, rows, model),
        grad_states.reshape(neighbours.shape),
        gains,
        bias_total,
        own_self[0],
        own_self[1],
        own_self[2],
        sum_output,
        sum_query,
        sum_key,
        sum_value,
        sum_cross,
        sum_inner,
        sum_outer,
    )


def solution(mesh):
    weight = P("dp", "seq")
    lane = P("dp", "seq", None)
    wide = P("dp", "seq", None, None, None)
    return jax.shard_map(
        on_device,
        mesh=mesh,
        in_specs=(lane, wide, P(), P()) + (weight,) * 10 + (lane,),
        out_specs=(lane, lane, wide, P(), P()) + (weight,) * 10,
        check_vma=False,
    )
```

```python
import functools

import jax
import jax.numpy as jnp
from jax import lax
from jax.experimental import pallas as pl
from jax.experimental.pallas import tpu as pltpu
from jax.sharding import PartitionSpec as P

HD = 64
SEGMENT = 64
BLOCK = 256
NB = 6
SEQ_MIN = 2048
EPSILON = 1e-06
NEGATIVE = -1e30
BF = jnp.bfloat16
F32 = jnp.float32
VMEM_LIMIT = 56 * 2**20
BOTH = ("dp", "seq")


def dot(a, b, ca=1, cb=0):
    return lax.dot_general(a, b, (((ca,), (cb,)), ((), ())), preferred_element_type=F32)


def linear(a, b):
    return dot(a, b)


def input_grad(a, b):
    return dot(a, b, 1, 1)


def weight_grad(a, b):
    return dot(a, b, 0, 0)


def rounded(v):
    return v.astype(BF)


def rms_apply(inputs, gain_row):
    factor = lax.rsqrt(jnp.mean(inputs * inputs, axis=-1, keepdims=True) + EPSILON)
    return inputs * factor * gain_row


def norm_back(inputs, gain_row, upstream):
    normed_value, pullback = jax.vjp(rms_apply, inputs, gain_row)
    return pullback(upstream)


def gelu_tanh(operand):
    return jax.nn.gelu(operand, approximate=True)


def swap(value, axis, by):
    peers = lax.axis_size(axis)
    return lax.ppermute(value, axis, [(i, i ^ by) for i in range(peers)])


def after(value, *others):
    return lax.optimization_barrier((value,) + others)[0]


def estimate(flops, bytes_accessed, transcendentals):
    return pl.CostEstimate(
        flops=flops // 50, bytes_accessed=bytes_accessed // 50, transcendentals=transcendentals // 50
    )


def vmem_spec():
    return pl.BlockSpec(memory_space=pltpu.VMEM)


def smem_spec():
    return pl.BlockSpec(memory_space=pltpu.SMEM)


def reorder_triple_kernel(place_ref, near_ref, far_ref, out_ref):
    count, rows, _ = near_ref.shape
    z, y = place_ref[0], place_ref[1]
    for ref, flip in ((near_ref, 0), (far_ref, 1)):
        for k in range(count):
            where = ((z ^ k) * 2 + (y ^ flip)) * rows
            out_ref[pl.ds(pl.multiple_of(where, rows), rows), :] = ref[k]


def project_kernel(place_ref, near_ref, far_ref, gain_ref, *refs):
    tokens, (normed_ref, qkv_ref, full_ref) = refs[:-3], refs[-3:]
    reorder_triple_kernel(place_ref, near_ref, far_ref, full_ref)
    rows = tokens[0].shape[0]
    part = rows // 2
    for k, ref in enumerate(tokens):

        def step(i, carry):
            here = pl.ds(pl.multiple_of(i * part, part), part)
            there = pl.ds(pl.multiple_of(k * rows + i * part, part), part)
            normed = rounded(rms_apply(ref[here, :].astype(F32), gain_ref[...]))
            normed_ref[there, :] = normed
            qkv_ref[there, :] = rounded(dot(normed, full_ref[...]))
            return carry

        lax.fori_loop(0, 2, step, 0)


def project(near, far, gain, tokens, place):
    count, height, cols = near.shape
    rows, model = tokens[0].shape
    total = rows * len(tokens)
    return pl.pallas_call(
        project_kernel,
        in_specs=[smem_spec()] + [vmem_spec()] * (3 + len(tokens)),
        out_specs=[vmem_spec()] * 3,
        out_shape=[
            jax.ShapeDtypeStruct((total, model), BF),
            jax.ShapeDtypeStruct((total, cols), BF),
            jax.ShapeDtypeStruct((2 * count * height, cols), BF),
        ],
        compiler_params=pltpu.CompilerParams(vmem_limit_bytes=VMEM_LIMIT),
        cost_estimate=estimate(
            flops=2 * total * model * cols, bytes_accessed=8 * total * model, transcendentals=0
        ),
    )(place, near, far, gain, *tokens)


def join_kernel(mine_ref, *refs):
    out_ref = refs[-1]
    cols = refs[0].shape[1]
    for k, ref in enumerate(refs[:-1]):
        out_ref[:, pl.ds(pl.multiple_of((mine_ref[0] ^ k) * cols, cols), cols)] = ref[...]


def join_columns(pieces, mine):
    rows, cols = pieces[0].shape
    return pl.pallas_call(
        join_kernel,
        in_specs=[smem_spec()] + [vmem_spec()] * len(pieces),
        out_specs=vmem_spec(),
        out_shape=jax.ShapeDtypeStruct((rows, cols * len(pieces)), pieces[0].dtype),
    )(mine.reshape(1), *pieces)


def split_kernel(mine_ref, in_ref, *outs):
    cols = outs[0].shape[1]
    for k, ref in enumerate(outs):
        ref[...] = in_ref[:, pl.ds(pl.multiple_of((mine_ref[0] ^ k) * cols, cols), cols)]


def split_columns(flat, count, mine):
    rows, width = flat.shape
    return pl.pallas_call(
        split_kernel,
        in_specs=[smem_spec(), vmem_spec()],
        out_specs=[vmem_spec()] * count,
        out_shape=[jax.ShapeDtypeStruct((rows, width // count), flat.dtype)] * count,
    )(mine.reshape(1), flat)


def assemble(blocks, dp, seq):
    _, rows, cols = blocks.shape
    return blocks.reshape(dp, seq, rows, cols).transpose(0, 2, 1, 3).reshape(dp * rows, seq * cols)


def block_sum(left, right):
    dp, seq = lax.axis_size("dp"), lax.axis_size("seq")
    rows, cols = left.shape[1] // dp, right.shape[1] // seq
    blocks = rounded(weight_grad(left, right)).reshape(dp, rows, seq, cols).transpose(0, 2, 1, 3)
    blocks = blocks.reshape(dp * seq, rows, cols)
    return lax.psum_scatter(blocks, BOTH, scatter_dimension=0, tiled=True)[0].astype(F32)


def device_pairs(target):
    dp, pairs = lax.axis_size("dp"), []
    for i in range(dp):
        for j in range(4):
            z, y, x, c = target(i // 2, i % 2, j // 2, j % 2)
            pairs.append((i * 4 + j, (z * 2 + y) * 4 + x * 2 + c))
    return pairs


def over_z(value, k):
    return lax.ppermute(value, BOTH, device_pairs(lambda z, y, x, c: (z ^ k, y, x, c)))


def over_a(value):
    return lax.ppermute(
        value, BOTH, device_pairs(lambda z, y, x, c: (z, y ^ c, x ^ (1 - c), c))
    )


def over_b(value):
    return lax.ppermute(
        value, BOTH, device_pairs(lambda z, y, x, c: (z, y ^ (1 - c), x ^ c, c))
    )


def over_core(value):
    return lax.ppermute(value, BOTH, device_pairs(lambda z, y, x, c: (z, y, x, 1 - c)))


def my_place():
    i, j = lax.axis_index("dp"), lax.axis_index("seq")
    return jnp.stack([i // 2, i % 2, j // 2, j % 2]).astype(jnp.int32)


def gather_near(shard):
    depth = lax.axis_size("dp") // 2
    return [shard] + [over_z(shard, k) for k in range(1, depth)]


def piece_origin(place_ref, c, b, t, depth):
    z, y, x, core = (place_ref[i] for i in range(4))
    a, k = t // depth, t % depth
    core = core ^ c
    dx = jnp.where(core == 0, a, b)
    dy = jnp.where(core == 0, b, a)
    return (z ^ k) * 2 + (y ^ dy), (x ^ dx) * 2 + core


def assemble_attention_kernel(depth, place_ref, *refs):
    pieces, (recall, query, out_self, out_cross), sems = refs[:4], refs[4:8], refs[8]
    rows = query.shape[0] // (2 * depth)
    cols = query.shape[1] // 4
    half = cols // 2

    def step(t, carry):
        for i in range(4):
            i_dp, i_seq = piece_origin(place_ref, i // 2, i % 2, t, depth)
            down = pl.ds(pl.multiple_of(i_dp * rows, rows), rows)
            across = pl.multiple_of(i_seq * cols, cols)
            piece = pieces[i].at[t]

            def move(first, target, sem):
                pltpu.make_async_copy(piece.at[pl.ds(first, rows), :], target, sems.at[sem]).start()

            move(0, recall.at[down, pl.ds(across, cols)], 0)
            move(rows, recall.at[down, pl.ds(across + 4 * cols, cols)], 0)
            move(2 * rows, query.at[down, pl.ds(across, cols)], 1)
            lanes = pl.ds(pl.multiple_of(i_dp * half, half), half)
            for w, out in ((0, out_self), (1, out_cross)):
                for h in range(2):
                    top = pl.multiple_of((i_seq * 2 + h) * rows, rows)
                    pltpu.make_async_copy(
                        piece.at[pl.ds((3 + w) * rows, rows), pl.ds(h * half, half)],
                        out.at[pl.ds(top, rows), lanes],
                        sems.at[2 + w],
                    ).start()
        return carry

    lax.fori_loop(0, 2 * depth, step, 0)
    for sem, out in enumerate((recall, query, out_self, out_cross)):
        pltpu.make_async_copy(out, out, sems.at[sem]).wait()


def assemble_attention(pieces, place):
    count, packed, cols = pieces[0].shape
    rows = packed // 5
    model, width = rows * count, cols * 4
    shapes = [(model, 2 * width), (model, width), (8 * rows, width), (8 * rows, width)]
    return pl.pallas_call(
        functools.partial(assemble_attention_kernel, count // 2),
        in_specs=[smem_spec()] + [pl.BlockSpec(memory_space=pl.ANY)] * 4,
        out_specs=[vmem_spec()] * 4,
        out_shape=[jax.ShapeDtypeStruct(s, BF) for s in shapes],
        scratch_shapes=[pltpu.SemaphoreType.DMA((4,))],
        compiler_params=pltpu.CompilerParams(vmem_limit_bytes=VMEM_LIMIT),
    )(place, *pieces)


def assemble_feed_kernel(depth, place_ref, *refs):
    pieces, (inner, outer, stage, sems) = refs[:4], refs[4:]
    rows, cols = stage.shape[2:]
    part = cols // 4

    def step(t, carry):
        for i in range(4):
            i_dp, i_seq = piece_origin(place_ref, i // 2, i % 2, t, depth)
            piece = pieces[i].at[t]
            down = pl.ds(pl.multiple_of(i_dp * rows, rows), rows)
            across = pl.ds(pl.multiple_of(i_seq * cols, cols), cols)
            pltpu.make_async_copy(
                piece.at[pl.ds(rows, rows), :], stage.at[i_dp, i_seq], sems.at[1]
            ).start()
            pltpu.make_async_copy(
                piece.at[pl.ds(0, rows), :], inner.at[down, across], sems.at[0]
            ).start()
        return carry

    lax.fori_loop(0, 2 * depth, step, 0)
    pltpu.make_async_copy(stage, stage, sems.at[1]).wait()

    def spread(i, carry):
        for t in range(4):
            line = [stage[i, j, :, t * part : (t + 1) * part] for j in range(4)]
            where = pl.multiple_of((i * 4 + t) * rows, rows)
            outer[pl.ds(where, rows), :] = jnp.concatenate(line, axis=1)
        return carry

    lax.fori_loop(0, 2 * depth, spread, 0)
    pltpu.make_async_copy(inner, inner, sems.at[0]).wait()


def assemble_feed(pieces, place):
    deep, packed, cols = pieces[0].shape
    rows = packed // 2
    return pl.pallas_call(
        functools.partial(assemble_feed_kernel, deep // 2),
        in_specs=[smem_spec()] + [pl.BlockSpec(memory_space=pl.ANY)] * 4,
        out_specs=[vmem_spec()] * 2,
        out_shape=[
            jax.ShapeDtypeStruct((rows * deep, cols * 4), BF),
            jax.ShapeDtypeStruct((4 * rows * deep, cols), BF),
        ],
        scratch_shapes=[
            pltpu.VMEM((deep, 4, rows, cols), BF),
            pltpu.SemaphoreType.DMA((2,)),
        ],
        compiler_params=pltpu.CompilerParams(vmem_limit_bytes=VMEM_LIMIT),
    )(place, *pieces)


def put_block(place_ref, out_ref, core, i_dp, flip, value):
    z, y = place_ref[0], place_ref[1]
    dy = (i_dp % 2) ^ y
    b = jnp.where(core == 0, dy, flip)
    a = jnp.where(core == 0, flip, dy)
    out_ref[b, a, (i_dp // 2) ^ z] = value


def wide_grad_kernel(*refs):
    place_ref, left, kept_right, sent_right = refs[:4]
    kept, sent = refs[-2:]
    flip = pl.program_id(1)
    rows = kept.shape[3]
    core = place_ref[3]
    for right, out, c in ((kept_right, kept, core), (sent_right, sent, 1 - core)):
        value = rounded(dot(left[...], right[...], 0, 0))
        for i_dp in range(value.shape[0] // rows):
            put_block(place_ref, out, c, i_dp, flip, value[i_dp * rows : (i_dp + 1) * rows])


def tall_grad_kernel(*refs):
    place_ref, left, right = refs[:3]
    kept, sent = refs[-2:]
    rows, cols = kept.shape[3], kept.shape[4]
    half = cols // 2
    x, core = place_ref[2], place_ref[3]
    for j in range(4):
        value = rounded(dot(right[:, 2 * j * rows : 2 * (j + 1) * rows], left[...], 0, 0))
        for out, mine in ((kept, core == j % 2), (sent, core != j % 2)):

            @pl.when(mine)
            def _():
                for i_dp in range(value.shape[1] // half):
                    lanes = slice(i_dp * half, (i_dp + 1) * half)
                    block = jnp.concatenate([value[:rows, lanes], value[rows:, lanes]], axis=1)
                    put_block(place_ref, out, j % 2, i_dp, (j // 2) ^ x, block)


def feed_outer_kernel(place_ref, left, right, kept, sent):
    rows, cols = kept.shape[3:]
    part = cols // 4
    y, x, core = place_ref[1], place_ref[2], place_ref[3]
    value = rounded(dot(left[...], right[...], 0, 0))
    for j in range(4):
        for out, mine in ((kept, core == j % 2), (sent, core != j % 2)):

            @pl.when(mine)
            def _():
                for i_y in range(2):
                    base = i_y * 4 * rows
                    lanes = slice(j * part, (j + 1) * part)
                    line = [value[base + t * rows : base + (t + 1) * rows, lanes] for t in range(4)]
                    dy, flip = i_y ^ y, (j // 2) ^ x
                    b, a = (dy, flip) if j % 2 == 0 else (flip, dy)
                    out[b, a, 0] = jnp.concatenate(line, axis=1)


def feed_grad(place, normed, grad_gate, hidden, grad_feed):
    dp = lax.axis_size("dp")
    depth = dp // 2
    tokens, model = normed.shape
    inner = grad_gate.shape[1]
    rows, cols = model // dp, inner // 4
    shape = jax.ShapeDtypeStruct((2, 2, depth, 2 * rows, cols), BF)
    out_spec = pl.BlockSpec((2, 2, 1, rows, cols), lambda i, m: (0, 0, m[0] ^ i, 1, 0))
    pieces = pl.pallas_call(
        feed_outer_kernel,
        grid_spec=pltpu.PrefetchScalarGridSpec(
            num_scalar_prefetch=1,
            grid=(depth,),
            in_specs=[
                pl.BlockSpec((tokens, inner // depth), lambda i, m: (0, i)),
                pl.BlockSpec((tokens, model), lambda i, m: (0, 0)),
            ],
            out_specs=[out_spec] * 2,
        ),
        out_shape=[shape, shape],
        compiler_params=pltpu.CompilerParams(vmem_limit_bytes=VMEM_LIMIT),
        cost_estimate=estimate(
            flops=2 * tokens * model * inner,
            bytes_accessed=2 * (tokens * (model + inner) + model * inner),
            transcendentals=0,
        ),
    )(place, hidden, grad_feed)
    return group_grad("wide", place, normed, grad_gate, 0, 2, pieces)


def group_grad(kind, place, left, right, first, total, before=None, parts=1):
    dp = lax.axis_size("dp")
    depth = dp // 2
    tokens, height = left.shape
    width = right.shape[1]
    if kind == "tall":
        rows, cols = width // 8, 2 * height // dp
    else:
        rows, cols = height // dp, width // 4 // parts
    whole = jax.ShapeDtypeStruct((2, 2, depth, total * rows, cols), BF)
    block = (2, 2, depth, rows, cols)
    if kind == "wide":
        kernel, grid, operands = wide_grad_kernel, (parts, 2), [left, right, right]
        specs = [
            pl.BlockSpec((tokens, height), lambda p, i, m: (0, 0)),
            pl.BlockSpec((tokens, cols), lambda p, i, m: (0, p * 4 + (m[2] ^ i) * 2 + m[3])),
            pl.BlockSpec((tokens, cols), lambda p, i, m: (0, p * 4 + (m[2] ^ i) * 2 + 1 - m[3])),
        ]
        out_spec = pl.BlockSpec(block, lambda p, i, m: (0, 0, 0, first + p, 0))
    else:
        kernel, grid, operands = tall_grad_kernel, (1,), [left, right]
        specs = [
            pl.BlockSpec((tokens, height), lambda i, m: (0, 0)),
            pl.BlockSpec((tokens, width), lambda i, m: (0, 0)),
        ]
        out_spec = pl.BlockSpec(block, lambda i, m: (0, 0, 0, first, 0))
    aliases = {}
    if before is not None:
        aliases = {1 + len(operands): 0, 2 + len(operands): 1}
        operands = operands + list(before)
        specs = specs + [pl.BlockSpec(memory_space=pl.ANY)] * 2
    return pl.pallas_call(
        kernel,
        grid_spec=pltpu.PrefetchScalarGridSpec(
            num_scalar_prefetch=1, grid=grid, in_specs=specs, out_specs=[out_spec] * 2
        ),
        out_shape=[whole, whole],
        input_output_aliases=aliases,
        compiler_params=pltpu.CompilerParams(vmem_limit_bytes=VMEM_LIMIT),
        cost_estimate=estimate(
            flops=2 * tokens * height * width,
            bytes_accessed=2 * (left.size + right.size + height * width),
            transcendentals=0,
        ),
    )(place, *operands)


def wide_sum(*values):
    total = values[0].astype(F32)
    for value in values[1:]:
        total = total + value.astype(F32)
    return total


def sum_second(kept, got, got_b):
    return rounded(wide_sum(kept[0, 1], got[0, 1], got_b[1]))


def sum_third(kept, got, got_b, got_a):
    return rounded(wide_sum(kept[0, 0], got[0, 0], got_b[0], got_a))


def all_over_z(line):
    return [over_z(line[k], k) for k in range(1, line.shape[0])]


def joint(values, *others):
    out = lax.optimization_barrier(tuple(values) + others)
    return list(out[: len(values)]), *out[len(values) :]


def small_sum_kernel(dp, seq, in_ref, out_ref, slots, send_sems, recv_sems):
    count = dp * seq
    me = lax.axis_index("dp") * seq + lax.axis_index("seq")
    barrier = pltpu.get_barrier_semaphore()

    def peer(d):
        other = lax.rem(me + d, count)
        return lax.div(other, seq), lax.rem(other, seq)

    def greet(d, carry):
        pl.semaphore_signal(
            barrier, inc=1, device_id=peer(d), device_id_type=pl.DeviceIdType.MESH
        )
        return carry

    lax.fori_loop(1, count, greet, 0)
    pl.semaphore_wait(barrier, count - 1)

    def copy(d):
        return pltpu.make_async_remote_copy(
            src_ref=in_ref,
            dst_ref=slots.at[d - 1],
            send_sem=send_sems.at[d - 1],
            recv_sem=recv_sems.at[d - 1],
            device_id=peer(d),
            device_id_type=pl.DeviceIdType.MESH,
        )

    def start(d, carry):
        copy(d).start()
        return carry

    def wait(d, carry):
        copy(d).wait()
        return carry

    lax.fori_loop(1, count, start, 0)
    lax.fori_loop(1, count, wait, 0)
    total = in_ref[...]
    for d in range(count - 1):
        total = total + slots[d]
    out_ref[...] = total


def small_sum(value):
    dp, seq = lax.axis_size("dp"), lax.axis_size("seq")
    others = dp * seq - 1
    return pl.pallas_call(
        functools.partial(small_sum_kernel, dp, seq),
        in_specs=[vmem_spec()],
        out_specs=vmem_spec(),
        out_shape=jax.ShapeDtypeStruct(value.shape, value.dtype),
        scratch_shapes=[
            pltpu.VMEM((others,) + value.shape, value.dtype),
            pltpu.SemaphoreType.DMA((others,)),
            pltpu.SemaphoreType.DMA((others,)),
        ],
        compiler_params=pltpu.CompilerParams(collective_id=0, has_side_effects=True),
    )(value)


def triple_grad_kernel(place_ref, left, right, kept, sent):
    value = rounded(dot(left[...], right[...], 0, 0))
    rows = kept.shape[1]
    z, y = place_ref[0], place_ref[1]
    for out, flip in ((kept, 0), (sent, 1)):
        for i_y in range(2):

            @pl.when((y ^ i_y) == flip)
            def _():
                for i_z in range(kept.shape[0]):
                    top = (i_z * 2 + i_y) * rows
                    out[i_z ^ z] = value[top : top + rows]


def triple_pieces(place, left, right):
    dp = lax.axis_size("dp")
    rows, cols = left.shape[1] // dp, right.shape[1]
    shape = jax.ShapeDtypeStruct((dp // 2, rows, cols), BF)
    return pl.pallas_call(
        triple_grad_kernel,
        in_specs=[smem_spec(), vmem_spec(), vmem_spec()],
        out_specs=[vmem_spec()] * 2,
        out_shape=[shape, shape],
        compiler_params=pltpu.CompilerParams(vmem_limit_bytes=VMEM_LIMIT),
        cost_estimate=estimate(
            flops=2 * left.size * cols, bytes_accessed=2 * (left.size + right.size), transcendentals=0
        ),
    )(place, left, right)


def lane_mask(shape, head):
    lanes = lax.broadcasted_iota(jnp.int32, shape, len(shape) - 1)
    return (lanes >= head * HD) & (lanes < (head + 1) * HD)


def transposed(value):
    return value.astype(F32).T


def block_bias(bias_ref, head, query_block, key_block):
    distance = query_block - key_block
    kept = bias_ref[head, jnp.clip(distance, 0, NB - 1)]
    return jnp.where(distance >= 0, kept, NEGATIVE)


def self_fwd_kernel(pos_ref, bias_ref, qkv_ref, o_ref, lse_ref, kh_ref, vt_ref, s_ref, acc_ref):
    heads = kh_ref.shape[0]
    width = heads * HD
    devs, _, rows = vt_ref.shape
    per = rows // BLOCK
    a = pl.program_id(0)
    pos = pos_ref[0]

    @pl.when(a == 0)
    def _():
        for h in range(heads):
            kh_ref[h] = qkv_ref[:, width + h * HD : width + (h + 1) * HD]
        for d in range(devs):
            vt_ref[d] = rounded(transposed(qkv_ref[d * rows : (d + 1) * rows, 2 * width :]))

    first = pl.multiple_of(((a // per) ^ pos) * rows + (a % per) * BLOCK, BLOCK)
    qt = rounded(transposed(qkv_ref[pl.ds(first, BLOCK), :width]) * HD**-0.5)

    def scores(d, tops):
        where = pl.multiple_of((d ^ pos) * rows, rows)
        out = []
        for h in range(heads):
            raw = dot(kh_ref[h, pl.ds(where, rows), :], qt[h * HD : (h + 1) * HD])
            top = tops[h]
            for half in range(per):
                c = block_bias(bias_ref, h, a, d * per + half)
                piece = raw[half * BLOCK : (half + 1) * BLOCK] + c
                s_ref[h, pl.ds(pl.multiple_of(d * rows + half * BLOCK, BLOCK), BLOCK), :] = piece
                top = jnp.maximum(top, jnp.max(piece.reshape(BLOCK // 8, 8, BLOCK), axis=0))
            out.append(top)
        return tuple(out)

    count = a // per + 1
    tops = lax.fori_loop(
        0, count, scores, tuple(jnp.full((8, BLOCK), NEGATIVE, F32) for _ in range(heads))
    )
    tops = [jnp.max(t, axis=0, keepdims=True) for t in tops]
    acc_ref[...] = jnp.zeros_like(acc_ref)

    def mix(d, sums):
        out = []
        slot = d ^ pos
        for h in range(heads):
            e = jnp.exp(s_ref[h, pl.ds(pl.multiple_of(d * rows, rows), rows), :] - tops[h])
            out.append(sums[h] + jnp.sum(e.reshape(rows // 8, 8, BLOCK), axis=0))
            acc_ref[h * HD : (h + 1) * HD, :] += dot(
                vt_ref[slot, h * HD : (h + 1) * HD, :], rounded(e)
            )
        return tuple(out)

    sums = lax.fori_loop(
        0, count, mix, tuple(jnp.zeros((8, BLOCK), F32) for _ in range(heads))
    )
    for h in range(heads):
        total = jnp.sum(sums[h], axis=0, keepdims=True)
        lse_ref[a, h : h + 1, :] = tops[h] + jnp.log(total)
        acc_ref[h * HD : (h + 1) * HD, :] = acc_ref[h * HD : (h + 1) * HD, :] / total
    o_ref[pl.ds(first, BLOCK), :] = rounded(acc_ref[...].T)


def self_fwd(pos, bias, qkv, rows):
    tokens, triple = qkv.shape
    width = triple // 3
    heads = width // HD
    blocks = tokens // BLOCK
    return pl.pallas_call(
        self_fwd_kernel,
        grid=(blocks,),
        in_specs=[smem_spec(), smem_spec(), vmem_spec()],
        out_specs=[vmem_spec(), vmem_spec()],
        out_shape=[
            jax.ShapeDtypeStruct((tokens, width), BF),
            jax.ShapeDtypeStruct((blocks, 8, BLOCK), F32),
        ],
        scratch_shapes=[
            pltpu.VMEM((heads, tokens, HD), BF),
            pltpu.VMEM((tokens // rows, width, rows), BF),
            pltpu.VMEM((heads, tokens, BLOCK), F32),
            pltpu.VMEM((width, BLOCK), F32),
        ],
        compiler_params=pltpu.CompilerParams(vmem_limit_bytes=VMEM_LIMIT),
        cost_estimate=estimate(
            flops=2 * tokens * tokens * width * 2, bytes_accessed=8 * tokens * width,
            transcendentals=tokens * tokens * heads // 2,
        ),
    )(pos.reshape(1), bias, qkv)


def self_bwd_kernel(
    pos_ref, bias_ref, qkv_ref, o_ref, go_ref, lse_ref, dqkv_ref, bsum_ref,
    kh_ref, vh_ref, kt_ref, qm_ref, gm_ref, p_ref, ds_ref, dst_ref, dq_ref, dk_ref, dv_ref,
):
    heads = kh_ref.shape[0]
    width = heads * HD
    devs, _, rows = kt_ref.shape
    per = rows // BLOCK
    a = pl.program_id(0)
    pos = pos_ref[0]

    @pl.when(a == 0)
    def _():
        for h in range(heads):
            kh_ref[h] = qkv_ref[:, width + h * HD : width + (h + 1) * HD]
            vh_ref[h] = qkv_ref[:, 2 * width + h * HD : 2 * width + (h + 1) * HD]
        for d in range(devs):
            kt_ref[d] = rounded(transposed(qkv_ref[d * rows : (d + 1) * rows, width : 2 * width]))
        dk_ref[...] = jnp.zeros_like(dk_ref)
        dv_ref[...] = jnp.zeros_like(dv_ref)
        bsum_ref[...] = jnp.zeros_like(bsum_ref)

    first = pl.multiple_of(((a // per) ^ pos) * rows + (a % per) * BLOCK, BLOCK)
    q = qkv_ref[pl.ds(first, BLOCK), :width] * jnp.asarray(HD**-0.5, BF)
    go = go_ref[pl.ds(first, BLOCK), :]
    qt = rounded(transposed(q))
    got = transposed(go)
    prod = got * transposed(o_ref[pl.ds(first, BLOCK), :])
    got = rounded(got)
    zero = jnp.zeros((BLOCK, width), BF)
    dots, lses = [], []
    for h in range(heads):
        mask = lane_mask((BLOCK, width), h)
        qm_ref[h * BLOCK : (h + 1) * BLOCK, :] = jnp.where(mask, q, zero)
        gm_ref[h * BLOCK : (h + 1) * BLOCK, :] = jnp.where(mask, go, zero)
        dots.append(jnp.sum(prod[h * HD : (h + 1) * HD], axis=0, keepdims=True))
        lses.append(lse_ref[a, h : h + 1, :])
    dq_ref[...] = jnp.zeros_like(dq_ref)

    def step(d, carry):
        where = pl.multiple_of((d ^ pos) * rows, rows)
        slot = d ^ pos
        for h in range(heads):
            lanes = slice(h * HD, (h + 1) * HD)
            cols = slice(h * BLOCK, (h + 1) * BLOCK)
            raw = dot(kh_ref[h, pl.ds(where, rows), :], qt[lanes])
            gp = dot(vh_ref[h, pl.ds(where, rows), :], got[lanes])
            for half in range(per):
                part = slice(half * BLOCK, (half + 1) * BLOCK)
                key_block = d * per + half
                c = block_bias(bias_ref, h, a, key_block)
                pf = jnp.exp(raw[part] + (c - lses[h]))
                p_ref[part, cols] = rounded(pf)
                ds = rounded(pf * (gp[part] - dots[h]))
                ds_ref[part, cols] = ds
                dst_ref[h, part, :] = ds
                bucket = jnp.clip(a - key_block, 0, NB - 1)
                bsum_ref[h, bucket] += jnp.sum(
                    ds.astype(F32).reshape(BLOCK // 8, 8, BLOCK), axis=0
                )
            dq_ref[lanes, :] += dot(kt_ref[slot, lanes, :], dst_ref[h])
        dv_ref[pl.ds(where, rows), :] += dot(p_ref[...], gm_ref[...])
        dk_ref[pl.ds(where, rows), :] += dot(ds_ref[...], qm_ref[...])
        return carry

    lax.fori_loop(0, a // per + 1, step, 0)
    dqkv_ref[pl.ds(first, BLOCK), :width] = rounded(dq_ref[...].T * HD**-0.5)

    @pl.when(a == pl.num_programs(0) - 1)
    def _():
        dqkv_ref[:, width : 2 * width] = rounded(dk_ref[...])
        dqkv_ref[:, 2 * width :] = rounded(dv_ref[...])


def self_bwd(pos, bias, qkv, mixed, grad, lse, rows):
    tokens, triple = qkv.shape
    width = triple // 3
    heads = width // HD
    blocks = tokens // BLOCK
    return pl.pallas_call(
        self_bwd_kernel,
        grid=(blocks,),
        in_specs=[smem_spec(), smem_spec()] + [vmem_spec()] * 4,
        out_specs=[vmem_spec(), vmem_spec()],
        out_shape=[
            jax.ShapeDtypeStruct((tokens, triple), BF),
            jax.ShapeDtypeStruct((heads, NB, 8, BLOCK), F32),
        ],
        scratch_shapes=[
            pltpu.VMEM((heads, tokens, HD), BF),
            pltpu.VMEM((heads, tokens, HD), BF),
            pltpu.VMEM((tokens // rows, width, rows), BF),
            pltpu.VMEM((heads * BLOCK, width), BF),
            pltpu.VMEM((heads * BLOCK, width), BF),
            pltpu.VMEM((rows, heads * BLOCK), BF),
            pltpu.VMEM((rows, heads * BLOCK), BF),
            pltpu.VMEM((heads, rows, BLOCK), BF),
            pltpu.VMEM((width, BLOCK), F32),
            pltpu.VMEM((tokens, width), F32),
            pltpu.VMEM((tokens, width), F32),
        ],
        compiler_params=pltpu.CompilerParams(vmem_limit_bytes=VMEM_LIMIT),
        cost_estimate=estimate(
            flops=5 * tokens * tokens * width * 2, bytes_accessed=16 * tokens * width,
            transcendentals=tokens * tokens * heads // 2,
        ),
    )(pos.reshape(1), bias, qkv, mixed, grad, lse)


def slotted(value, pad_ref):
    rows = value.shape[0]
    rolled = pltpu.roll(value.astype(F32), 1, 0)
    first = lax.broadcasted_iota(jnp.int32, rolled.shape, 0) == 0
    pad_ref[:rows] = rounded(jnp.where(first, 0.0, rolled))
    pad_ref[rows:] = rounded(jnp.where(first, rolled, 0.0)[:SEGMENT])


def unslotted(pad_ref, rows):
    value = pad_ref[:rows]
    first = lax.broadcasted_iota(jnp.int32, value.shape, 0) == 0
    value = jnp.where(first, jnp.broadcast_to(pad_ref[rows : rows + 1], value.shape), value)
    return pltpu.roll(value, rows - 1, 0)


def masked_stack(value, group):
    return jnp.concatenate(
        [jnp.where(lane_mask(value.shape, h), value, jnp.zeros_like(value)) for h in range(group)], 0
    )


def cross_soft(keys, stacked):
    s = dot(keys, stacked, 1, 1)
    top = jnp.max(s, axis=0, keepdims=True)
    e = jnp.exp(s - top)
    return e / jnp.sum(e, axis=0, keepdims=True)


def merged(tall, group):
    rows, width = tall.shape[0] // group, tall.shape[1]
    out = jnp.zeros((rows, width), F32)
    for h in range(group):
        out = jnp.where(lane_mask((rows, width), h), tall[h * rows : (h + 1) * rows], out)
    return out


def cross_fwd_kernel(q_ref, k_ref, v_ref, out_ref, qp_ref, op_ref):
    slot = pl.program_id(0)
    rows = q_ref.shape[0]
    lanes = 4 * HD

    @pl.when(slot == 0)
    def _():
        slotted(q_ref[...], qp_ref)

    here = pl.ds(pl.multiple_of(slot * SEGMENT, SEGMENT), SEGMENT)
    scaled = qp_ref[here, :] * jnp.asarray(HD**-0.5, BF)
    for g in range(q_ref.shape[1] // lanes):
        part = slice(g * lanes, (g + 1) * lanes)
        soft = rounded(cross_soft(k_ref[:, part], masked_stack(scaled[:, part], 4)))
        op_ref[here, part] = merged(dot(soft, v_ref[:, part], 0, 0), 4)

    @pl.when(slot == pl.num_programs(0) - 1)
    def _():
        out_ref[...] = rounded(unslotted(op_ref, rows))


def cross_fwd(queries, pairs, neigh_rows):
    rows, width = queries.shape
    slots = rows // SEGMENT + 1
    return pl.pallas_call(
        cross_fwd_kernel,
        grid=(slots,),
        in_specs=[
            vmem_spec(),
            pl.BlockSpec((neigh_rows, width), lambda i: (i, 0)),
            pl.BlockSpec((neigh_rows, width), lambda i: (i, 1)),
        ],
        out_specs=vmem_spec(),
        out_shape=jax.ShapeDtypeStruct((rows, width), BF),
        scratch_shapes=[
            pltpu.VMEM((slots * SEGMENT, width), BF),
            pltpu.VMEM((slots * SEGMENT, width), F32),
        ],
        compiler_params=pltpu.CompilerParams(vmem_limit_bytes=VMEM_LIMIT),
        cost_estimate=estimate(
            flops=16 * slots * SEGMENT * neigh_rows * width, bytes_accessed=2 * pairs.size,
            transcendentals=slots * neigh_rows * width,
        ),
    )(queries, pairs, pairs)


def cross_bwd_kernel(q_ref, g_ref, k_ref, v_ref, dq_ref, dkv_ref, qp_ref, gp_ref, op_ref):
    slot = pl.program_id(0)
    rows, width = q_ref.shape
    lanes = 4 * HD

    @pl.when(slot == 0)
    def _():
        slotted(q_ref[...], qp_ref)
        slotted(g_ref[...], gp_ref)

    here = pl.ds(pl.multiple_of(slot * SEGMENT, SEGMENT), SEGMENT)
    scaled = qp_ref[here, :] * jnp.asarray(HD**-0.5, BF)
    grads = gp_ref[here, :]
    for g in range(width // lanes):
        part = slice(g * lanes, (g + 1) * lanes)
        queries = masked_stack(scaled[:, part], 4)
        grad = masked_stack(grads[:, part], 4)
        soft = cross_soft(k_ref[:, part], queries)
        gp = dot(v_ref[:, part], grad, 1, 1)
        ds = rounded(soft * (gp - jnp.sum(soft * gp, axis=0, keepdims=True)))
        op_ref[here, part] = merged(dot(ds, k_ref[:, part], 0, 0), 4) * HD**-0.5
        dkv_ref[:, part] = rounded(dot(ds, queries))
        dkv_ref[:, width + g * lanes : width + (g + 1) * lanes] = rounded(dot(rounded(soft), grad))

    @pl.when(slot == pl.num_programs(0) - 1)
    def _():
        dq_ref[...] = rounded(unslotted(op_ref, rows))


def cross_bwd(queries, grads, pairs, neigh_rows):
    rows, width = queries.shape
    slots = rows // SEGMENT + 1
    return pl.pallas_call(
        cross_bwd_kernel,
        grid=(slots,),
        in_specs=[
            vmem_spec(),
            vmem_spec(),
            pl.BlockSpec((neigh_rows, width), lambda i: (i, 0)),
            pl.BlockSpec((neigh_rows, width), lambda i: (i, 1)),
        ],
        out_specs=[vmem_spec(), pl.BlockSpec((neigh_rows, 2 * width), lambda i: (i, 0))],
        out_shape=[
            jax.ShapeDtypeStruct((rows, width), BF),
            jax.ShapeDtypeStruct(pairs.shape, BF),
        ],
        scratch_shapes=[
            pltpu.VMEM((slots * SEGMENT, width), BF),
            pltpu.VMEM((slots * SEGMENT, width), BF),
            pltpu.VMEM((slots * SEGMENT, width), F32),
        ],
        compiler_params=pltpu.CompilerParams(vmem_limit_bytes=VMEM_LIMIT),
        cost_estimate=estimate(
            flops=40 * slots * SEGMENT * neigh_rows * width, bytes_accessed=4 * pairs.size,
            transcendentals=slots * neigh_rows * width,
        ),
    )(queries, grads, pairs, pairs)


def on_device(
    tokens, neighbours, norm_gains, position_bias, query_self, key_self, value_self, output_self,
    query_cross, key_cross, value_cross, output_cross, inner_weight, outer_weight, cotangent,
):
    dp, seq = lax.axis_size("dp"), lax.axis_size("seq")
    rows, model = tokens.shape[1], tokens.shape[2]
    heads = position_bias.shape[0]
    width = heads * HD
    segments = rows // SEGMENT
    neigh_rows = neighbours.shape[2] * neighbours.shape[3]
    span = min(seq, max(2, SEQ_MIN // rows))
    group_width = width // span
    group_heads = heads // span
    my_dp = lax.axis_index("dp")
    pos = lax.axis_index("seq") % span

    fast = seq == 4 and span == 4 and rows % (2 * BLOCK) == 0 and model == 896
    place = my_place() if fast else None

    def whole(shard):
        return assemble(lax.all_gather(shard, BOTH, axis=0, tiled=False), dp, seq)

    own_tokens = tokens.reshape(rows, model)
    states = neighbours.reshape(segments * neigh_rows, model)
    forward_pairs = [(i, i + 1) for i in range(seq - 1) if (i + 1) % span]
    back_pairs = [(i + 1, i) for i in range(seq - 1) if (i + 1) % span]
    inputs = own_tokens.astype(F32)
    upstream = cotangent.reshape(rows, model).astype(F32)
    bias = lax.dynamic_slice_in_dim(position_bias, pos * group_heads, group_heads, 0)
    triple = jnp.concatenate([query_self, key_self, value_self], axis=1)

    pieces_tok = {0: own_tokens}
    bit = span // 2
    while bit:
        for k in list(pieces_tok):
            pieces_tok[k | bit] = swap(pieces_tok[k], "seq", bit)
        bit //= 2
    lane_tokens = [pieces_tok[k] for k in range(span)]

    if fast:
        near = jnp.stack([triple] + [swap(triple, "dp", 2 * k) for k in range(1, dp // 2)])
        far = swap(near, "dp", 1)
        lane_tokens = list(lax.optimization_barrier(tuple(lane_tokens) + (far,)))
        far = lane_tokens.pop()

        def turned(shard):
            flat = shard.T
            half = flat.shape[0] // 2
            return jnp.concatenate([flat[:half], flat[half:]], axis=1)

        packed = jnp.concatenate(
            [key_cross, value_cross, query_cross, turned(output_self), turned(output_cross)], axis=0
        )
        part = outer_weight.shape[0] // 4
        line = [outer_weight[t * part : (t + 1) * part] for t in range(4)]
        feed = jnp.concatenate([inner_weight, jnp.concatenate(line, axis=1)], axis=0)
        group_near = jnp.stack(gather_near(packed))
        feed_line = gather_near(after(feed, group_near))
        edge_source = after(states[(segments - 1) * neigh_rows :], far)
        group_near = after(group_near, far)
        group_both = jnp.concatenate([group_near, over_a(group_near)], axis=0)
        first_normed, qkv, triple_full = project(near, far, norm_gains[:1], lane_tokens, place)
        group_both = after(group_both, qkv)
        group_far = over_b(group_both)
    else:
        edge_source = states[(segments - 1) * neigh_rows :]
        pieces = []
        for shard in (query_self, key_self, value_self):
            pieces.append(lax.dynamic_slice_in_dim(whole(shard), pos * group_width, group_width, 1))
        triple_full = jnp.concatenate(pieces, axis=1)
        recall_full = jnp.concatenate([whole(key_cross), whole(value_cross)], axis=1)
        query_full = whole(query_cross)
        output_turned, cross_turned = whole(output_self).T, whole(output_cross).T
        inner_full, outer_full = whole(inner_weight), whole(outer_weight)
        first_normed = jnp.concatenate(
            [rounded(rms_apply(v.astype(F32), norm_gains[0])) for v in lane_tokens], axis=0
        )
        qkv = rounded(linear(first_normed, triple_full))

    edge = lax.ppermute(edge_source, "seq", forward_pairs)
    mixed_group, lse = self_fwd(pos, bias, qkv, rows)
    if fast:
        feed_line = list(lax.optimization_barrier(tuple(feed_line) + (edge, mixed_group, group_far)))
        group_far, mixed_group, edge = feed_line.pop(), feed_line.pop(), feed_line.pop()

    states_all = lax.optimization_barrier(jnp.concatenate([edge, states], axis=0))

    def exchanged(blocks):
        return [blocks[0]] + [swap(blocks[k], "seq", k) for k in range(1, span)]

    mixed_blocks = [mixed_group[k * rows : (k + 1) * rows] for k in range(span)]
    mixed_self = join_columns(exchanged(mixed_blocks), pos)
    if fast:
        feed_near = after(jnp.stack(feed_line), mixed_self)
        feed_next = over_a(feed_near)
        recall_full, query_full, output_turned, cross_turned = assemble_attention(
            [group_both, group_far, over_core(group_both), over_core(group_far)], place
        )

    recall_pairs = rounded(linear(states_all, recall_full))

    after_self = inputs + input_grad(mixed_self, output_turned)
    second_normed = rounded(rms_apply(after_self, norm_gains[1]))
    if fast:
        feed_both = jnp.concatenate([feed_near, after(feed_next, second_normed)], axis=0)
        feed_far = over_b(feed_both)
    cross_queries = rounded(linear(second_normed, query_full))
    mixed_cross = cross_fwd(cross_queries, recall_pairs, neigh_rows)
    if fast:
        mixed_cross, feed_far = lax.optimization_barrier((mixed_cross, feed_far))
    after_cross = after_self + input_grad(mixed_cross, cross_turned)
    third_normed = rounded(rms_apply(after_cross, norm_gains[2]))
    if fast:
        inner_full, outer_full = assemble_feed(
            [feed_both, feed_far, over_core(feed_both), over_core(feed_far)], place
        )
    gate_value = linear(third_normed, inner_full)
    activated, gelu_pull = jax.vjp(gelu_tanh, gate_value)
    hidden_act = rounded(activated)

    grad_feed = rounded(upstream)
    grad_hidden = input_grad(grad_feed, outer_full)
    grad_gate = rounded(gelu_pull(grad_hidden)[0])
    if fast:
        kept, sent = feed_grad(place, third_normed, grad_gate, hidden_act, grad_feed)
        got = over_core(sent)
    else:
        sum_outer = block_sum(hidden_act, grad_feed)
        sum_inner = block_sum(third_normed, grad_gate)
    norm_grad, gain_three = norm_back(after_cross, norm_gains[2], input_grad(grad_gate, inner_full))
    grad_late = upstream + norm_grad

    grad_cross = rounded(grad_late)
    grad_mixed = rounded(linear(grad_cross, cross_turned))
    if fast:
        got = after(got, grad_mixed)
        sent_b = rounded(wide_sum(kept[1], got[1]))
        grad_mixed = after(grad_mixed, sent_b)
        got_b = over_b(sent_b)
    probe, pair_round = cross_bwd(cross_queries, grad_mixed, recall_pairs, neigh_rows)

    def turned_back(own):
        half = own.shape[1] // 2
        return jnp.concatenate([own[:, :half].T, own[:, half:].T], axis=1)

    if fast:
        pieces = group_grad("tall", place, mixed_cross, grad_cross, 3, 5)
        pieces = group_grad("wide", place, second_normed, probe, 2, 5, pieces)
        pieces = group_grad("wide", place, states_all, pair_round, 0, 5, pieces, 2)
        probe, got_b = lax.optimization_barrier((probe, got_b, pieces[0]))[:2]
        sent_a = sum_second(kept, got, got_b)
        got_a = over_a(sent_a)
    else:
        sum_cross = block_sum(mixed_cross, grad_cross)
        sum_key = block_sum(states_all, pair_round[:, :width])
        sum_value = block_sum(states_all, pair_round[:, width:])
        sum_query = block_sum(second_normed, probe)
    norm_grad, gain_two = norm_back(after_self, norm_gains[1], input_grad(probe, query_full))
    grad_early = grad_late + norm_grad

    grad_self = rounded(grad_early)
    if fast:
        last_kept, last_sent = group_grad("tall", place, mixed_self, grad_self, 4, 5, pieces)
        last_got = over_core(last_sent)
    else:
        sum_output = block_sum(mixed_self, grad_self)
    grad_attended = rounded(linear(grad_self, output_turned))
    if fast:
        grad_attended = after(grad_attended, sent_a)
    grad_parts = exchanged(split_columns(grad_attended, span, pos))
    if fast:
        pair_round = after(pair_round, grad_attended)
    states_round = rounded(input_grad(pair_round, recall_full))
    if fast:
        grad_parts = list(lax.optimization_barrier(tuple(grad_parts) + (states_round, last_got)))
        last_got, states_round = grad_parts.pop(), grad_parts.pop()
        line = sum_third(kept, got, got_b, after(got_a, grad_parts[-1]))
        last_b = rounded(wide_sum(last_kept[1], last_got[1]))
        grad_parts[0] = after(grad_parts[0], line, last_b)
        last_far = over_b(last_b)
        feed_own = [line[0]] + all_over_z(line)
    grad_group = jnp.concatenate(grad_parts, axis=0)
    def joined_states(whole_round, edge_round):
        last = whole_round[segments * neigh_rows :].astype(F32) + edge_round.astype(F32)
        return jnp.concatenate(
            [whole_round[neigh_rows : segments * neigh_rows], rounded(last)], axis=0
        )

    returned = lax.ppermute(states_round[:neigh_rows], "seq", back_pairs)
    triple_grad, bias_sums = self_bwd(pos, bias, qkv, mixed_group, grad_group, lse, rows)
    if fast:
        feed_own, triple_grad, last_far, returned = joint(feed_own, triple_grad, last_far, returned)
        last_a = sum_second(last_kept, last_got, last_far)
        last_near = over_a(last_a)
        own_y, other_y = triple_pieces(place, first_normed, after(triple_grad, last_a))
        feed_own = wide_sum(*feed_own)
        part = feed_own.shape[0] // 2
        sum_inner = feed_own[:part]
        sum_outer = feed_own[part:].reshape(part, 4, model // 4)
        sum_outer = sum_outer.transpose(1, 0, 2).reshape(4 * part, -1)
        fillers, other_y, last_near, triple_grad = joint(
            [sum_inner, sum_outer], other_y, last_near, triple_grad
        )
        sum_inner, sum_outer = fillers
        got_y = swap(other_y, "dp", 1)
    else:
        grad_states = joined_states(states_round, returned)
    partial = input_grad(triple_grad, triple_full)
    gain_one = jnp.sum(partial * first_normed.astype(F32), axis=0) / norm_gains[0]
    partial = rounded(partial)
    if fast:
        last_near = after(last_near, partial)
        line = sum_third(last_kept, last_got, last_far, last_near)
        last_own = [line[0]] + all_over_z(line)
    partial = partial.reshape(span, rows, model)
    blocks = {k: partial[k] for k in range(span)}
    if fast:
        near_zero, near_two = swap(partial[1], "seq", 1), swap(partial[3], "seq", 1)
        leaves = rounded(wide_sum(partial[2], near_two))
        last_own[1:-1], leaves, got_y, near_zero = joint(last_own[1:-1], leaves, got_y, near_zero)
        arrived = swap(leaves, "seq", 2)
        line = rounded(wide_sum(own_y, got_y))
        own = [line[0]] + all_over_z(line)
        returned, hidden_act = lax.optimization_barrier((returned, hidden_act, own[1]))[:2]
        outcome = rounded(after_cross + linear(hidden_act, outer_full))
        grad_states = joined_states(states_round, returned)
    else:
        outcome = rounded(after_cross + linear(hidden_act, outer_full))
        bit = 1
        while bit < span:
            for k in sorted(blocks):
                if not k & bit:
                    got = swap(blocks[k | bit], "seq", bit)
                    blocks[k] = blocks[k].astype(F32) + got.astype(F32)
                    if bit * 2 < span and k:
                        blocks[k] = rounded(blocks[k])
            blocks = {k: v for k, v in blocks.items() if not k & bit}
            bit *= 2
    bias_local = jnp.sum(bias_sums, axis=(2, 3))
    bias_all = lax.dynamic_update_slice_in_dim(
        jnp.zeros((heads, NB), F32), bias_local, pos * group_heads, 0
    )
    small = jnp.concatenate([gain_one, gain_two, gain_three, bias_all.reshape(-1)])
    if fast:
        size = small.shape[0]
        small = jnp.pad(small, (0, -size % 1024)).reshape(-1, 128)
        small = small_sum(after(small, own[1], outcome, grad_states))
        rest, small = joint(own[1:] + last_own[-1:] + [arrived], small)
        own[1:], last_own[-1], arrived = rest[:-2], rest[-2], rest[-1]
        blocks[0] = wide_sum(partial[0], near_zero, arrived)
        small = small.reshape(-1)[:size]
    else:
        small = lax.psum(small, BOTH)
    if fast:
        own_sum = wide_sum(*own)
        own_self = [own_sum[:, i * group_width : (i + 1) * group_width] for i in range(3)]
        last_own = wide_sum(*last_own)
        part = last_own.shape[0] // 5
        sum_key, sum_value, sum_query = (last_own[i * part : (i + 1) * part] for i in range(3))
        sum_cross = turned_back(last_own[3 * part : 4 * part])
        sum_output = turned_back(last_own[4 * part :])
    norm_grad, _ = norm_back(inputs, norm_gains[0], blocks[0])
    grad_inputs = grad_early + norm_grad

    if not fast:
        own_self = []
        for i in range(3):
            columns = triple_grad[:, i * group_width : (i + 1) * group_width]
            wide = jnp.zeros((span * rows, width), BF)
            wide = lax.dynamic_update_slice_in_dim(wide, columns, pos * group_width, 1)
            own_self.append(block_sum(first_normed, wide))

    gains = small[: 3 * model].reshape(3, model)
    bias_total = small[3 * model :].reshape(heads, NB)
    return (
        outcome.reshape(1, rows, model),
        rounded(grad_inputs).reshape(1, rows, model),
        grad_states.reshape(neighbours.shape),
        gains,
        bias_total,
        own_self[0],
        own_self[1],
        own_self[2],
        sum_output,
        sum_query,
        sum_key,
        sum_value,
        sum_cross,
        sum_inner,
        sum_outer,
    )


def solution(mesh):
    weight = P("dp", "seq")
    lane = P("dp", "seq", None)
    wide = P("dp", "seq", None, None, None)
    return jax.shard_map(
        on_device,
        mesh=mesh,
        in_specs=(lane, wide, P(), P()) + (weight,) * 10 + (lane,),
        out_specs=(lane, lane, wide, P(), P()) + (weight,) * 10,
        check_vma=False,
    )
```
